32 devices in a mesh: dp: 4 (over y, x), context: 8 (over z, core).
Axes of the slice: x: 2, y: 2, z: 4, core: 2. Of those that a mesh axis runs over, the one named last changes fastest.
Arguments:
- projected: bfloat16 [4096, 6144], P(('dp', 'context')), may hold values from -6 to 6
- short_taps: float32 [3, 6144], replicated, may hold values from -4 to 4
- long_filter: float32 [2048, 1024], P('context'), may hold values from -1.5 to 1.5
- skip_gain: float32 [2048], P('context'), may hold values from -4 to 4
- out_proj: bfloat16 [2048, 2048], P('dp'), may hold values from -0.125 to 0.125
- cotangent: bfloat16 [4096, 2048], P(('dp', 'context')), may hold values from -25 to 25
Outputs:
- grad_inputs: bfloat16 [4096, 6144], P(('dp', 'context'))
- grad_taps: float32 [3, 6144], replicated
- grad_filter: float32 [2048, 1024], P('context', 'dp')
- grad_skip: float32 [2048], P('context')
- grad_proj: float32 [2048, 2048], P(('dp', 'context'))
The draws below stay inside these ranges and needn't reach their ends.
All inputs are finite; a program needn't handle non-finite values.
Results may differ from the reference program's by a relative error of at most 0.012.
Values may be sent and summed in bfloat16 or wider, within the bound.
No kernel may reach another device: no remote copies, remote signals or barrier semaphores. Data moves between devices by JAX's collectives and lax.ppermute only.
A program may use at most 128 MiB of HBM per device.

```python
import math
import jax
import jax.numpy as jnp
from jax import lax

FILTER_FEATURES = 2048
DOUT = 2048
TIME_POINTS = 1024
SEQS = 4
TOKENS = 4096


def draw_long_filter(key, part):
    noise_key = jax.random.fold_in(key, 11)
    rate_key = jax.random.fold_in(key, 12)
    pick_key = jax.random.fold_in(key, 13)
    pulse_seed_handle = jax.random.fold_in(key, 14)
    arrival_lags = jnp.arange(TIME_POINTS, dtype=jnp.float32)[None, :]
    stochastic_perturbation = jnp.clip(jax.random.normal(noise_key, (FILTER_FEATURES, TIME_POINTS), jnp.float32), -4.0, 4.0)
    slow_share = 0.5
    picks = jax.random.uniform(pick_key, (FILTER_FEATURES, 1), jnp.float32)
    levels = jax.random.uniform(rate_key, (FILTER_FEATURES, 1), jnp.float32)
    slow_rate = 0.25 / TIME_POINTS * jnp.exp(levels * jnp.log(8.0))
    fast_low = 2.0 / TIME_POINTS
    fast_rate = fast_low * jnp.exp(levels * jnp.log(0.05 / fast_low))
    fading_exponents = jnp.where(picks < slow_share, slow_rate, fast_rate)
    impulse_series = jax.random.uniform(pulse_seed_handle, (FILTER_FEATURES, 1), jnp.float32) * TIME_POINTS
    pulse_amplitude = jnp.sqrt(2.0 * fading_exponents + 1.0 / TIME_POINTS)
    return stochastic_perturbation * jnp.exp(-fading_exponents * arrival_lags) * pulse_amplitude * jnp.where(arrival_lags >= impulse_series, 0.6, 1.0)


def draw_cotangent(key, part):
    noise_key = jax.random.fold_in(key, 21)
    places = jnp.arange(TOKENS, dtype=jnp.float32)[:, None] / TOKENS
    stochastic_perturbation = jnp.clip(jax.random.normal(noise_key, (TOKENS, DOUT), jnp.float32), -4.0, 4.0)
    ramp = 1.0 + 2.0 * places
    return (stochastic_perturbation * ramp).astype(jnp.bfloat16)


def level_of(own_key, dims, cuts, low, largest):
    level = 1.0
    for position, shards_of in cuts:
        draws = jax.random.uniform(jax.random.fold_in(jax.random.fold_in(own_key, 6), position), (shards_of,), jnp.float32, low / len(cuts), largest / len(cuts))
        level = level * jnp.repeat(jnp.exp(draws), dims[position] // shards_of).reshape((-1,) + (1,) * (len(dims) - 1 - position))
    return level


def gaussian(own_key, extent, scale, bound, pieces=(), kind=jnp.bfloat16):
    entries = scale * jax.random.normal(own_key, extent, jnp.float32)
    if pieces:
        entries = entries * level_of(own_key, extent, pieces, -0.22, 0.18)
    return jnp.clip(entries, -bound, bound).astype(kind)


def setup_inputs(seed: int = 0) -> dict:
    splits = jax.random.split(jax.random.key(seed), 7)
    return {
        "projected": gaussian(splits[0], (TOKENS, 3 * FILTER_FEATURES), 1.0, 6.0, ((0, 32),)),
        "short_taps": gaussian(splits[1], (3, 3 * FILTER_FEATURES), 0.7, 4.0, (), jnp.float32),
        "long_filter": draw_long_filter(jax.random.fold_in(splits[6], 71), 0),
        "skip_gain": gaussian(splits[3], (FILTER_FEATURES,), 1.0, 4.0, ((0, 8),), jnp.float32),
        "out_proj": gaussian(splits[4], (FILTER_FEATURES, DOUT), FILTER_FEATURES ** -0.5, 0.125, ((0, 4),)),
        "cotangent": draw_cotangent(jax.random.fold_in(splits[6], 71), 0),
    }


def shifted_down(values, steps):
    width = values.shape[1]
    return jnp.concatenate([jnp.zeros((steps, width), values.dtype), values[:values.shape[0] - steps]], 0)

def shifted_up(values, steps):
    width = values.shape[1]
    return jnp.concatenate([values[steps:], jnp.zeros((steps, width), values.dtype)], 0)

def reference(projected, short_taps, long_filter, skip_gain, out_proj, cotangent):
    length = TIME_POINTS
    period = 2 * TIME_POINTS
    chans = FILTER_FEATURES
    filter_spec = jnp.fft.rfft(long_filter, n=period, axis=1)
    streams = projected.reshape(SEQS, TIME_POINTS, 3 * FILTER_FEATURES)
    grads_out = cotangent.reshape(SEQS, TIME_POINTS, DOUT)

    def one_sequence(carry, inputs):
        seq_in, seq_cot = inputs
        inputs_f = seq_in.astype(jnp.float32)
        once_back = shifted_down(inputs_f, 1)
        twice_back = shifted_down(inputs_f, 2)
        mixed = short_taps[0] * inputs_f + short_taps[1] * once_back + short_taps[2] * twice_back
        query = mixed[:, :chans].astype(jnp.bfloat16)
        keyed = mixed[:, chans:2 * chans].astype(jnp.bfloat16)
        valued = mixed[:, 2 * chans:].astype(jnp.bfloat16)
        product = (keyed.astype(jnp.float32) * valued.astype(jnp.float32)).astype(jnp.bfloat16)
        prod_chan = product.astype(jnp.float32).T
        prod_spec = jnp.fft.rfft(prod_chan, n=period, axis=1)
        long_chan = jnp.fft.irfft(filter_spec * prod_spec, n=period, axis=1)[:, :length] + skip_gain[:, None] * prod_chan
        long_out = long_chan.T.astype(jnp.bfloat16)
        gate = (query.astype(jnp.float32) * long_out.astype(jnp.float32)).astype(jnp.bfloat16)
        grad_gate = lax.dot_general(seq_cot, out_proj, (((1,), (1,)), ((), ())), preferred_element_type=jnp.float32).astype(jnp.bfloat16)
        grad_query = grad_gate.astype(jnp.float32) * long_out.astype(jnp.float32)
        grad_long = (grad_gate.astype(jnp.float32) * query.astype(jnp.float32)).astype(jnp.bfloat16)
        grad_chan = grad_long.astype(jnp.float32).T
        grad_spec = jnp.fft.rfft(grad_chan, n=period, axis=1)
        back_chan = jnp.fft.irfft(jnp.conj(filter_spec) * grad_spec, n=period, axis=1)[:, :length] + skip_gain[:, None] * grad_chan
        grad_product = back_chan.T.astype(jnp.bfloat16)
        filter_term = jnp.fft.irfft(jnp.conj(prod_spec) * grad_spec, n=period, axis=1)[:, :length]
        skip_term = lax.optimization_barrier(jnp.sum(grad_chan * prod_chan, axis=1))
        grad_key = grad_product.astype(jnp.float32) * valued.astype(jnp.float32)
        grad_value = grad_product.astype(jnp.float32) * keyed.astype(jnp.float32)
        grad_mixed = jnp.concatenate([grad_query, grad_key, grad_value], 1)
        grad_in = (short_taps[0] * grad_mixed + short_taps[1] * shifted_up(grad_mixed, 1) + short_taps[2] * shifted_up(grad_mixed, 2)).astype(jnp.bfloat16)
        taps_term = jnp.stack([lax.optimization_barrier(jnp.sum(grad_mixed * inputs_f, 0)), lax.optimization_barrier(jnp.sum(grad_mixed * once_back, 0)), lax.optimization_barrier(jnp.sum(grad_mixed * twice_back, 0))])
        new_carry = (carry[0] + filter_term, carry[1] + skip_term, carry[2] + taps_term)
        return (new_carry, (grad_in, gate))
    start = (jnp.zeros((FILTER_FEATURES, TIME_POINTS), jnp.float32), jnp.zeros((FILTER_FEATURES,), jnp.float32), jnp.zeros((3, 3 * FILTER_FEATURES), jnp.float32))
    sums, stacked = lax.scan(one_sequence, start, (streams, grads_out))
    grad_inputs = stacked[0].reshape(TOKENS, 3 * FILTER_FEATURES)
    gates = stacked[1].reshape(TOKENS, FILTER_FEATURES)
    scale_factor = 1.0 / math.sqrt(TOKENS)
    grad_proj = lax.dot_general(gates, cotangent, (((0,), (0,)), ((), ())), preferred_element_type=jnp.float32) * scale_factor
    return (grad_inputs, sums[2] * scale_factor, sums[0] * scale_factor, sums[1] * scale_factor, grad_proj)
```

```python
import math

import jax
import jax.numpy as jnp
from jax import lax
from jax.experimental import pallas as pl
from jax.experimental.pallas import tpu as pltpu
from jax.sharding import PartitionSpec as P

BF16 = jnp.bfloat16
F32 = jnp.float32


def passed_along(value, axis, steps):
    count = lax.axis_size(axis)
    initial, last = (max(0, -steps), min(count, count - steps))
    return lax.ppermute(value, axis, [(source, source + steps) for source in range(initial, last)])


def swapped(value, axis, mask):
    return lax.ppermute(value, axis, [(i, i ^ mask) for i in range(lax.axis_size(axis))])


def exchanged(pieces, axis):
    return [pieces[0]] + [swapped(pieces[k], axis, k) for k in range(1, len(pieces))]


def rows_down(values, steps, before):
    row = lax.broadcasted_iota(jnp.int32, values.shape, 0)
    moved = pltpu.roll(values, steps, axis=0)
    if steps == 1:
        return jnp.where(row == 0, before[1:2], moved)
    return jnp.where(row == 0, before[0:1], jnp.where(row == 1, before[1:2], moved))


def rows_up(values, steps, after):
    count = values.shape[0]
    row = lax.broadcasted_iota(jnp.int32, values.shape, 0)
    moved = pltpu.roll(values, count - steps, axis=0)
    if steps == 1:
        return jnp.where(row == count - 1, after[0:1], moved)
    return jnp.where(row == count - 1, after[1:2], jnp.where(row == count - 2, after[0:1], moved))


def short_kernel(parts, chans, me_ref, proj_ref, prev_ref, taps_ref, *outs):
    query_refs, product_refs = outs[:parts], outs[parts : 2 * parts]
    keyed_ref, valued_ref = outs[2 * parts :]
    blk = chans // parts
    me = me_ref[0]
    for k in range(parts):
        start = (me ^ k) * blk

        def mixed(stream):
            cols = pl.ds(pl.multiple_of(start + stream * chans, blk), blk)
            values = proj_ref[:, cols].astype(F32)
            before = prev_ref[:, cols]
            taps = taps_ref[:, cols]
            return (
                taps[0:1] * values
                + taps[1:2] * rows_down(values, 1, before)
                + taps[2:3] * rows_down(values, 2, before)
            ).astype(BF16)

        own = pl.ds(pl.multiple_of(start, blk), blk)
        query_refs[k][...] = mixed(0)
        keyed, valued = (mixed(1), mixed(2))
        keyed_ref[:, own] = keyed
        valued_ref[:, own] = valued
        product_refs[k][...] = (keyed.astype(F32) * valued.astype(F32)).astype(BF16)


def final_kernel(parts, chans, me_ref, *refs):
    query_grads, product_grads = refs[:parts], refs[parts : 2 * parts]
    keyed_ref, valued_ref, after_ref, proj_ref, prev_ref, taps_ref = refs[2 * parts : 2 * parts + 6]
    out_ref = refs[2 * parts + 6]
    share_refs = refs[2 * parts + 7 :]
    blk = chans // parts
    rows = proj_ref.shape[0]
    me = me_ref[0]
    for k in range(parts):
        start = (me ^ k) * blk
        own = pl.ds(pl.multiple_of(start, blk), blk)
        other = pl.ds(pl.multiple_of(start + chans, blk), blk)
        back = product_grads[k][0:rows].astype(F32)
        back_after = product_grads[k][rows : rows + 2].astype(F32)
        grads = (
            (query_grads[k][0:rows].astype(F32), query_grads[k][rows : rows + 2].astype(F32)),
            (back * valued_ref[:, own].astype(F32), back_after * after_ref[:, other]),
            (back * keyed_ref[:, own].astype(F32), back_after * after_ref[:, own]),
        )
        sums = []
        for stream, (grad, grad_after) in enumerate(grads):
            cols = pl.ds(pl.multiple_of(start + stream * chans, blk), blk)
            taps = taps_ref[:, cols]
            out_ref[:, cols] = (
                taps[0:1] * grad
                + taps[1:2] * rows_up(grad, 1, grad_after)
                + taps[2:3] * rows_up(grad, 2, grad_after)
            ).astype(BF16)
            values = proj_ref[:, cols].astype(F32)
            before = prev_ref[:, cols]
            sums.append(jnp.sum(grad * values, 0, keepdims=True))
            sums.append(jnp.sum(grad * rows_down(values, 1, before), 0, keepdims=True))
            sums.append(jnp.sum(grad * rows_down(values, 2, before), 0, keepdims=True))
        for i, term in enumerate(sums):
            share_refs[k][i : i + 1, :] = term


VMEM = pl.BlockSpec(memory_space=pltpu.VMEM)
SMEM = pl.BlockSpec(memory_space=pltpu.SMEM)


def cost(*arrays):
    moved = sum(math.prod(a.shape) * a.dtype.itemsize for a in arrays)
    return pl.CostEstimate(flops=8 * moved, transcendentals=0, bytes_accessed=moved)


def short_convs(me, projected, prev_rows, taps, parts):
    rows, width = projected.shape
    chans = width // 3
    piece = jax.ShapeDtypeStruct((rows, chans // parts), BF16)
    whole = jax.ShapeDtypeStruct((rows, chans), BF16)
    outs = pl.pallas_call(
        lambda *refs: short_kernel(parts, chans, *refs),
        out_shape=[piece] * (2 * parts) + [whole] * 2,
        in_specs=[SMEM, VMEM, VMEM, VMEM],
        out_specs=[VMEM] * (2 * parts + 2),
        compiler_params=pltpu.CompilerParams(vmem_limit_bytes=40 * 2**20),
        cost_estimate=cost(projected, projected, projected),
        name="short_convs",
    )(me, projected, prev_rows, taps)
    return (outs[:parts], outs[parts : 2 * parts], outs[-2], outs[-1])


def stream_grads(me, query_grads, product_grads, keyed, valued, after, projected, prev_rows, taps):
    parts = len(query_grads)
    rows, width = projected.shape
    chans = width // 3
    share = jax.ShapeDtypeStruct((9, chans // parts), F32)
    outs = pl.pallas_call(
        lambda *refs: final_kernel(parts, chans, *refs),
        out_shape=[jax.ShapeDtypeStruct((rows, width), BF16)] + [share] * parts,
        in_specs=[SMEM] + [VMEM] * (2 * parts + 6),
        out_specs=[VMEM] * (1 + parts),
        compiler_params=pltpu.CompilerParams(vmem_limit_bytes=40 * 2**20),
        cost_estimate=cost(projected, projected, projected),
        name="stream_grads",
    )(me, *query_grads, *product_grads, keyed, valued, after, projected, prev_rows, taps)
    return (outs[0], outs[1:])


def shifted(values, before):
    rows = values.shape[0]
    down = jnp.concatenate([before, values], 0)
    return [down[i : i + rows] for i in range(3)]


def reordered(blocks, me):
    picks = [lax.dynamic_index_in_dim(blocks, me ^ k, 0, False) for k in range(blocks.shape[0])]
    return picks


def plain_short_convs(me, projected, prev_rows, taps, parts):
    chans = projected.shape[1] // 3
    blk = chans // parts
    two_back, once_back, current = shifted(projected.astype(F32), prev_rows)
    mixed = (taps[0] * current + taps[1] * once_back + taps[2] * two_back).astype(BF16)
    query, keyed, valued = (mixed[:, i * chans : (i + 1) * chans] for i in range(3))
    product = (keyed.astype(F32) * valued.astype(F32)).astype(BF16)

    def cut(values):
        return reordered(values.reshape(-1, parts, blk).transpose(1, 0, 2), me[0])

    return (cut(query), cut(product), keyed, valued)


def plain_stream_grads(
    me, query_grads, product_grads, keyed, valued, after, projected, prev_rows, taps
):
    parts = len(query_grads)
    rows, width = projected.shape
    blk = width // 3 // parts

    def joined(pieces):
        blocks = jnp.stack(reordered(jnp.stack(pieces), me[0])).astype(F32)
        return blocks.transpose(1, 0, 2).reshape(rows + 2, parts * blk)

    back = joined(product_grads)
    keyed_all = jnp.concatenate([keyed.astype(F32), after[:, : parts * blk]], 0)
    valued_all = jnp.concatenate([valued.astype(F32), after[:, parts * blk :]], 0)
    grads = jnp.concatenate([joined(query_grads), back * valued_all, back * keyed_all], 1)
    own = grads[:rows]
    out = (taps[0] * own + taps[1] * grads[1 : rows + 1] + taps[2] * grads[2:]).astype(BF16)
    two_back, once_back, current = shifted(projected.astype(F32), prev_rows)
    sums = [jnp.sum(own * values, 0) for values in (current, once_back, two_back)]
    blocks = jnp.stack(sums).reshape(3, 3, parts, blk).transpose(2, 1, 0, 3).reshape(parts, 9, blk)
    return (out, reordered(blocks, me[0]))


def table(places, first, freqs, seq_len):
    inner = min(32, freqs)
    outer = freqs // inner

    def waves(odd):
        phases = odd[:, None] * places[None, :] % (4 * seq_len)
        angles = phases.astype(F32) * (2.0 * math.pi / (4 * seq_len))
        return (jnp.cos(angles), jnp.sin(angles))

    outer_cos, outer_sin = waves(2 * (first + inner * jnp.arange(outer)))
    inner_cos, inner_sin = waves(2 * jnp.arange(inner) + 1)
    oc, os = (outer_cos[:, None], outer_sin[:, None])
    ic, is_ = (inner_cos[None], inner_sin[None])
    both = jnp.stack([oc * ic - os * is_, -(os * ic + oc * is_)])
    return both.astype(BF16).reshape(2 * freqs, places.shape[0])


def dot(left, right, left_dim, right_dim):
    return lax.dot_general(
        left, right, (((left_dim,), (right_dim,)), ((), ())), preferred_element_type=F32
    )


def spectral_product(left, right, conjugate_left):
    half = left.shape[0] // 2
    left_re, left_im = (left[:half], left[half:])
    right_re, right_im = (right[:half], right[half:])
    if conjugate_left:
        real = left_re * right_re + left_im * right_im
        imag = left_re * right_im - left_im * right_re
    else:
        real = left_re * right_re - left_im * right_im
        imag = left_re * right_im + left_im * right_re
    return jnp.concatenate([real, imag], 0).astype(BF16)


def long_terms(first, freqs, places, lags, long_filter, product, grad_long):
    seq_len = places.shape[0]
    own = table(places, first, freqs, seq_len)
    plain = table(lags, first, freqs, seq_len)
    filter_spec = dot(plain, long_filter, 1, 1)
    product_spec = dot(own, product, 1, 0)
    grad_spec = dot(own, grad_long, 1, 0)
    out = dot(own, spectral_product(filter_spec, product_spec, False), 0, 0)
    back = dot(own, spectral_product(filter_spec, grad_spec, True), 0, 0)
    lag_grad = dot(spectral_product(product_spec, grad_spec, True), plain, 0, 0)
    return (out, back, lag_grad)


def own_rows(weights, parts_dp, parts_ctx):
    ratio = parts_ctx // parts_dp
    context = lax.axis_index("context")
    block = weights.shape[0] // ratio
    half = lax.dynamic_slice_in_dim(weights, (context % ratio) * block, block, 0)
    holder = context // ratio
    found = half
    for k in range(1, parts_dp):
        pairs = [
            ((c // ratio) * parts_ctx + c, ((c // ratio) ^ k) * parts_ctx + c)
            for c in range(parts_ctx)
        ]
        sent = lax.ppermute(half, ("dp", "context"), pairs)
        found = jnp.where(lax.axis_index("dp") == (holder ^ k), sent, found)
    return found


def gathered(value, axis):
    pieces = [value]
    for k in range(2, lax.axis_size(axis), 2):
        pieces.append(swapped(value, axis, k))
    out = []
    for piece in pieces:
        out += [piece, swapped(piece, axis, 1)]
    return jnp.concatenate(out, 0)


def summed_blocks(value, axis, dim):
    count = lax.axis_size(axis)
    size = value.shape[dim] // count
    me = lax.axis_index(axis)
    total = lax.dynamic_slice_in_dim(value, me * size, size, dim)
    for k in range(1, count):
        sent = lax.dynamic_slice_in_dim(value, (me ^ k) * size, size, dim).astype(BF16)
        total = total + swapped(sent, axis, k).astype(F32)
    return total


def body(projected, short_taps, long_filter, skip_gain, out_proj, cotangent):
    rows, width = projected.shape
    chans = width // 3
    parts_dp, parts = (lax.axis_size("dp"), lax.axis_size("context"))
    blk = chans // parts
    seq_len = rows * parts
    me = lax.axis_index("context")
    me_arr = me.astype(jnp.int32)[None]
    scale_factor = 1.0 / math.sqrt(seq_len * parts_dp)

    prev_rows = passed_along(projected[rows - 2 :], "context", 1).astype(F32)
    cot_seq = gathered(cotangent, "context")
    weights = own_rows(out_proj, parts_dp, parts)
    wide = blk % 128 == 0 and rows % 16 == 0
    query_out, product_out, keyed, valued = (short_convs if wide else plain_short_convs)(
        me_arr, projected, prev_rows, short_taps, parts
    )
    after = passed_along(
        jnp.concatenate([keyed[:2], valued[:2]], 1), "context", -1
    ).astype(F32)
    product = jnp.concatenate(exchanged(product_out, "context"), 0)
    query = jnp.concatenate(exchanged(query_out, "context"), 0).astype(F32)

    lags = jnp.arange(seq_len)
    order = (jnp.arange(parts) ^ me)[:, None] * rows + jnp.arange(rows)[None, :]
    places = order.reshape(seq_len)
    grad_gate = dot(cot_seq, weights, 1, 1).astype(BF16).astype(F32)
    grad_long = (grad_gate * query).astype(BF16)
    filter_b = long_filter.astype(BF16)
    freqs = seq_len if seq_len <= 1024 else 256
    if freqs == seq_len:
        terms = long_terms(0, freqs, places, lags, filter_b, product, grad_long)
    else:

        def step(carry, first):
            new = long_terms(first, freqs, places, lags, filter_b, product, grad_long)
            return (tuple(a + b for a, b in zip(carry, new)), None)

        zero = jnp.zeros((seq_len, blk), F32)
        start = (zero, zero, jnp.zeros((blk, seq_len), F32))
        terms, _ = lax.scan(step, start, jnp.arange(0, seq_len, freqs))
    out_sum, back_sum, lag_sum = terms
    inverse = 1.0 / seq_len
    product_f, grad_long_f = (product.astype(F32), grad_long.astype(F32))
    long_out = (out_sum * inverse + skip_gain[None, :] * product_f).astype(BF16).astype(F32)
    grad_product = (back_sum * inverse + skip_gain[None, :] * grad_long_f).astype(BF16)
    gate = (query * long_out).astype(BF16)
    grad_query = (grad_gate * long_out).astype(BF16)

    follows = (jnp.arange(parts) ^ me) + 1
    picks = (follows[:, None] == (jnp.arange(parts) ^ me)[None, :]).astype(F32)

    def with_next(values):
        blocks = values.reshape(parts, rows, blk)
        heads = blocks[:, :2].astype(F32)
        after_rows = jnp.sum(picks[:, :, None, None] * heads[None], 1).astype(BF16)
        return [jnp.concatenate([blocks[k], after_rows[k]], 0) for k in range(parts)]

    query_grads = exchanged(with_next(grad_query), "context")
    product_grads = exchanged(with_next(grad_product), "context")
    grad_inputs, shares = (stream_grads if wide else plain_stream_grads)(
        me_arr, query_grads, product_grads, keyed, valued, after, projected, prev_rows, short_taps
    )

    proj_part = summed_blocks(dot(gate, cot_seq, 0, 0), "dp", 0).astype(BF16)
    rank = [
        (d * parts + c, c * parts_dp + d) for d in range(parts_dp) for c in range(parts)
    ]
    grad_proj = lax.ppermute(proj_part, ("dp", "context"), rank).astype(F32) * scale_factor
    grad_filter = summed_blocks(lag_sum, "dp", 1) * (scale_factor * inverse)
    skip_part = jnp.sum(grad_long_f * product_f, 0, keepdims=True)
    grad_skip = skip_part
    for k in range(1, parts_dp):
        grad_skip = grad_skip + swapped(skip_part, "dp", k)

    tap_sum = sum(exchanged(shares, "context"))
    tap_all = tap_sum
    for k in range(1, parts_dp):
        tap_all = tap_all + swapped(tap_sum, "dp", k)
    taps = jnp.stack(exchanged([tap_all * scale_factor] * parts, "context"))
    bit = 1
    while bit < parts:
        view = taps.reshape(parts // (2 * bit), 2, bit, 9, blk)
        taps = jnp.where(me & bit != 0, view[:, ::-1], view).reshape(parts, 9, blk)
        bit *= 2
    grad_taps = taps.reshape(parts, 3, 3, blk).transpose(2, 1, 0, 3).reshape(3, width)
    return (grad_inputs, grad_taps, grad_filter, grad_skip[0] * scale_factor, grad_proj)


def solution(mesh):
    placed = (
        P(("dp", "context"), None),
        P(),
        P("context", None),
        P("context"),
        P("dp", None),
        P(("dp", "context"), None),
    )
    return jax.shard_map(
        body,
        mesh=mesh,
        in_specs=placed,
        out_specs=(
            P(("dp", "context"), None),
            P(),
            P("context", "dp"),
            P("context"),
            P(("dp", "context"), None),
        ),
        check_vma=False,
    )
```

```python
import math

import jax
import jax.numpy as jnp
from jax import lax
from jax.experimental import pallas as pl
from jax.experimental.pallas import tpu as pltpu
from jax.sharding import PartitionSpec as P

BF16 = jnp.bfloat16
F32 = jnp.float32


def swapped(value, axis, mask):
    return lax.ppermute(value, axis, [(i, i ^ mask) for i in range(lax.axis_size(axis))])


def rows_down(values, steps):
    row = lax.broadcasted_iota(jnp.int32, values.shape, 0)
    return jnp.where(row < steps, 0.0, pltpu.roll(values, steps, axis=0))


def rows_up(values, steps):
    count = values.shape[0]
    row = lax.broadcasted_iota(jnp.int32, values.shape, 0)
    return jnp.where(row >= count - steps, 0.0, pltpu.roll(values, count - steps, axis=0))


def flat(ref):
    return ref[...].reshape(-1, ref.shape[-1]).astype(F32)


def short_kernel(query_in, key_in, value_in, taps_ref, query_ref, keyed_ref, valued_ref, product_ref):
    def mixed(ref, stream):
        values = flat(ref)
        taps = taps_ref[stream]
        total = taps[0:1] * values + taps[1:2] * rows_down(values, 1)
        return (total + taps[2:3] * rows_down(values, 2)).astype(BF16)

    query_ref[...] = mixed(query_in, 0)
    keyed, valued = (mixed(key_in, 1), mixed(value_in, 2))
    keyed_ref[...] = keyed
    valued_ref[...] = valued
    product_ref[...] = (keyed.astype(F32) * valued.astype(F32)).astype(BF16)


def final_kernel(*refs):
    query_in, key_in, value_in, taps_ref, gate_grad, long_ref, back_ref, keyed_ref, valued_ref = refs[:9]
    out_refs, sums_ref = refs[9:12], refs[12]
    back = back_ref[...].astype(F32)
    for stream, ref in enumerate((query_in, key_in, value_in)):
        if stream == 0:
            grad = gate_grad[...].astype(F32) * long_ref[...].astype(F32)
        elif stream == 1:
            grad = back * valued_ref[...].astype(F32)
        else:
            grad = back * keyed_ref[...].astype(F32)
        taps = taps_ref[stream]
        total = taps[0:1] * grad + taps[1:2] * rows_up(grad, 1) + taps[2:3] * rows_up(grad, 2)
        out_refs[stream][...] = total.astype(BF16).reshape(out_refs[stream].shape)
        values = flat(ref)
        for j in range(3):
            moved = rows_down(values, j) if j else values
            sums_ref[stream, j : j + 1, :] = jnp.sum(grad * moved, 0, keepdims=True)


def cost(*arrays):
    moved = sum(math.prod(a.shape) * a.dtype.itemsize for a in arrays)
    return pl.CostEstimate(flops=8 * moved, transcendentals=0, bytes_accessed=moved)


def stream_specs(parts, rows, tile):
    return [
        pl.BlockSpec((parts, None, rows, tile), lambda j, s=s: (0, s, 0, j)) for s in range(3)
    ]


def short_convs(streams, taps):
    parts, _, rows, blk = streams.shape
    seq_len = parts * rows
    tile = min(128, blk)
    plane = pl.BlockSpec((seq_len, tile), lambda j: (0, j))
    return pl.pallas_call(
        short_kernel,
        out_shape=[jax.ShapeDtypeStruct((seq_len, blk), BF16)] * 4,
        grid=(blk // tile,),
        in_specs=stream_specs(parts, rows, tile)
        + [pl.BlockSpec((3, 3, tile), lambda j: (0, 0, j))],
        out_specs=[plane] * 4,
        compiler_params=pltpu.CompilerParams(vmem_limit_bytes=48 * 2**20),
        cost_estimate=cost(streams, streams),
        name="short_convs",
    )(streams, streams, streams, taps)


def stream_grads(streams, taps, grad_gate, long_out, back, keyed, valued):
    parts, _, rows, blk = streams.shape
    seq_len = parts * rows
    tile = min(128, blk)
    plane = pl.BlockSpec((seq_len, tile), lambda j: (0, j))
    piece = pl.BlockSpec((parts, rows, tile), lambda j: (0, 0, j))
    rank_three = pl.BlockSpec((3, 3, tile), lambda j: (0, 0, j))
    return pl.pallas_call(
        final_kernel,
        out_shape=[jax.ShapeDtypeStruct((parts, rows, blk), BF16)] * 3
        + [jax.ShapeDtypeStruct((3, 3, blk), F32)],
        grid=(blk // tile,),
        in_specs=stream_specs(parts, rows, tile) + [rank_three] + [plane] * 5,
        out_specs=[piece] * 3 + [rank_three],
        compiler_params=pltpu.CompilerParams(vmem_limit_bytes=56 * 2**20),
        cost_estimate=cost(streams, streams),
        name="stream_grads",
    )(streams, streams, streams, taps, grad_gate, long_out, back, keyed, valued)


def table(first, freqs, seq_len):
    places = jnp.arange(seq_len)
    inner = min(32, freqs)
    outer = freqs // inner

    def waves(odd):
        phases = odd[:, None] * places[None, :] % (4 * seq_len)
        angles = phases.astype(F32) * (2.0 * math.pi / (4 * seq_len))
        return (jnp.cos(angles), jnp.sin(angles))

    outer_cos, outer_sin = waves(2 * (first + inner * jnp.arange(outer)))
    inner_cos, inner_sin = waves(2 * jnp.arange(inner) + 1)
    oc, os = (outer_cos[:, None], outer_sin[:, None])
    ic, is_ = (inner_cos[None], inner_sin[None])
    both = jnp.stack([oc * ic - os * is_, -(os * ic + oc * is_)])
    return both.astype(BF16).reshape(2 * freqs, seq_len)


def dot(left, right, left_dim, right_dim):
    return lax.dot_general(
        left, right, (((left_dim,), (right_dim,)), ((), ())), preferred_element_type=F32
    )


def spectral_product(left, right, conjugate_left):
    half = left.shape[0] // 2
    left_re, left_im = (left[:half], left[half:])
    right_re, right_im = (right[:half], right[half:])
    if conjugate_left:
        real = left_re * right_re + left_im * right_im
        imag = left_re * right_im - left_im * right_re
    else:
        real = left_re * right_re - left_im * right_im
        imag = left_re * right_im + left_im * right_re
    return jnp.concatenate([real, imag], 0).astype(BF16)


def long_terms(first, freqs, long_filter, product, grad_long):
    waves = table(first, freqs, product.shape[0])
    filter_spec = dot(waves, long_filter, 1, 1)
    product_spec = dot(waves, product, 1, 0)
    grad_spec = dot(waves, grad_long, 1, 0)
    out = dot(waves, spectral_product(filter_spec, product_spec, False), 0, 0)
    back = dot(waves, spectral_product(filter_spec, grad_spec, True), 0, 0)
    lag_grad = dot(spectral_product(product_spec, grad_spec, True), waves, 0, 0)
    return (out, back, lag_grad)


def own_rows(weights, parts_dp, parts_ctx):
    ratio = parts_ctx // parts_dp
    context = lax.axis_index("context")
    block = weights.shape[0] // ratio
    half = lax.dynamic_slice_in_dim(weights, (context % ratio) * block, block, 0)
    holder = context // ratio
    found = half
    for k in range(1, parts_dp):
        pairs = [
            ((c // ratio) * parts_ctx + c, ((c // ratio) ^ k) * parts_ctx + c)
            for c in range(parts_ctx)
        ]
        sent = lax.ppermute(half, ("dp", "context"), pairs)
        found = jnp.where(lax.axis_index("dp") == (holder ^ k), sent, found)
    return found


def summed_blocks(value, axis, dim):
    count = lax.axis_size(axis)
    size = value.shape[dim] // count
    me = lax.axis_index(axis)
    total = lax.dynamic_slice_in_dim(value, me * size, size, dim)
    for k in range(1, count):
        sent = lax.dynamic_slice_in_dim(value, (me ^ k) * size, size, dim).astype(BF16)
        total = total + swapped(sent, axis, k).astype(F32)
    return total


def body(projected, short_taps, long_filter, skip_gain, out_proj, cotangent):
    rows, width = projected.shape
    chans = width // 3
    parts_dp, parts = (lax.axis_size("dp"), lax.axis_size("context"))
    blk = chans // parts
    seq_len = rows * parts
    me = lax.axis_index("context")
    scale_factor = 1.0 / math.sqrt(seq_len * parts_dp)

    groups = [list(range(core, parts, 2)) for core in range(2)]
    cot_own = lax.all_gather(cotangent, "context", axis=0, tiled=True, axis_index_groups=groups)
    cot_other = swapped(cot_own, "context", 1)
    weights = own_rows(out_proj, parts_dp, parts)
    blocks = projected.reshape(rows, 3, parts, blk).transpose(2, 1, 0, 3)
    streams = lax.all_to_all(blocks, "context", split_axis=0, concat_axis=0, tiled=True)
    taps = lax.dynamic_slice_in_dim(short_taps.reshape(3, 3, chans), me * blk, blk, 2)
    taps = taps.transpose(1, 0, 2)
    query, keyed, valued, product = short_convs(streams, taps)

    first_core = me % 2 == 0

    def by_core(own, other):
        shape = (parts // 2, 1, rows, -1)
        even = jnp.where(first_core, own, other).reshape(shape)
        odd = jnp.where(first_core, other, own).reshape(shape)
        return jnp.concatenate([even, odd], 1).reshape(seq_len, -1)

    grad_gate = by_core(
        dot(cot_own, weights, 1, 1).astype(BF16), dot(cot_other, weights, 1, 1).astype(BF16)
    )
    grad_long = (grad_gate.astype(F32) * query.astype(F32)).astype(BF16)
    filter_b = long_filter.astype(BF16)
    freqs = seq_len if seq_len <= 1024 else 256
    if freqs == seq_len:
        terms = long_terms(0, freqs, filter_b, product, grad_long)
    else:

        def step(carry, first):
            new = long_terms(first, freqs, filter_b, product, grad_long)
            return (tuple(a + b for a, b in zip(carry, new)), None)

        zero = jnp.zeros((seq_len, blk), F32)
        start = (zero, zero, jnp.zeros((blk, seq_len), F32))
        terms, _ = lax.scan(step, start, jnp.arange(0, seq_len, freqs))
    out_sum, back_sum, lag_sum = terms
    inverse = 1.0 / seq_len
    product_f, grad_long_f = (product.astype(F32), grad_long.astype(F32))
    long_out = (out_sum * inverse + skip_gain[None, :] * product_f).astype(BF16)
    grad_product = (back_sum * inverse + skip_gain[None, :] * grad_long_f).astype(BF16)
    gate = (query.astype(F32) * long_out.astype(F32)).astype(BF16)

    *grads, tap_sums = stream_grads(
        streams, taps, grad_gate, long_out, grad_product, keyed, valued
    )
    sent = jnp.stack(grads, 1)
    back = lax.all_to_all(sent, "context", split_axis=0, concat_axis=0, tiled=True)
    grad_inputs = back.transpose(2, 1, 0, 3).reshape(rows, width)

    pairs = gate.reshape(parts // 2, 2, rows, blk)
    even, odd = (pairs[:, i].reshape(seq_len // 2, blk) for i in range(2))
    proj_sum = dot(jnp.where(first_core, even, odd), cot_own, 0, 0) + dot(
        jnp.where(first_core, odd, even), cot_other, 0, 0
    )
    proj_part = summed_blocks(proj_sum, "dp", 0).astype(BF16)
    rank = [
        (d * parts + c, c * parts_dp + d) for d in range(parts_dp) for c in range(parts)
    ]
    grad_proj = lax.ppermute(proj_part, ("dp", "context"), rank).astype(F32) * scale_factor
    grad_filter = summed_blocks(lag_sum, "dp", 1) * (scale_factor * inverse)

    skip_sum = jnp.sum(grad_long_f * product_f, 0, keepdims=True)
    small = jnp.concatenate([tap_sums.reshape(9, blk), skip_sum], 0)
    small_all = small
    for k in range(1, parts_dp):
        small_all = small_all + swapped(small, "dp", k)
    small_all = small_all * scale_factor
    grad_skip = small_all[9]
    every = jnp.broadcast_to(small_all[None, :9], (parts, 9, blk))
    taps_out = lax.all_to_all(every, "context", split_axis=0, concat_axis=0, tiled=True)
    grad_taps = taps_out.reshape(parts, 3, 3, blk).transpose(2, 1, 0, 3).reshape(3, width)
    return (grad_inputs, grad_taps, grad_filter, grad_skip, grad_proj)


def solution(mesh):
    placed = (
        P(("dp", "context"), None),
        P(),
        P("context", None),
        P("context"),
        P("dp", None),
        P(("dp", "context"), None),
    )
    return jax.shard_map(
        body,
        mesh=mesh,
        in_specs=placed,
        out_specs=(
            P(("dp", "context"), None),
            P(),
            P("context", "dp"),
            P("context"),
            P(("dp", "context"), None),
        ),
        check_vma=False,
    )
```

```python
import math

import jax
import jax.numpy as jnp
from jax import lax
from jax.experimental import pallas as pl
from jax.experimental.pallas import tpu as pltpu
from jax.sharding import PartitionSpec as P

BF16 = jnp.bfloat16
F32 = jnp.float32


def passed_along(value, axis, steps):
    count = lax.axis_size(axis)
    initial, last = (max(0, -steps), min(count, count - steps))
    return lax.ppermute(value, axis, [(source, source + steps) for source in range(initial, last)])


def swapped(value, axis, mask):
    return lax.ppermute(value, axis, [(i, i ^ mask) for i in range(lax.axis_size(axis))])


VMEM = pl.BlockSpec(memory_space=pltpu.VMEM)
SMEM = pl.BlockSpec(memory_space=pltpu.SMEM)


def rows_down(values, steps, before):
    row = lax.broadcasted_iota(jnp.int32, values.shape, 0)
    moved = pltpu.roll(values, steps, axis=0)
    if steps == 1:
        return jnp.where(row == 0, before[1:2], moved)
    return jnp.where(row == 0, before[0:1], jnp.where(row == 1, before[1:2], moved))


def rows_up(values, steps, after):
    count = values.shape[0]
    row = lax.broadcasted_iota(jnp.int32, values.shape, 0)
    moved = pltpu.roll(values, count - steps, axis=0)
    if steps == 1:
        return jnp.where(row == count - 1, after[0:1], moved)
    return jnp.where(row == count - 1, after[1:2], jnp.where(row == count - 2, after[0:1], moved))


def call(kernel, name, outs, smem, *args):
    moved = sum(math.prod(a.shape) * a.dtype.itemsize for a in args)
    return pl.pallas_call(
        kernel,
        out_shape=outs,
        in_specs=[SMEM] * smem + [VMEM] * (len(args) - smem),
        out_specs=[VMEM] * len(outs),
        compiler_params=pltpu.CompilerParams(vmem_limit_bytes=40 * 2**20),
        cost_estimate=pl.CostEstimate(flops=8 * moved, transcendentals=0, bytes_accessed=2 * moved),
        name=name,
    )(*args)


def columns(index, size):
    return slice(index * size, (index + 1) * size)


def short_kernel(proj_ref, prev_ref, taps_ref, query_ref, keyed_ref, valued_ref, product_ref):
    parts, _, blk = query_ref.shape
    for b in range(parts):

        def mixed(stream):
            cols = columns(stream * parts + b, blk)
            values = proj_ref[:, cols].astype(F32)
            before = prev_ref[:, cols]
            taps = taps_ref[:, cols]
            total = taps[0:1] * values + taps[1:2] * rows_down(values, 1, before)
            return (total + taps[2:3] * rows_down(values, 2, before)).astype(BF16)

        query_ref[b] = mixed(0)
        keyed, valued = (mixed(1), mixed(2))
        keyed_ref[b] = keyed
        valued_ref[b] = valued
        product_ref[b] = (keyed.astype(F32) * valued.astype(F32)).astype(BF16)


def grad_long_kernel(me_ref, query_ref, *refs):
    pieces, (gate_grad_ref, grad_long_ref) = refs[:-2], refs[-2:]
    parts, _, blk = query_ref.shape
    ratio = parts // len(pieces)
    for k, piece in enumerate(pieces):
        for i in range(ratio):
            b = (me_ref[0] ^ k) * ratio + i
            values = piece[:, columns(i, blk)]
            gate_grad_ref[b] = values
            grad_long_ref[b] = (values.astype(F32) * query_ref[b].astype(F32)).astype(BF16)


def gate_kernel(me_ref, query_ref, long_ref, *pieces):
    parts, _, blk = query_ref.shape
    ratio = parts // len(pieces)
    for k, piece in enumerate(pieces):
        for i in range(ratio):
            b = (me_ref[0] ^ k) * ratio + i
            gate = query_ref[b].astype(F32) * long_ref[b].astype(F32)
            piece[:, columns(i, blk)] = gate.astype(BF16)


def final_kernel(*refs):
    proj_ref, prev_ref, taps_ref, gate_grad_ref, long_ref, back_ref, keyed_ref, valued_ref = refs[:8]
    query_after_ref, pair_after_ref, out_ref, sums_ref = refs[8:]
    parts, rows, blk = long_ref.shape
    for b in range(parts):
        back = back_ref[b, 0:rows].astype(F32)
        back_after = back_ref[b, rows : rows + 2].astype(F32)
        grads = (
            (
                gate_grad_ref[b].astype(F32) * long_ref[b].astype(F32),
                query_after_ref[b],
            ),
            (back * valued_ref[b].astype(F32), back_after * pair_after_ref[1, b]),
            (back * keyed_ref[b].astype(F32), back_after * pair_after_ref[0, b]),
        )
        for stream, (grad, after) in enumerate(grads):
            cols = columns(stream * parts + b, blk)
            taps = taps_ref[:, cols]
            total = taps[0:1] * grad + taps[1:2] * rows_up(grad, 1, after)
            out_ref[:, cols] = (total + taps[2:3] * rows_up(grad, 2, after)).astype(BF16)
            values = proj_ref[:, cols].astype(F32)
            before = prev_ref[:, cols]
            for j in range(3):
                moved = rows_down(values, j, before) if j else values
                term = jnp.sum(grad * moved, 0, keepdims=True)
                sums_ref[b, 3 * stream + j : 3 * stream + j + 1, :] = term


def table(first, freqs, seq_len):
    places = jnp.arange(seq_len)
    inner = min(32, freqs)
    outer = freqs // inner

    def waves(odd):
        phases = odd[:, None] * places[None, :] % (4 * seq_len)
        angles = phases.astype(F32) * (2.0 * math.pi / (4 * seq_len))
        return (jnp.cos(angles), jnp.sin(angles))

    outer_cos, outer_sin = waves(2 * (first + inner * jnp.arange(outer)))
    inner_cos, inner_sin = waves(2 * jnp.arange(inner) + 1)
    oc, os = (outer_cos[:, None], outer_sin[:, None])
    ic, is_ = (inner_cos[None], inner_sin[None])
    both = jnp.stack([oc * ic - os * is_, -(os * ic + oc * is_)])
    return both.astype(BF16).reshape(2 * freqs, seq_len)


def dot(left, right, left_dim, right_dim):
    return lax.dot_general(
        left, right, (((left_dim,), (right_dim,)), ((), ())), preferred_element_type=F32
    )


def spectral_product(left, right, conjugate_left):
    half = left.shape[0] // 2
    left_re, left_im = (left[:half], left[half:])
    right_re, right_im = (right[:half], right[half:])
    if conjugate_left:
        real = left_re * right_re + left_im * right_im
        imag = left_re * right_im - left_im * right_re
    else:
        real = left_re * right_re - left_im * right_im
        imag = left_re * right_im + left_im * right_re
    return jnp.concatenate([real, imag], 0).astype(BF16)


def long_terms(first, freqs, long_filter, product, grad_long):
    waves = table(first, freqs, product.shape[0])
    filter_spec = dot(waves, long_filter, 1, 1)
    product_spec = dot(waves, product, 1, 0)
    grad_spec = dot(waves, grad_long, 1, 0)
    out = dot(waves, spectral_product(filter_spec, product_spec, False), 0, 0)
    back = dot(waves, spectral_product(filter_spec, grad_spec, True), 0, 0)
    lag_grad = dot(spectral_product(product_spec, grad_spec, True), waves, 0, 0)
    return (out, back, lag_grad)


def summed_blocks(value, axis, dim):
    count = lax.axis_size(axis)
    size = value.shape[dim] // count
    me = lax.axis_index(axis)
    total = lax.dynamic_slice_in_dim(value, me * size, size, dim)
    for k in range(1, count):
        sent = lax.dynamic_slice_in_dim(value, (me ^ k) * size, size, dim).astype(BF16)
        total = total + swapped(sent, axis, k).astype(F32)
    return total


def own_share(partial, parts):
    blocks = partial.reshape(parts // 2, 2, -1, partial.shape[-1])
    core = lax.axis_index("context") % 2
    mine = lax.dynamic_index_in_dim(blocks, core, 1, False)
    other = lax.dynamic_index_in_dim(blocks, 1 - core, 1, False).astype(BF16)
    pair = (mine + swapped(other, "context", 1).astype(F32)).astype(BF16)
    groups = [list(range(core, parts, 2)) for core in range(2)]
    came = lax.all_to_all(
        pair, "context", split_axis=0, concat_axis=0, tiled=True, axis_index_groups=groups
    )
    return jnp.sum(came.astype(F32), 0)


def to_channels(blocks):
    came = lax.all_to_all(blocks, "context", split_axis=0, concat_axis=0, tiled=True)
    return came.reshape(-1, came.shape[-1])


def to_positions(blocks):
    return lax.all_to_all(blocks, "context", split_axis=0, concat_axis=0, tiled=True)


def body(projected, short_taps, long_filter, skip_gain, out_proj, cotangent):
    rows, width = projected.shape
    chans = width // 3
    parts_dp, parts = (lax.axis_size("dp"), lax.axis_size("context"))
    blk = chans // parts
    seq_len = rows * parts
    scale_factor = 1.0 / math.sqrt(seq_len * parts_dp)
    me_dp = lax.axis_index("dp").astype(jnp.int32)[None]
    plane = jax.ShapeDtypeStruct((parts, rows, blk), BF16)

    prev_rows = passed_along(projected[rows - 2 :], "context", 1).astype(F32)
    cots = [cotangent] + [swapped(cotangent, "dp", k) for k in range(1, parts_dp)]
    query, keyed, valued, product_out = call(
        short_kernel, "short_convs", [plane] * 4, 0, projected, prev_rows, short_taps
    )
    heads = jnp.stack([keyed[:, :2], valued[:, :2]])
    pair_after = passed_along(heads, "context", -1).astype(F32)
    product = to_channels(product_out)

    found = [dot(cot, out_proj, 1, 1).astype(BF16) for cot in cots]
    found = [found[0]] + [swapped(found[k], "dp", k) for k in range(1, parts_dp)]
    gate_grad, grad_long_out = call(
        grad_long_kernel, "grad_long", [plane] * 2, 1, me_dp, query, *found
    )
    grad_long = to_channels(grad_long_out)

    filter_b = long_filter.astype(BF16)
    freqs = seq_len if seq_len <= 1024 else 256
    if freqs == seq_len:
        terms = long_terms(0, freqs, filter_b, product, grad_long)
    else:

        def step(carry, first):
            new = long_terms(first, freqs, filter_b, product, grad_long)
            return (tuple(a + b for a, b in zip(carry, new)), None)

        zero = jnp.zeros((seq_len, blk), F32)
        start = (zero, zero, jnp.zeros((blk, seq_len), F32))
        terms, _ = lax.scan(step, start, jnp.arange(0, seq_len, freqs))
    out_sum, back_sum, lag_sum = terms
    inverse = 1.0 / seq_len
    product_f, grad_long_f = (product.astype(F32), grad_long.astype(F32))
    long_chan = (out_sum * inverse + skip_gain[None, :] * product_f).astype(BF16)
    long_out = to_positions(long_chan.reshape(parts, rows, blk))
    back_chan = (back_sum * inverse + skip_gain[None, :] * grad_long_f).astype(BF16)
    back_blocks = back_chan.reshape(parts, rows, blk)
    next_heads = jnp.concatenate([back_blocks[1:, :2], jnp.zeros((1, 2, blk), BF16)], 0)
    grad_product = to_positions(jnp.concatenate([back_blocks, next_heads], 1))

    piece = jax.ShapeDtypeStruct((rows, chans // parts_dp), BF16)
    gates = call(gate_kernel, "gate", [piece] * parts_dp, 1, me_dp, query, long_out)
    gates = [gates[0]] + [swapped(gates[k], "dp", k) for k in range(1, parts_dp)]
    proj_sum = dot(jnp.concatenate(gates, 0), jnp.concatenate(cots, 0), 0, 0)
    grad_proj = own_share(proj_sum, parts) * scale_factor

    query_heads = gate_grad[:, :2].astype(F32) * long_out[:, :2].astype(F32)
    query_after = passed_along(query_heads, "context", -1)
    grad_inputs, tap_sums = call(
        final_kernel,
        "stream_grads",
        [
            jax.ShapeDtypeStruct((rows, width), BF16),
            jax.ShapeDtypeStruct((parts, 9, blk), F32),
        ],
        0,
        projected,
        prev_rows,
        short_taps,
        gate_grad,
        long_out,
        grad_product,
        keyed,
        valued,
        query_after,
        pair_after,
    )

    grad_filter = summed_blocks(lag_sum, "dp", 1) * (scale_factor * inverse)
    skip_sum = jnp.sum(grad_long_f * product_f, 0, keepdims=True)
    grad_skip = skip_sum
    for k in range(1, parts_dp):
        grad_skip = grad_skip + swapped(skip_sum, "dp", k)

    shares = lax.all_to_all(tap_sums, "context", split_axis=0, concat_axis=0, tiled=True)
    share = jnp.sum(shares, 0)
    total = share
    for k in range(1, parts_dp):
        total = total + swapped(share, "dp", k)
    every = jnp.broadcast_to((total * scale_factor)[None], (parts, 9, blk))
    taps_out = lax.all_to_all(every, "context", split_axis=0, concat_axis=0, tiled=True)
    grad_taps = taps_out.reshape(parts, 3, 3, blk).transpose(2, 1, 0, 3).reshape(3, width)
    return (grad_inputs, grad_taps, grad_filter, grad_skip[0] * scale_factor, grad_proj)


def solution(mesh):
    placed = (
        P(("dp", "context"), None),
        P(),
        P("context", None),
        P("context"),
        P("dp", None),
        P(("dp", "context"), None),
    )
    return jax.shard_map(
        body,
        mesh=mesh,
        in_specs=placed,
        out_specs=(
            P(("dp", "context"), None),
            P(),
            P("context", "dp"),
            P("context"),
            P(("dp", "context"), None),
        ),
        check_vma=False,
    )
```

```python
import math

import jax
import jax.numpy as jnp
from jax import lax
from jax.experimental import pallas as pl
from jax.experimental.pallas import tpu as pltpu
from jax.sharding import PartitionSpec as P

BF16 = jnp.bfloat16
F32 = jnp.float32


def passed_along(value, axis, steps):
    count = lax.axis_size(axis)
    initial, last = (max(0, -steps), min(count, count - steps))
    return lax.ppermute(value, axis, [(source, source + steps) for source in range(initial, last)])


def swapped(value, axis, mask):
    return lax.ppermute(value, axis, [(i, i ^ mask) for i in range(lax.axis_size(axis))])


VMEM = pl.BlockSpec(memory_space=pltpu.VMEM)
SMEM = pl.BlockSpec(memory_space=pltpu.SMEM)


def rows_down(values, steps, before):
    row = lax.broadcasted_iota(jnp.int32, values.shape, 0)
    moved = pltpu.roll(values, steps, axis=0)
    if steps == 1:
        return jnp.where(row == 0, before[1:2], moved)
    return jnp.where(row == 0, before[0:1], jnp.where(row == 1, before[1:2], moved))


def rows_up(values, steps, after):
    count = values.shape[0]
    row = lax.broadcasted_iota(jnp.int32, values.shape, 0)
    moved = pltpu.roll(values, count - steps, axis=0)
    if steps == 1:
        return jnp.where(row == count - 1, after[0:1], moved)
    return jnp.where(row == count - 1, after[1:2], jnp.where(row == count - 2, after[0:1], moved))


def call(kernel, name, outs, smem, *args):
    moved = sum(math.prod(a.shape) * a.dtype.itemsize for a in args)
    return pl.pallas_call(
        kernel,
        out_shape=outs,
        in_specs=[SMEM] * smem + [VMEM] * (len(args) - smem),
        out_specs=[VMEM] * len(outs),
        compiler_params=pltpu.CompilerParams(vmem_limit_bytes=40 * 2**20),
        cost_estimate=pl.CostEstimate(flops=8 * moved, transcendentals=0, bytes_accessed=2 * moved),
        name=name,
    )(*args)


def columns(index, size):
    return slice(index * size, (index + 1) * size)


def short_kernel(proj_ref, prev_ref, taps_ref, query_ref, keyed_ref, valued_ref, product_ref):
    parts, _, blk = query_ref.shape
    for b in range(parts):

        def mixed(stream):
            cols = columns(stream * parts + b, blk)
            values = proj_ref[:, cols].astype(F32)
            before = prev_ref[:, cols]
            taps = taps_ref[:, cols]
            total = taps[0:1] * values + taps[1:2] * rows_down(values, 1, before)
            return (total + taps[2:3] * rows_down(values, 2, before)).astype(BF16)

        query_ref[b] = mixed(0)
        keyed, valued = (mixed(1), mixed(2))
        keyed_ref[b] = keyed
        valued_ref[b] = valued
        product_ref[b] = (keyed.astype(F32) * valued.astype(F32)).astype(BF16)


def grad_long_kernel(me_ref, query_ref, *refs):
    pieces, (gate_grad_ref, grad_long_ref) = refs[:-2], refs[-2:]
    parts, _, blk = query_ref.shape
    ratio = parts // len(pieces)
    for k, piece in enumerate(pieces):
        for i in range(ratio):
            b = (me_ref[0] ^ k) * ratio + i
            values = piece[:, columns(i, blk)]
            gate_grad_ref[b] = values
            grad_long_ref[b] = (values.astype(F32) * query_ref[b].astype(F32)).astype(BF16)


def gate_kernel(me_ref, query_ref, long_ref, *pieces):
    parts, _, blk = query_ref.shape
    ratio = parts // len(pieces)
    for k, piece in enumerate(pieces):
        for i in range(ratio):
            b = (me_ref[0] ^ k) * ratio + i
            gate = query_ref[b].astype(F32) * long_ref[b].astype(F32)
            piece[:, columns(i, blk)] = gate.astype(BF16)


def final_kernel(*refs):
    proj_ref, prev_ref, taps_ref, gate_grad_ref, long_ref, back_ref, keyed_ref, valued_ref = refs[:8]
    query_after_ref, pair_after_ref, out_ref, sums_ref = refs[8:]
    parts, rows, blk = long_ref.shape
    for b in range(parts):
        back = back_ref[b, 0:rows].astype(F32)
        back_after = back_ref[b, rows : rows + 2].astype(F32)
        grads = (
            (
                gate_grad_ref[b].astype(F32) * long_ref[b].astype(F32),
                query_after_ref[b],
            ),
            (back * valued_ref[b].astype(F32), back_after * pair_after_ref[1, b]),
            (back * keyed_ref[b].astype(F32), back_after * pair_after_ref[0, b]),
        )
        for stream, (grad, after) in enumerate(grads):
            cols = columns(stream * parts + b, blk)
            taps = taps_ref[:, cols]
            total = taps[0:1] * grad + taps[1:2] * rows_up(grad, 1, after)
            out_ref[:, cols] = (total + taps[2:3] * rows_up(grad, 2, after)).astype(BF16)
            values = proj_ref[:, cols].astype(F32)
            before = prev_ref[:, cols]
            for j in range(3):
                moved = rows_down(values, j, before) if j else values
                sums_ref[j : j + 1, cols] = jnp.sum(grad * moved, 0, keepdims=True)


def table(first, freqs, seq_len):
    places = jnp.arange(seq_len)
    inner = min(32, freqs)
    outer = freqs // inner

    def waves(odd):
        phases = odd[:, None] * places[None, :] % (4 * seq_len)
        angles = phases.astype(F32) * (2.0 * math.pi / (4 * seq_len))
        return (jnp.cos(angles), jnp.sin(angles))

    outer_cos, outer_sin = waves(2 * (first + inner * jnp.arange(outer)))
    inner_cos, inner_sin = waves(2 * jnp.arange(inner) + 1)
    oc, os = (outer_cos[:, None], outer_sin[:, None])
    ic, is_ = (inner_cos[None], inner_sin[None])
    both = jnp.stack([oc * ic - os * is_, -(os * ic + oc * is_)])
    return both.astype(BF16).reshape(2 * freqs, seq_len)


def dot(left, right, left_dim, right_dim):
    return lax.dot_general(
        left, right, (((left_dim,), (right_dim,)), ((), ())), preferred_element_type=F32
    )


def spectral_product(left, right, conjugate_left):
    half = left.shape[0] // 2
    left_re, left_im = (left[:half], left[half:])
    right_re, right_im = (right[:half], right[half:])
    if conjugate_left:
        real = left_re * right_re + left_im * right_im
        imag = left_re * right_im - left_im * right_re
    else:
        real = left_re * right_re - left_im * right_im
        imag = left_re * right_im + left_im * right_re
    return jnp.concatenate([real, imag], 0).astype(BF16)


def ordered(value, *first):
    return lax.optimization_barrier((value, *first))[0]


def transforms(waves, long_filter, product, grad_long):
    filter_spec = dot(waves, long_filter, 1, 1)
    product_spec = dot(waves, product, 1, 0)
    grad_spec = dot(waves, grad_long, 1, 0)
    out = dot(waves, spectral_product(filter_spec, product_spec, False), 0, 0)
    back = dot(waves, spectral_product(filter_spec, grad_spec, True), 0, 0)
    lag_grad = dot(spectral_product(product_spec, grad_spec, True), waves, 0, 0)
    return (out, back, lag_grad)


def all_sum(value, axis, bits):
    for pair in [bits[i : i + 2] for i in range(0, len(bits), 2)]:
        sums = [value]
        for bit in pair:
            sums += [swapped(value, axis, bit)]
        if len(pair) == 2:
            far = swapped(value, axis, pair[0] + pair[1])
            value = (sums[0] + sums[1]) + (sums[2] + far)
        else:
            value = sums[0] + sums[1]
    return value


def bits_of(count, first=1):
    return [1 << i for i in range(count.bit_length() - 1) if 1 << i >= first]


def summed_blocks(value, axis, dim):
    count = lax.axis_size(axis)
    size = value.shape[dim] // count
    me = lax.axis_index(axis)
    total = lax.dynamic_slice_in_dim(value, me * size, size, dim)
    for k in range(1, count):
        sent = lax.dynamic_slice_in_dim(value, (me ^ k) * size, size, dim).astype(BF16)
        total = total + swapped(sent, axis, k).astype(F32)
    return total


def own_share(partial, parts):
    blocks = partial.reshape(parts // 2, 2, -1, partial.shape[-1])
    core = lax.axis_index("context") % 2
    mine = lax.dynamic_index_in_dim(blocks, core, 1, False)
    other = lax.dynamic_index_in_dim(blocks, 1 - core, 1, False).astype(BF16)
    pair = (mine + swapped(other, "context", 1).astype(F32)).astype(BF16)
    row = lax.axis_index("context") // 2
    total = lax.dynamic_index_in_dim(pair, row, 0, False).astype(F32)
    for k in range(1, parts // 2):
        sent = lax.dynamic_index_in_dim(pair, row ^ k, 0, False)
        total = total + swapped(sent, "context", 2 * k).astype(F32)
    return (pair, total)


def to_channels(blocks):
    came = lax.all_to_all(blocks, "context", split_axis=0, concat_axis=0, tiled=True)
    return came.reshape(-1, came.shape[-1])


def to_positions(blocks):
    return lax.all_to_all(blocks, "context", split_axis=0, concat_axis=0, tiled=True)


def body(projected, short_taps, long_filter, skip_gain, out_proj, cotangent):
    rows, width = projected.shape
    chans = width // 3
    parts_dp, parts = (lax.axis_size("dp"), lax.axis_size("context"))
    blk = chans // parts
    seq_len = rows * parts
    scale_factor = 1.0 / math.sqrt(seq_len * parts_dp)
    me_dp = lax.axis_index("dp").astype(jnp.int32)[None]
    plane = jax.ShapeDtypeStruct((parts, rows, blk), BF16)

    prev_rows = passed_along(projected[rows - 2 :], "context", 1).astype(F32)
    cots = [cotangent] + [swapped(cotangent, "dp", k) for k in range(1, parts_dp)]
    query, keyed, valued, product_out = call(
        short_kernel, "short_convs", [plane] * 4, 0, projected, prev_rows, short_taps
    )
    heads = jnp.stack([keyed[:, :2], valued[:, :2]])
    pair_after = passed_along(heads, "context", -1).astype(F32)
    product = to_channels(product_out)

    filter_b = long_filter.astype(BF16)
    inverse = 1.0 / seq_len
    straight = seq_len <= 1024
    weights = out_proj
    if straight:
        waves = table(0, seq_len, seq_len)
        filter_spec = dot(waves, filter_b, 1, 1)
        weights = ordered(out_proj, filter_spec)
    found = [dot(cot, weights, 1, 1).astype(BF16) for cot in cots]
    found = [found[0]] + [swapped(found[k], "dp", k) for k in range(1, parts_dp)]
    gate_grad, grad_long_out = call(
        grad_long_kernel, "grad_long", [plane] * 2, 1, me_dp, query, *found
    )
    grad_long = to_channels(grad_long_out)
    product_f, grad_long_f = (product.astype(F32), grad_long.astype(F32))

    def finished(total, direct):
        return (total * inverse + skip_gain[None, :] * direct).astype(BF16)

    if straight:
        product_spec = dot(waves, ordered(product, grad_long_out), 1, 0)
        out_sum = dot(waves, spectral_product(filter_spec, product_spec, False), 0, 0)
        long_chan = finished(out_sum, product_f)
        grad_spec = dot(waves, ordered(grad_long, long_chan), 1, 0)
        back_sum = dot(waves, spectral_product(filter_spec, grad_spec, True), 0, 0)
        back_chan = finished(back_sum, grad_long_f)
        late_spec = ordered(grad_spec, back_chan)
        lag_sum = dot(spectral_product(product_spec, late_spec, True), waves, 0, 0)
    else:
        freqs = 256

        def step(carry, first):
            new = transforms(table(first, freqs, seq_len), filter_b, product, grad_long)
            return (tuple(a + b for a, b in zip(carry, new)), None)

        zero = jnp.zeros((seq_len, blk), F32)
        start = (zero, zero, jnp.zeros((blk, seq_len), F32))
        terms, _ = lax.scan(step, start, jnp.arange(0, seq_len, freqs))
        out_sum, back_sum, lag_sum = terms
        long_chan = finished(out_sum, product_f)
        back_chan = finished(back_sum, grad_long_f)
    long_out = to_positions(long_chan.reshape(parts, rows, blk))
    back_blocks = back_chan.reshape(parts, rows, blk)
    next_heads = jnp.concatenate([back_blocks[1:, :2], jnp.zeros((1, 2, blk), BF16)], 0)
    grad_product = to_positions(jnp.concatenate([back_blocks, next_heads], 1))

    grad_filter = summed_blocks(lag_sum, "dp", 1) * (scale_factor * inverse)
    skip_sum = jnp.sum(grad_long_f * product_f, 0, keepdims=True)
    grad_skip = all_sum(skip_sum, "dp", bits_of(parts_dp)) * scale_factor

    piece = jax.ShapeDtypeStruct((rows, chans // parts_dp), BF16)
    gates = call(gate_kernel, "gate", [piece] * parts_dp, 1, me_dp, query, long_out)
    gates = [gates[0]] + [swapped(gates[k], "dp", k) for k in range(1, parts_dp)]
    proj_sum = dot(jnp.concatenate(gates, 0), jnp.concatenate(cots, 0), 0, 0)
    pair, share = own_share(proj_sum, parts)
    grad_proj = share * scale_factor
    grad_product = ordered(grad_product, pair, grad_filter, grad_skip)

    query_heads = gate_grad[:, :2].astype(F32) * long_out[:, :2].astype(F32)
    query_after = passed_along(query_heads, "context", -1)
    grad_inputs, tap_sums = call(
        final_kernel,
        "stream_grads",
        [
            jax.ShapeDtypeStruct((rows, width), BF16),
            jax.ShapeDtypeStruct((3, width), F32),
        ],
        0,
        projected,
        prev_rows,
        short_taps,
        gate_grad,
        long_out,
        grad_product,
        keyed,
        valued,
        query_after,
        pair_after,
    )

    tap_sums = tap_sums + swapped(tap_sums, "context", 1)
    tap_sums = all_sum(tap_sums, "dp", bits_of(parts_dp))
    grad_taps = all_sum(tap_sums, "context", bits_of(parts, 2)) * scale_factor
    return (grad_inputs, grad_taps, grad_filter, grad_skip[0], grad_proj)


def solution(mesh):
    placed = (
        P(("dp", "context"), None),
        P(),
        P("context", None),
        P("context"),
        P("dp", None),
        P(("dp", "context"), None),
    )
    return jax.shard_map(
        body,
        mesh=mesh,
        in_specs=placed,
        out_specs=(
            P(("dp", "context"), None),
            P(),
            P("context", "dp"),
            P("context"),
            P(("dp", "context"), None),
        ),
        check_vma=False,
    )
```

```python
import math

import jax
import jax.numpy as jnp
from jax import lax
from jax.experimental import pallas as pl
from jax.experimental.pallas import tpu as pltpu
from jax.sharding import PartitionSpec as P

BF16 = jnp.bfloat16
F32 = jnp.float32


def passed_along(value, axis, steps):
    count = lax.axis_size(axis)
    initial, last = (max(0, -steps), min(count, count - steps))
    return lax.ppermute(value, axis, [(source, source + steps) for source in range(initial, last)])


def swapped(value, axis, mask):
    return lax.ppermute(value, axis, [(i, i ^ mask) for i in range(lax.axis_size(axis))])


VMEM = pl.BlockSpec(memory_space=pltpu.VMEM)
SMEM = pl.BlockSpec(memory_space=pltpu.SMEM)


def rows_down(values, steps, before):
    row = lax.broadcasted_iota(jnp.int32, values.shape, 0)
    moved = pltpu.roll(values, steps, axis=0)
    if steps == 1:
        return jnp.where(row == 0, before[1:2], moved)
    return jnp.where(row == 0, before[0:1], jnp.where(row == 1, before[1:2], moved))


def rows_up(values, steps, after):
    count = values.shape[0]
    row = lax.broadcasted_iota(jnp.int32, values.shape, 0)
    moved = pltpu.roll(values, count - steps, axis=0)
    if steps == 1:
        return jnp.where(row == count - 1, after[0:1], moved)
    return jnp.where(row == count - 1, after[1:2], jnp.where(row == count - 2, after[0:1], moved))


def call(kernel, name, outs, smem, *args):
    moved = sum(math.prod(a.shape) * a.dtype.itemsize for a in args)
    return pl.pallas_call(
        kernel,
        out_shape=outs,
        in_specs=[SMEM] * smem + [VMEM] * (len(args) - smem),
        out_specs=[VMEM] * len(outs),
        compiler_params=pltpu.CompilerParams(vmem_limit_bytes=40 * 2**20),
        cost_estimate=pl.CostEstimate(flops=8 * moved, transcendentals=0, bytes_accessed=2 * moved),
        name=name,
    )(*args)


def columns(index, size):
    return slice(index * size, (index + 1) * size)


def short_kernel(proj_ref, prev_ref, taps_ref, query_ref, keyed_ref, valued_ref, product_ref):
    parts, _, blk = query_ref.shape
    for b in range(parts):

        def mixed(stream):
            cols = columns(stream * parts + b, blk)
            values = proj_ref[:, cols].astype(F32)
            before = prev_ref[:, cols]
            taps = taps_ref[:, cols]
            total = taps[0:1] * values + taps[1:2] * rows_down(values, 1, before)
            return (total + taps[2:3] * rows_down(values, 2, before)).astype(BF16)

        query_ref[b] = mixed(0)
        keyed, valued = (mixed(1), mixed(2))
        keyed_ref[b] = keyed
        valued_ref[b] = valued
        product_ref[b] = (keyed.astype(F32) * valued.astype(F32)).astype(BF16)


def grad_long_kernel(me_ref, query_ref, *refs):
    pieces, (gate_grad_ref, grad_long_ref) = refs[:-2], refs[-2:]
    parts, _, blk = query_ref.shape
    ratio = parts // len(pieces)
    for k, piece in enumerate(pieces):
        for i in range(ratio):
            b = (me_ref[0] ^ k) * ratio + i
            values = piece[:, columns(i, blk)]
            gate_grad_ref[b] = values
            grad_long_ref[b] = (values.astype(F32) * query_ref[b].astype(F32)).astype(BF16)


def place_kernel(me_ref, *refs):
    pieces, out_ref = refs[:-1], refs[-1]
    for k, piece in enumerate(pieces):
        out_ref[me_ref[0] ^ k] = piece[...]


def gate_kernel(me_ref, query_ref, long_ref, *pieces):
    parts, _, blk = query_ref.shape
    ratio = parts // len(pieces)
    for k, piece in enumerate(pieces):
        for i in range(ratio):
            b = (me_ref[0] ^ k) * ratio + i
            gate = query_ref[b].astype(F32) * long_ref[b].astype(F32)
            piece[:, columns(i, blk)] = gate.astype(BF16)


def final_kernel(*refs):
    proj_ref, prev_ref, taps_ref, gate_grad_ref, long_ref, back_ref, keyed_ref, valued_ref = refs[:8]
    query_after_ref, pair_after_ref, skip_ref, out_ref, sums_ref = refs[8:]
    parts, rows, blk = long_ref.shape
    sums_ref[3:4, :] = jnp.zeros((1, sums_ref.shape[1]), F32)
    sums_ref[3:4, 0:blk] = skip_ref[...]
    for b in range(parts):
        back = back_ref[b, 0:rows].astype(F32)
        back_after = back_ref[b, rows : rows + 2].astype(F32)
        grads = (
            (
                gate_grad_ref[b].astype(F32) * long_ref[b].astype(F32),
                query_after_ref[b],
            ),
            (back * valued_ref[b].astype(F32), back_after * pair_after_ref[1, b]),
            (back * keyed_ref[b].astype(F32), back_after * pair_after_ref[0, b]),
        )
        for stream, (grad, after) in enumerate(grads):
            cols = columns(stream * parts + b, blk)
            taps = taps_ref[:, cols]
            total = taps[0:1] * grad + taps[1:2] * rows_up(grad, 1, after)
            out_ref[:, cols] = (total + taps[2:3] * rows_up(grad, 2, after)).astype(BF16)
            values = proj_ref[:, cols].astype(F32)
            before = prev_ref[:, cols]
            for j in range(3):
                moved = rows_down(values, j, before) if j else values
                sums_ref[j : j + 1, cols] = jnp.sum(grad * moved, 0, keepdims=True)


def table(first, freqs, seq_len):
    places = jnp.arange(seq_len)
    inner = min(32, freqs)
    outer = freqs // inner

    def waves(odd):
        phases = odd[:, None] * places[None, :] % (4 * seq_len)
        angles = phases.astype(F32) * (2.0 * math.pi / (4 * seq_len))
        return (jnp.cos(angles), jnp.sin(angles))

    outer_cos, outer_sin = waves(2 * (first + inner * jnp.arange(outer)))
    inner_cos, inner_sin = waves(2 * jnp.arange(inner) + 1)
    oc, os = (outer_cos[:, None], outer_sin[:, None])
    ic, is_ = (inner_cos[None], inner_sin[None])
    both = jnp.stack([oc * ic - os * is_, -(os * ic + oc * is_)])
    return both.astype(BF16).reshape(2 * freqs, seq_len)


def dot(left, right, left_dim, right_dim):
    return lax.dot_general(
        left, right, (((left_dim,), (right_dim,)), ((), ())), preferred_element_type=F32
    )


def spectral_product(left, right, conjugate_left):
    half = left.shape[0] // 2
    left_re, left_im = (left[:half], left[half:])
    right_re, right_im = (right[:half], right[half:])
    if conjugate_left:
        real = left_re * right_re + left_im * right_im
        imag = left_re * right_im - left_im * right_re
    else:
        real = left_re * right_re - left_im * right_im
        imag = left_re * right_im + left_im * right_re
    return jnp.concatenate([real, imag], 0).astype(BF16)


def ordered(value, *first):
    return lax.optimization_barrier((value, *first))[0]


def transforms(waves, long_filter, product, grad_long):
    filter_spec = dot(waves, long_filter, 1, 1)
    product_spec = dot(waves, product, 1, 0)
    grad_spec = dot(waves, grad_long, 1, 0)
    out = dot(waves, spectral_product(filter_spec, product_spec, False), 0, 0)
    back = dot(waves, spectral_product(filter_spec, grad_spec, True), 0, 0)
    lag_grad = dot(spectral_product(product_spec, grad_spec, True), waves, 0, 0)
    return (out, back, lag_grad)


def all_sum(value, axis, bits):
    for pair in [bits[i : i + 2] for i in range(0, len(bits), 2)]:
        sums = [value]
        for bit in pair:
            sums += [swapped(value, axis, bit)]
        if len(pair) == 2:
            far = swapped(value, axis, pair[0] + pair[1])
            value = (sums[0] + sums[1]) + (sums[2] + far)
        else:
            value = sums[0] + sums[1]
    return value


def bits_of(count, first=1):
    return [1 << i for i in range(count.bit_length() - 1) if 1 << i >= first]


def summed_blocks(value, axis, dim):
    count = lax.axis_size(axis)
    size = value.shape[dim] // count
    me = lax.axis_index(axis)
    total = lax.dynamic_slice_in_dim(value, me * size, size, dim)
    for k in range(1, count):
        sent = lax.dynamic_slice_in_dim(value, (me ^ k) * size, size, dim).astype(BF16)
        total = total + swapped(sent, axis, k).astype(F32)
    return total


def own_share(partial, parts):
    blocks = partial.reshape(parts // 2, 2, -1, partial.shape[-1])
    core = lax.axis_index("context") % 2
    mine = lax.dynamic_index_in_dim(blocks, core, 1, False)
    other = lax.dynamic_index_in_dim(blocks, 1 - core, 1, False).astype(BF16)
    pair = (mine + swapped(other, "context", 1).astype(F32)).astype(BF16)
    row = lax.axis_index("context") // 2
    shares = [lax.dynamic_index_in_dim(pair, row, 0, False)]
    for k in range(1, parts // 2):
        sent = lax.dynamic_index_in_dim(pair, row ^ k, 0, False)
        shares.append(swapped(sent, "context", 2 * k))
    return (other, shares)


def to_channels(blocks):
    came = lax.all_to_all(blocks, "context", split_axis=0, concat_axis=0, tiled=True)
    return came.reshape(-1, came.shape[-1])


def to_positions(blocks):
    return lax.all_to_all(blocks, "context", split_axis=0, concat_axis=0, tiled=True)


def body(projected, short_taps, long_filter, skip_gain, out_proj, cotangent):
    rows, width = projected.shape
    chans = width // 3
    parts_dp, parts = (lax.axis_size("dp"), lax.axis_size("context"))
    blk = chans // parts
    seq_len = rows * parts
    scale_factor = 1.0 / math.sqrt(seq_len * parts_dp)
    me = lax.axis_index("context").astype(jnp.int32)
    me_dp = lax.axis_index("dp").astype(jnp.int32)[None]
    plane = jax.ShapeDtypeStruct((parts, rows, blk), BF16)

    prev_rows = passed_along(projected[rows - 2 :], "context", 1).astype(F32)
    cots = [cotangent] + [swapped(cotangent, "dp", k) for k in range(1, parts_dp)]
    query, keyed, valued, product_out = call(
        short_kernel, "short_convs", [plane] * 4, 0, projected, prev_rows, short_taps
    )
    product = to_channels(product_out)

    filter_b = long_filter.astype(BF16)
    inverse = 1.0 / seq_len
    straight = seq_len <= 1024
    weights = out_proj
    if straight:
        waves = table(0, seq_len, seq_len)
        filter_spec = dot(waves, filter_b, 1, 1)
        weights = ordered(out_proj, filter_spec)
    found = [dot(cot, weights, 1, 1).astype(BF16) for cot in cots]
    found = [found[0]] + [swapped(found[k], "dp", k) for k in range(1, parts_dp)]
    gate_grad, grad_long_out = call(
        grad_long_kernel, "grad_long", [plane] * 2, 1, me_dp, query, *found
    )
    grad_long = to_channels(grad_long_out)
    heads = ordered(jnp.stack([keyed[:, :2], valued[:, :2]]), grad_long_out)
    pair_after = passed_along(heads, "context", -1).astype(F32)
    product_f, grad_long_f = (product.astype(F32), grad_long.astype(F32))

    def finished(total, direct):
        return (total * inverse + skip_gain[None, :] * direct).astype(BF16)

    if straight:
        product_spec = dot(waves, ordered(product, grad_long_out), 1, 0)
        out_sum = dot(waves, spectral_product(filter_spec, product_spec, False), 0, 0)
        long_chan = finished(out_sum, product_f)
        grad_spec = dot(waves, ordered(grad_long, long_chan), 1, 0)
        back_sum = dot(waves, spectral_product(filter_spec, grad_spec, True), 0, 0)
        back_chan = finished(back_sum, grad_long_f)
        late_spec = ordered(grad_spec, back_chan)
        lag_sum = dot(spectral_product(product_spec, late_spec, True), waves, 0, 0)
    else:
        freqs = 256

        def step(carry, first):
            new = transforms(table(first, freqs, seq_len), filter_b, product, grad_long)
            return (tuple(a + b for a, b in zip(carry, new)), None)

        zero = jnp.zeros((seq_len, blk), F32)
        start = (zero, zero, jnp.zeros((blk, seq_len), F32))
        terms, _ = lax.scan(step, start, jnp.arange(0, seq_len, freqs))
        out_sum, back_sum, lag_sum = terms
        long_chan = finished(out_sum, product_f)
        back_chan = finished(back_sum, grad_long_f)
    long_blocks = long_chan.reshape(parts, rows, blk)
    long_sent = [lax.dynamic_index_in_dim(long_blocks, me ^ k, 0, False) for k in range(parts)]
    long_came = [long_sent[0]] + [swapped(long_sent[k], "context", k) for k in range(1, parts)]
    back_blocks = back_chan.reshape(parts, rows, blk)
    next_heads = jnp.concatenate([back_blocks[1:, :2], jnp.zeros((1, 2, blk), BF16)], 0)
    back_sent = jnp.concatenate([back_blocks, next_heads], 1)
    grad_product = to_positions(back_sent)
    long_came = lax.optimization_barrier((*long_came, back_sent))[:parts]
    (long_out,) = call(place_kernel, "long_out", [plane], 1, me[None], *long_came)

    grad_filter = summed_blocks(lag_sum, "dp", 1) * (scale_factor * inverse)
    skip_sum = jnp.sum(grad_long_f * product_f, 0, keepdims=True)

    piece = jax.ShapeDtypeStruct((rows, chans // parts_dp), BF16)
    gates = call(gate_kernel, "gate", [piece] * parts_dp, 1, me_dp, query, long_out)
    gates = [gates[0]] + [swapped(gates[k], "dp", k) for k in range(1, parts_dp)]
    query_heads = gate_grad[:, :2].astype(F32) * long_out[:, :2].astype(F32)
    query_after = passed_along(query_heads, "context", -1)
    early = (grad_product, grad_filter, skip_sum, pair_after, query_after)
    gate_all = ordered(jnp.concatenate(gates, 0), *early)
    proj_sum = dot(gate_all, jnp.concatenate(cots, 0), 0, 0)
    other, shares = own_share(proj_sum, parts)
    grad_product = ordered(grad_product, other)

    grad_inputs, tap_sums = call(
        final_kernel,
        "stream_grads",
        [
            jax.ShapeDtypeStruct((rows, width), BF16),
            jax.ShapeDtypeStruct((4, width), F32),
        ],
        0,
        projected,
        prev_rows,
        short_taps,
        gate_grad,
        long_out,
        grad_product,
        keyed,
        valued,
        query_after,
        pair_after,
        skip_sum,
    )

    tap_sums = all_sum(tap_sums, "dp", bits_of(parts_dp))
    grad_skip = tap_sums[3, :blk] * scale_factor
    tap_sums = ordered(tap_sums[:3], shares[1])
    tap_sums = tap_sums + swapped(tap_sums, "context", 1)
    tap_sums = ordered(tap_sums, *shares[2:])
    grad_taps = all_sum(tap_sums, "context", bits_of(parts, 2)) * scale_factor
    grad_proj = sum(share.astype(F32) for share in shares) * scale_factor
    return (grad_inputs, grad_taps, grad_filter, grad_skip, grad_proj)


def solution(mesh):
    placed = (
        P(("dp", "context"), None),
        P(),
        P("context", None),
        P("context"),
        P("dp", None),
        P(("dp", "context"), None),
    )
    return jax.shard_map(
        body,
        mesh=mesh,
        in_specs=placed,
        out_specs=(
            P(("dp", "context"), None),
            P(),
            P("context", "dp"),
            P("context"),
            P(("dp", "context"), None),
        ),
        check_vma=False,
    )
```

```python
import math

import jax
import jax.numpy as jnp
from jax import lax
from jax.experimental import pallas as pl
from jax.experimental.pallas import tpu as pltpu
from jax.sharding import PartitionSpec as P

BF16 = jnp.bfloat16
F32 = jnp.float32


def passed_along(value, axis, steps):
    count = lax.axis_size(axis)
    initial, last = (max(0, -steps), min(count, count - steps))
    return lax.ppermute(value, axis, [(source, source + steps) for source in range(initial, last)])


def swapped(value, axis, mask):
    return lax.ppermute(value, axis, [(i, i ^ mask) for i in range(lax.axis_size(axis))])


SMEM = pl.BlockSpec(memory_space=pltpu.SMEM)


def rows_down(values, steps, before):
    row = lax.broadcasted_iota(jnp.int32, values.shape, 0)
    moved = pltpu.roll(values, steps, axis=0)
    if steps == 1:
        return jnp.where(row == 0, before[1:2], moved)
    return jnp.where(row == 0, before[0:1], jnp.where(row == 1, before[1:2], moved))


def rows_up(values, steps, after):
    count = values.shape[0]
    row = lax.broadcasted_iota(jnp.int32, values.shape, 0)
    moved = pltpu.roll(values, count - steps, axis=0)
    if steps == 1:
        return jnp.where(row == count - 1, after[0:1], moved)
    return jnp.where(row == count - 1, after[1:2], jnp.where(row == count - 2, after[0:1], moved))


def call(kernel, name, outs, smem, limit, *args):
    arrays = args[smem:]
    count, given = (len(arrays), len(outs))

    def run(*refs):
        ends = refs[smem : smem + count + given]
        *buffers, sems = refs[smem + count + given :]
        copies = []
        for i, (end, buffer) in enumerate(zip(ends, buffers)):
            pair = (end, buffer) if i < count else (buffer, end)
            copies.append(pltpu.make_async_copy(*pair, sems.at[i]))
        for copy in copies[:count]:
            copy.start()
        for copy in copies[:count]:
            copy.wait()
        kernel(*refs[:smem], *buffers)
        for copy in copies[count:]:
            copy.start()
        for copy in copies[count:]:
            copy.wait()

    anywhere = pl.BlockSpec(memory_space=pl.ANY)
    return pl.pallas_call(
        run,
        out_shape=outs,
        in_specs=[SMEM] * smem + [anywhere] * count,
        out_specs=[anywhere] * given,
        scratch_shapes=[pltpu.VMEM(a.shape, a.dtype) for a in (*arrays, *outs)]
        + [pltpu.SemaphoreType.DMA((count + given,))],
        compiler_params=pltpu.CompilerParams(vmem_limit_bytes=limit * 2**20),
        cost_estimate=pl.CostEstimate(flops=0, transcendentals=0, bytes_accessed=0),
        name=name,
    )(*args)


def columns(index, size):
    return slice(index * size, (index + 1) * size)


def short_kernel(proj_ref, prev_ref, taps_ref, query_ref, keyed_ref, valued_ref, product_ref):
    parts, _, blk = query_ref.shape
    for b in range(parts):

        def mixed(stream):
            cols = columns(stream * parts + b, blk)
            values = proj_ref[:, cols].astype(F32)
            before = prev_ref[:, cols]
            taps = taps_ref[:, cols]
            total = taps[0:1] * values + taps[1:2] * rows_down(values, 1, before)
            return (total + taps[2:3] * rows_down(values, 2, before)).astype(BF16)

        query_ref[b] = mixed(0)
        keyed, valued = (mixed(1), mixed(2))
        keyed_ref[b] = keyed
        valued_ref[b] = valued
        product_ref[b] = (keyed.astype(F32) * valued.astype(F32)).astype(BF16)


def grad_long_kernel(me_ref, query_ref, *refs):
    pieces, (gate_grad_ref, grad_long_ref) = refs[:-2], refs[-2:]
    parts, _, blk = query_ref.shape
    ratio = parts // len(pieces)
    for k, piece in enumerate(pieces):
        for i in range(ratio):
            b = (me_ref[0] ^ k) * ratio + i
            values = piece[:, columns(i, blk)]
            gate_grad_ref[b] = values
            grad_long_ref[b] = (values.astype(F32) * query_ref[b].astype(F32)).astype(BF16)


def gate_kernel(me_ref, me_dp_ref, query_ref, *refs):
    parts, _, blk = query_ref.shape
    came, long_ref, pieces = refs[:parts], refs[parts], refs[parts + 1 :]
    ratio = parts // len(pieces)
    for k, piece in enumerate(came):
        long_ref[me_ref[0] ^ k] = piece[...]
    for k, piece in enumerate(pieces):
        for i in range(ratio):
            b = (me_dp_ref[0] ^ k) * ratio + i
            gate = query_ref[b].astype(F32) * long_ref[b].astype(F32)
            piece[:, columns(i, blk)] = gate.astype(BF16)


def final_kernel(*refs):
    proj_ref, prev_ref, taps_ref, gate_grad_ref, long_ref, back_ref, keyed_ref, valued_ref = refs[:8]
    query_after_ref, pair_after_ref, skip_ref, out_ref, sums_ref = refs[8:]
    parts, rows, blk = long_ref.shape
    sums_ref[3:4, :] = jnp.zeros((1, sums_ref.shape[1]), F32)
    sums_ref[3:4, 0:blk] = skip_ref[...]
    for b in range(parts):
        back = back_ref[b, 0:rows].astype(F32)
        back_after = back_ref[b, rows : rows + 2].astype(F32)
        grads = (
            (
                gate_grad_ref[b].astype(F32) * long_ref[b].astype(F32),
                query_after_ref[b],
            ),
            (back * valued_ref[b].astype(F32), back_after * pair_after_ref[1, b]),
            (back * keyed_ref[b].astype(F32), back_after * pair_after_ref[0, b]),
        )
        for stream, (grad, after) in enumerate(grads):
            cols = columns(stream * parts + b, blk)
            taps = taps_ref[:, cols]
            total = taps[0:1] * grad + taps[1:2] * rows_up(grad, 1, after)
            out_ref[:, cols] = (total + taps[2:3] * rows_up(grad, 2, after)).astype(BF16)
            values = proj_ref[:, cols].astype(F32)
            before = prev_ref[:, cols]
            for j in range(3):
                moved = rows_down(values, j, before) if j else values
                sums_ref[j : j + 1, cols] = jnp.sum(grad * moved, 0, keepdims=True)


def table(first, freqs, seq_len):
    places = jnp.arange(seq_len)
    inner = min(32, freqs)
    outer = freqs // inner

    def waves(odd):
        phases = odd[:, None] * places[None, :] % (4 * seq_len)
        angles = phases.astype(F32) * (2.0 * math.pi / (4 * seq_len))
        return (jnp.cos(angles), jnp.sin(angles))

    outer_cos, outer_sin = waves(2 * (first + inner * jnp.arange(outer)))
    inner_cos, inner_sin = waves(2 * jnp.arange(inner) + 1)
    oc, os = (outer_cos[:, None], outer_sin[:, None])
    ic, is_ = (inner_cos[None], inner_sin[None])
    both = jnp.stack([oc * ic - os * is_, -(os * ic + oc * is_)])
    return both.astype(BF16).reshape(2 * freqs, seq_len)


def dot(left, right, left_dim, right_dim):
    return lax.dot_general(
        left, right, (((left_dim,), (right_dim,)), ((), ())), preferred_element_type=F32
    )


def spectral_product(left, right, conjugate_left):
    half = left.shape[0] // 2
    left_re, left_im = (left[:half], left[half:])
    right_re, right_im = (right[:half], right[half:])
    if conjugate_left:
        real = left_re * right_re + left_im * right_im
        imag = left_re * right_im - left_im * right_re
    else:
        real = left_re * right_re - left_im * right_im
        imag = left_re * right_im + left_im * right_re
    return jnp.concatenate([real, imag], 0).astype(BF16)


def ordered(value, *first):
    return lax.optimization_barrier((value, *first))[0]


def transforms(waves, long_filter, product, grad_long):
    filter_spec = dot(waves, long_filter, 1, 1)
    product_spec = dot(waves, product, 1, 0)
    grad_spec = dot(waves, grad_long, 1, 0)
    out = dot(waves, spectral_product(filter_spec, product_spec, False), 0, 0)
    back = dot(waves, spectral_product(filter_spec, grad_spec, True), 0, 0)
    lag_grad = dot(spectral_product(product_spec, grad_spec, True), waves, 0, 0)
    return (out, back, lag_grad)


def all_sum(value, axis, bits):
    for pair in [bits[i : i + 2] for i in range(0, len(bits), 2)]:
        sums = [value]
        for bit in pair:
            sums += [swapped(value, axis, bit)]
        if len(pair) == 2:
            far = swapped(value, axis, pair[0] + pair[1])
            value = (sums[0] + sums[1]) + (sums[2] + far)
        else:
            value = sums[0] + sums[1]
    return value


def bits_of(count, first=1):
    return [1 << i for i in range(count.bit_length() - 1) if 1 << i >= first]


def own_share(partial, parts):
    blocks = partial.reshape(parts // 2, 2, -1, partial.shape[-1])
    core = lax.axis_index("context") % 2
    mine = lax.dynamic_index_in_dim(blocks, core, 1, False)
    other = lax.dynamic_index_in_dim(blocks, 1 - core, 1, False).astype(BF16)
    pair = (mine + swapped(other, "context", 1).astype(F32)).astype(BF16)
    row = lax.axis_index("context") // 2
    shares = [lax.dynamic_index_in_dim(pair, row, 0, False)]
    for k in range(1, parts // 2):
        sent = lax.dynamic_index_in_dim(pair, row ^ k, 0, False)
        shares.append(swapped(sent, "context", 2 * k))
    return (pair, shares)


def to_channels(blocks):
    came = lax.all_to_all(blocks, "context", split_axis=0, concat_axis=0, tiled=True)
    return came.reshape(-1, came.shape[-1])


def to_positions(blocks):
    return lax.all_to_all(blocks, "context", split_axis=0, concat_axis=0, tiled=True)


def body(projected, short_taps, long_filter, skip_gain, out_proj, cotangent):
    rows, width = projected.shape
    chans = width // 3
    parts_dp, parts = (lax.axis_size("dp"), lax.axis_size("context"))
    blk = chans // parts
    seq_len = rows * parts
    scale_factor = 1.0 / math.sqrt(seq_len * parts_dp)
    me = lax.axis_index("context").astype(jnp.int32)
    me_dp = lax.axis_index("dp").astype(jnp.int32)[None]
    plane = jax.ShapeDtypeStruct((parts, rows, blk), BF16)

    prev_rows = passed_along(projected[rows - 2 :], "context", 1).astype(F32)
    cots = [cotangent] + [swapped(cotangent, "dp", k) for k in range(1, parts_dp)]
    query, keyed, valued, product_out = call(
        short_kernel, "short_convs", [plane] * 4, 0, 60, projected, prev_rows, short_taps
    )
    product = to_channels(product_out)

    filter_b = long_filter.astype(BF16)
    inverse = 1.0 / seq_len
    straight = seq_len <= 1024
    weights = out_proj
    if straight:
        waves = table(0, seq_len, seq_len)
        filter_spec = dot(waves, filter_b, 1, 1)
        weights = ordered(out_proj, filter_spec)
    found = [dot(cot, weights, 1, 1).astype(BF16) for cot in cots]
    found = [found[0]] + [swapped(found[k], "dp", k) for k in range(1, parts_dp)]
    gate_grad, grad_long_out = call(
        grad_long_kernel, "grad_long", [plane] * 2, 1, 12, me_dp, query, *found
    )
    grad_long = to_channels(grad_long_out)
    product_f, grad_long_f = (product.astype(F32), grad_long.astype(F32))

    def finished(total, direct):
        return (total * inverse + skip_gain[None, :] * direct).astype(BF16)

    if straight:
        product_spec = dot(waves, ordered(product, grad_long_out), 1, 0)
        out_sum = dot(waves, spectral_product(filter_spec, product_spec, False), 0, 0)
        long_chan = finished(out_sum, product_f)
        grad_spec = dot(waves, ordered(grad_long, long_chan), 1, 0)
        back_sum = dot(waves, spectral_product(filter_spec, grad_spec, True), 0, 0)
        back_chan = finished(back_sum, grad_long_f)
        late_spec = ordered(grad_spec, back_chan)
        lag_sum = dot(spectral_product(product_spec, late_spec, True), waves, 0, 0)
    else:
        freqs = 256

        def step(carry, first):
            new = transforms(table(first, freqs, seq_len), filter_b, product, grad_long)
            return (tuple(a + b for a, b in zip(carry, new)), None)

        zero = jnp.zeros((seq_len, blk), F32)
        start = (zero, zero, jnp.zeros((blk, seq_len), F32))
        terms, _ = lax.scan(step, start, jnp.arange(0, seq_len, freqs))
        out_sum, back_sum, lag_sum = terms
        long_chan = finished(out_sum, product_f)
        back_chan = finished(back_sum, grad_long_f)
    long_blocks = long_chan.reshape(parts, rows, blk)
    long_sent = [lax.dynamic_index_in_dim(long_blocks, me ^ k, 0, False) for k in range(parts)]
    long_came = [long_sent[0]] + [swapped(long_sent[k], "context", k) for k in range(1, parts)]
    back_blocks = back_chan.reshape(parts, rows, blk)
    next_heads = jnp.concatenate([back_blocks[1:, :2], jnp.zeros((1, 2, blk), BF16)], 0)
    back_sent = jnp.concatenate([back_blocks, next_heads], 1)
    grad_product = to_positions(back_sent)
    heads = ordered(jnp.stack([keyed[:, :2], valued[:, :2]]), back_sent)
    pair_after = passed_along(heads, "context", -1).astype(F32)
    long_came = lax.optimization_barrier((*long_came, back_sent))[:parts]

    grad_filter = lax.psum_scatter(lag_sum, "dp", scatter_dimension=1, tiled=True)
    grad_filter = grad_filter * (scale_factor * inverse)
    skip_sum = jnp.sum(grad_long_f * product_f, 0, keepdims=True)

    piece = jax.ShapeDtypeStruct((rows, chans // parts_dp), BF16)
    long_out, *gates = call(
        gate_kernel, "gate", [plane] + [piece] * parts_dp, 2, 12, me[None], me_dp, query, *long_came
    )
    gates = [gates[0]] + [swapped(gates[k], "dp", k) for k in range(1, parts_dp)]
    query_heads = gate_grad[:, :2].astype(F32) * long_out[:, :2].astype(F32)
    query_after = passed_along(query_heads, "context", -1)
    early = (grad_product, lag_sum, skip_sum, pair_after, query_after)
    gate_all = ordered(jnp.concatenate(gates, 0), *early)
    proj_sum = dot(gate_all, jnp.concatenate(cots, 0), 0, 0)
    pair, shares = own_share(proj_sum, parts)
    grad_product = ordered(grad_product, pair)

    grad_inputs, tap_sums = call(
        final_kernel,
        "stream_grads",
        [
            jax.ShapeDtypeStruct((rows, width), BF16),
            jax.ShapeDtypeStruct((4, width), F32),
        ],
        0,
        60,
        projected,
        prev_rows,
        short_taps,
        gate_grad,
        long_out,
        grad_product,
        keyed,
        valued,
        query_after,
        pair_after,
        skip_sum,
    )

    tap_sums = all_sum(ordered(tap_sums, grad_filter), "dp", bits_of(parts_dp))
    grad_skip = tap_sums[3, :blk] * scale_factor
    tap_sums = tap_sums[:3] + swapped(tap_sums[:3], "context", 1)
    tap_sums = ordered(tap_sums, *shares[1:])
    grad_taps = all_sum(tap_sums, "context", bits_of(parts, 2)) * scale_factor
    grad_proj = sum(share.astype(F32) for share in shares) * scale_factor
    return (grad_inputs, grad_taps, grad_filter, grad_skip, grad_proj)


def solution(mesh):
    placed = (
        P(("dp", "context"), None),
        P(),
        P("context", None),
        P("context"),
        P("dp", None),
        P(("dp", "context"), None),
    )
    return jax.shard_map(
        body,
        mesh=mesh,
        in_specs=placed,
        out_specs=(
            P(("dp", "context"), None),
            P(),
            P("context", "dp"),
            P("context"),
            P(("dp", "context"), None),
        ),
        check_vma=False,
    )
```

```python
import math

import jax
import jax.numpy as jnp
from jax import lax
from jax.experimental import pallas as pl
from jax.experimental.pallas import tpu as pltpu
from jax.sharding import PartitionSpec as P

BF16 = jnp.bfloat16
F32 = jnp.float32


def passed_along(value, axis, steps):
    count = lax.axis_size(axis)
    initial, last = (max(0, -steps), min(count, count - steps))
    return lax.ppermute(value, axis, [(source, source + steps) for source in range(initial, last)])


def swapped(value, axis, mask):
    return lax.ppermute(value, axis, [(i, i ^ mask) for i in range(lax.axis_size(axis))])


SMEM = pl.BlockSpec(memory_space=pltpu.SMEM)


def rows_down(values, steps, before):
    row = lax.broadcasted_iota(jnp.int32, values.shape, 0)
    moved = pltpu.roll(values, steps, axis=0)
    if steps == 1:
        return jnp.where(row == 0, before[1:2], moved)
    return jnp.where(row == 0, before[0:1], jnp.where(row == 1, before[1:2], moved))


def rows_up(values, steps, after):
    count = values.shape[0]
    row = lax.broadcasted_iota(jnp.int32, values.shape, 0)
    moved = pltpu.roll(values, count - steps, axis=0)
    if steps == 1:
        return jnp.where(row == count - 1, after[0:1], moved)
    return jnp.where(row == count - 1, after[1:2], jnp.where(row == count - 2, after[0:1], moved))


def call(kernel, name, outs, smem, limit, *args):
    arrays = args[smem:]
    count, given = (len(arrays), len(outs))

    def run(*refs):
        ends = refs[smem : smem + count + given]
        *buffers, sems = refs[smem + count + given :]
        copies = []
        for i, (end, buffer) in enumerate(zip(ends, buffers)):
            pair = (end, buffer) if i < count else (buffer, end)
            copies.append(pltpu.make_async_copy(*pair, sems.at[i]))
        for copy in copies[:count]:
            copy.start()
        for copy in copies[:count]:
            copy.wait()
        kernel(*refs[:smem], *buffers)
        for copy in copies[count:]:
            copy.start()
        for copy in copies[count:]:
            copy.wait()

    anywhere = pl.BlockSpec(memory_space=pl.ANY)
    return pl.pallas_call(
        run,
        out_shape=outs,
        in_specs=[SMEM] * smem + [anywhere] * count,
        out_specs=[anywhere] * given,
        scratch_shapes=[pltpu.VMEM(a.shape, a.dtype) for a in (*arrays, *outs)]
        + [pltpu.SemaphoreType.DMA((count + given,))],
        compiler_params=pltpu.CompilerParams(vmem_limit_bytes=limit * 2**20),
        cost_estimate=pl.CostEstimate(flops=0, transcendentals=0, bytes_accessed=0),
        name=name,
    )(*args)


def columns(index, size):
    return slice(index * size, (index + 1) * size)


def short_kernel(proj_ref, prev_ref, taps_ref, query_ref, keyed_ref, valued_ref, product_ref):
    parts, _, blk = query_ref.shape
    for b in range(parts):

        def mixed(stream):
            cols = columns(stream * parts + b, blk)
            values = proj_ref[:, cols].astype(F32)
            before = prev_ref[:, cols]
            taps = taps_ref[:, cols]
            total = taps[0:1] * values + taps[1:2] * rows_down(values, 1, before)
            return (total + taps[2:3] * rows_down(values, 2, before)).astype(BF16)

        query_ref[b] = mixed(0)
        keyed, valued = (mixed(1), mixed(2))
        keyed_ref[b] = keyed
        valued_ref[b] = valued
        product_ref[b] = (keyed.astype(F32) * valued.astype(F32)).astype(BF16)


def grad_long_kernel(me_ref, query_ref, *refs):
    pieces, (gate_grad_ref, grad_long_ref) = refs[:-2], refs[-2:]
    parts, _, blk = query_ref.shape
    ratio = parts // len(pieces)
    for k, piece in enumerate(pieces):
        for i in range(ratio):
            b = (me_ref[0] ^ k) * ratio + i
            values = piece[:, columns(i, blk)]
            gate_grad_ref[b] = values
            grad_long_ref[b] = (values.astype(F32) * query_ref[b].astype(F32)).astype(BF16)


def gate_kernel(me_ref, me_dp_ref, query_ref, *refs):
    parts, _, blk = query_ref.shape
    came, long_ref, pieces = refs[: parts // 2], refs[parts // 2], refs[parts // 2 + 1 :]
    ratio = parts // len(pieces)
    size = blk * ratio // parts
    for k, piece in enumerate(came):
        b = me_ref[0] ^ (2 * k)
        long_ref[b] = piece[0]
        long_ref[b ^ 1] = piece[1]
    for k, piece in enumerate(pieces):
        for i in range(ratio):
            b = (me_dp_ref[0] ^ k) * ratio + i
            gate = (query_ref[b].astype(F32) * long_ref[b].astype(F32)).astype(BF16)
            for q in range(blk // size):
                c = i * (blk // size) + q
                piece[:, columns(c % 2 * (parts // 2) + c // 2, size)] = gate[:, columns(q, size)]


def final_kernel(*refs):
    proj_ref, prev_ref, taps_ref, gate_grad_ref, long_ref, back_ref, keyed_ref, valued_ref = refs[:8]
    query_after_ref, pair_after_ref, skip_ref, out_ref, sums_ref = refs[8:]
    parts, rows, blk = long_ref.shape
    sums_ref[3:4, :] = jnp.zeros((1, sums_ref.shape[1]), F32)
    sums_ref[3:4, 0:blk] = skip_ref[...]
    for b in range(parts):
        back = back_ref[b, 0:rows].astype(F32)
        back_after = back_ref[b, rows : rows + 2].astype(F32)
        grads = (
            (
                gate_grad_ref[b].astype(F32) * long_ref[b].astype(F32),
                query_after_ref[b],
            ),
            (back * valued_ref[b].astype(F32), back_after * pair_after_ref[1, b]),
            (back * keyed_ref[b].astype(F32), back_after * pair_after_ref[0, b]),
        )
        for stream, (grad, after) in enumerate(grads):
            cols = columns(stream * parts + b, blk)
            taps = taps_ref[:, cols]
            total = taps[0:1] * grad + taps[1:2] * rows_up(grad, 1, after)
            out_ref[:, cols] = (total + taps[2:3] * rows_up(grad, 2, after)).astype(BF16)
            values = proj_ref[:, cols].astype(F32)
            before = prev_ref[:, cols]
            for j in range(3):
                moved = rows_down(values, j, before) if j else values
                sums_ref[j : j + 1, cols] = jnp.sum(grad * moved, 0, keepdims=True)


def table(first, freqs, seq_len):
    places = jnp.arange(seq_len)
    inner = min(32, freqs)
    outer = freqs // inner

    def waves(odd):
        phases = odd[:, None] * places[None, :] % (4 * seq_len)
        angles = phases.astype(F32) * (2.0 * math.pi / (4 * seq_len))
        return (jnp.cos(angles), jnp.sin(angles))

    outer_cos, outer_sin = waves(2 * (first + inner * jnp.arange(outer)))
    inner_cos, inner_sin = waves(2 * jnp.arange(inner) + 1)
    oc, os = (outer_cos[:, None], outer_sin[:, None])
    ic, is_ = (inner_cos[None], inner_sin[None])
    both = jnp.stack([oc * ic - os * is_, -(os * ic + oc * is_)])
    return both.astype(BF16).reshape(2 * freqs, seq_len)


def dot(left, right, left_dim, right_dim):
    return lax.dot_general(
        left, right, (((left_dim,), (right_dim,)), ((), ())), preferred_element_type=F32
    )


def spectral_product(left, right, conjugate_left):
    half = left.shape[0] // 2
    left_re, left_im = (left[:half], left[half:])
    right_re, right_im = (right[:half], right[half:])
    if conjugate_left:
        real = left_re * right_re + left_im * right_im
        imag = left_re * right_im - left_im * right_re
    else:
        real = left_re * right_re - left_im * right_im
        imag = left_re * right_im + left_im * right_re
    return jnp.concatenate([real, imag], 0).astype(BF16)


def ordered(value, *first):
    return lax.optimization_barrier((value, *first))[0]


def transforms(waves, long_filter, product, grad_long):
    filter_spec = dot(waves, long_filter, 1, 1)
    product_spec = dot(waves, product, 1, 0)
    grad_spec = dot(waves, grad_long, 1, 0)
    out = dot(waves, spectral_product(filter_spec, product_spec, False), 0, 0)
    back = dot(waves, spectral_product(filter_spec, grad_spec, True), 0, 0)
    lag_grad = dot(spectral_product(product_spec, grad_spec, True), waves, 0, 0)
    return (out, back, lag_grad)


def all_sum(value, axis, bits):
    for pair in [bits[i : i + 2] for i in range(0, len(bits), 2)]:
        sums = [value]
        for bit in pair:
            sums += [swapped(value, axis, bit)]
        if len(pair) == 2:
            far = swapped(value, axis, pair[0] + pair[1])
            value = (sums[0] + sums[1]) + (sums[2] + far)
        else:
            value = sums[0] + sums[1]
    return value


def bits_of(count, first=1):
    return [1 << i for i in range(count.bit_length() - 1) if 1 << i >= first]


def own_share(gate_all, cot_all, parts):
    core = lax.axis_index("context") % 2
    width = gate_all.shape[1] // 2
    other = dot(lax.dynamic_slice_in_dim(gate_all, (1 - core) * width, width, 1), cot_all, 0, 0)
    other = other.astype(BF16)
    own_gate = ordered(lax.dynamic_slice_in_dim(gate_all, core * width, width, 1), other)
    own = dot(own_gate, cot_all, 0, 0)
    pair = (own + swapped(other, "context", 1).astype(F32)).astype(BF16)
    pair = pair.reshape(parts // 2, -1, pair.shape[-1])
    row = lax.axis_index("context") // 2
    shares = [lax.dynamic_index_in_dim(pair, row, 0, False)]
    for k in range(1, parts // 2):
        sent = lax.dynamic_index_in_dim(pair, row ^ k, 0, False)
        shares.append(swapped(sent, "context", 2 * k))
    return (pair, shares)


def summed_blocks(value, axis, dim):
    count = lax.axis_size(axis)
    size = value.shape[dim] // count
    me = lax.axis_index(axis)
    total = lax.dynamic_slice_in_dim(value, me * size, size, dim)
    for k in range(1, count):
        sent = lax.dynamic_slice_in_dim(value, (me ^ k) * size, size, dim).astype(BF16)
        total = total + swapped(sent, axis, k).astype(F32)
    return total


def to_channels(blocks):
    came = lax.all_to_all(blocks, "context", split_axis=0, concat_axis=0, tiled=True)
    return came.reshape(-1, came.shape[-1])


def to_positions(blocks):
    return lax.all_to_all(blocks, "context", split_axis=0, concat_axis=0, tiled=True)


def body(projected, short_taps, long_filter, skip_gain, out_proj, cotangent):
    rows, width = projected.shape
    chans = width // 3
    parts_dp, parts = (lax.axis_size("dp"), lax.axis_size("context"))
    blk = chans // parts
    seq_len = rows * parts
    scale_factor = 1.0 / math.sqrt(seq_len * parts_dp)
    me = lax.axis_index("context").astype(jnp.int32)
    me_dp = lax.axis_index("dp").astype(jnp.int32)[None]
    plane = jax.ShapeDtypeStruct((parts, rows, blk), BF16)

    prev_rows = passed_along(projected[rows - 2 :], "context", 1).astype(F32)
    cots = [cotangent] + [swapped(cotangent, "dp", k) for k in range(1, parts_dp)]
    query, keyed, valued, product_out = call(
        short_kernel, "short_convs", [plane] * 4, 0, 60, projected, prev_rows, short_taps
    )
    product = to_channels(product_out)

    filter_b = long_filter.astype(BF16)
    inverse = 1.0 / seq_len
    straight = seq_len <= 1024
    weights = out_proj
    if straight:
        waves = table(0, seq_len, seq_len)
        filter_spec = dot(waves, filter_b, 1, 1)
        weights = ordered(out_proj, filter_spec)
    found = [dot(cot, weights, 1, 1).astype(BF16) for cot in cots]
    found = [found[0]] + [swapped(found[k], "dp", k) for k in range(1, parts_dp)]
    gate_grad, grad_long_out = call(
        grad_long_kernel, "grad_long", [plane] * 2, 1, 12, me_dp, query, *found
    )
    grad_long = to_channels(grad_long_out)
    product_f, grad_long_f = (product.astype(F32), grad_long.astype(F32))

    def finished(total, direct):
        return (total * inverse + skip_gain[None, :] * direct).astype(BF16)

    if straight:
        product_spec = dot(waves, ordered(product, grad_long_out), 1, 0)
        out_sum = dot(waves, spectral_product(filter_spec, product_spec, False), 0, 0)
        long_chan = finished(out_sum, product_f)
        grad_spec = dot(waves, ordered(grad_long, long_chan), 1, 0)
        back_sum = dot(waves, spectral_product(filter_spec, grad_spec, True), 0, 0)
        back_chan = finished(back_sum, grad_long_f)
    else:
        freqs = 256

        def step(carry, first):
            new = transforms(table(first, freqs, seq_len), filter_b, product, grad_long)
            return (tuple(a + b for a, b in zip(carry, new)), None)

        zero = jnp.zeros((seq_len, blk), F32)
        start = (zero, zero, jnp.zeros((blk, seq_len), F32))
        terms, _ = lax.scan(step, start, jnp.arange(0, seq_len, freqs))
        out_sum, back_sum, lag_sum = terms
        long_chan = finished(out_sum, product_f)
        back_chan = finished(back_sum, grad_long_f)
    by_core = long_chan.reshape(parts // 2, 2, rows, blk)
    core, row = (me % 2, me // 2)
    mine = lax.dynamic_index_in_dim(by_core, core, 1, False)
    near = swapped(lax.dynamic_index_in_dim(by_core, 1 - core, 1, False), "context", 1)
    long_came = []
    for k in range(parts // 2):
        halves = [lax.dynamic_index_in_dim(part, row ^ k, 0, True) for part in (mine, near)]
        both = jnp.concatenate(halves, 0)
        long_came.append(swapped(both, "context", 2 * k) if k else both)
    back_blocks = back_chan.reshape(parts, rows, blk)
    next_heads = jnp.concatenate([back_blocks[1:, :2], jnp.zeros((1, 2, blk), BF16)], 0)
    back_sent = jnp.concatenate([back_blocks, next_heads], 1)
    grad_product = to_positions(back_sent)
    heads = ordered(jnp.stack([keyed[:, :2], valued[:, :2]]), grad_long_out)
    pair_after = passed_along(heads, "context", -1).astype(F32)
    long_came = lax.optimization_barrier((*long_came, back_sent, pair_after))[: parts // 2]

    skip_sum = jnp.sum(grad_long_f * product_f, 0, keepdims=True)

    piece = jax.ShapeDtypeStruct((rows, chans // parts_dp), BF16)
    long_out, *gates = call(
        gate_kernel, "gate", [plane] + [piece] * parts_dp, 2, 12, me[None], me_dp, query, *long_came
    )
    gates = [gates[0]] + [swapped(gates[k], "dp", k) for k in range(1, parts_dp)]
    query_heads = gate_grad[:, :2].astype(F32) * long_out[:, :2].astype(F32)
    query_after = passed_along(query_heads, "context", -1)
    if straight:
        late_spec = ordered(grad_spec, long_out)
        lag_sum = dot(spectral_product(product_spec, late_spec, True), waves, 0, 0)
    early = (grad_product, skip_sum, query_after, lag_sum)
    gate_all = ordered(jnp.concatenate(gates, 0), *early)
    cot_all = jnp.concatenate(cots, 0)
    pair, shares = own_share(gate_all, cot_all, parts)
    grad_product = ordered(grad_product, pair)

    grad_inputs, tap_sums = call(
        final_kernel,
        "stream_grads",
        [
            jax.ShapeDtypeStruct((rows, width), BF16),
            jax.ShapeDtypeStruct((4, width), F32),
        ],
        0,
        60,
        projected,
        prev_rows,
        short_taps,
        gate_grad,
        long_out,
        grad_product,
        keyed,
        valued,
        query_after,
        pair_after,
        skip_sum,
    )

    tap_sums = all_sum(tap_sums, "dp", bits_of(parts_dp))
    lag_sum = ordered(lag_sum, tap_sums)
    grad_filter = summed_blocks(lag_sum, "dp", 1) * (scale_factor * inverse)
    grad_skip = tap_sums[3, :blk] * scale_factor
    tap_sums = tap_sums[:3] + swapped(tap_sums[:3], "context", 1)
    tap_sums = ordered(tap_sums, *shares[1:])
    grad_taps = all_sum(tap_sums, "context", bits_of(parts, 2)) * scale_factor
    grad_proj = sum(share.astype(F32) for share in shares) * scale_factor
    return (grad_inputs, grad_taps, grad_filter, grad_skip, grad_proj)


def solution(mesh):
    placed = (
        P(("dp", "context"), None),
        P(),
        P("context", None),
        P("context"),
        P("dp", None),
        P(("dp", "context"), None),
    )
    return jax.shard_map(
        body,
        mesh=mesh,
        in_specs=placed,
        out_specs=(
            P(("dp", "context"), None),
            P(),
            P("context", "dp"),
            P("context"),
            P(("dp", "context"), None),
        ),
        check_vma=False,
    )
```

```python
import math

import jax
import jax.numpy as jnp
import numpy as np
from jax import lax
from jax.experimental import pallas as pl
from jax.experimental.pallas import tpu as pltpu
from jax.sharding import PartitionSpec as P

BF16 = jnp.bfloat16
F32 = jnp.float32


def passed_along(value, axis, steps):
    count = lax.axis_size(axis)
    initial, last = (max(0, -steps), min(count, count - steps))
    return lax.ppermute(value, axis, [(source, source + steps) for source in range(initial, last)])


def swapped(value, axis, mask):
    return lax.ppermute(value, axis, [(i, i ^ mask) for i in range(lax.axis_size(axis))])


SMEM = pl.BlockSpec(memory_space=pltpu.SMEM)


def rows_down(values, steps, before):
    row = lax.broadcasted_iota(jnp.int32, values.shape, 0)
    moved = pltpu.roll(values, steps, axis=0)
    if steps == 1:
        return jnp.where(row == 0, before[1:2], moved)
    return jnp.where(row == 0, before[0:1], jnp.where(row == 1, before[1:2], moved))


def rows_up(values, steps, after):
    count = values.shape[0]
    row = lax.broadcasted_iota(jnp.int32, values.shape, 0)
    moved = pltpu.roll(values, count - steps, axis=0)
    if steps == 1:
        return jnp.where(row == count - 1, after[0:1], moved)
    return jnp.where(row == count - 1, after[1:2], jnp.where(row == count - 2, after[0:1], moved))


def call(kernel, name, outs, smem, limit, *args):
    arrays = args[smem:]
    count, given = (len(arrays), len(outs))

    def run(*refs):
        ends = refs[smem : smem + count + given]
        *buffers, sems = refs[smem + count + given :]
        copies = []
        for i, (end, buffer) in enumerate(zip(ends, buffers)):
            pair = (end, buffer) if i < count else (buffer, end)
            copies.append(pltpu.make_async_copy(*pair, sems.at[i]))
        for copy in copies[:count]:
            copy.start()
        for copy in copies[:count]:
            copy.wait()
        kernel(*refs[:smem], *buffers)
        for copy in copies[count:]:
            copy.start()
        for copy in copies[count:]:
            copy.wait()

    anywhere = pl.BlockSpec(memory_space=pl.ANY)
    return pl.pallas_call(
        run,
        out_shape=outs,
        in_specs=[SMEM] * smem + [anywhere] * count,
        out_specs=[anywhere] * given,
        scratch_shapes=[pltpu.VMEM(a.shape, a.dtype) for a in (*arrays, *outs)]
        + [pltpu.SemaphoreType.DMA((count + given,))],
        compiler_params=pltpu.CompilerParams(vmem_limit_bytes=limit * 2**20),
        cost_estimate=pl.CostEstimate(flops=0, transcendentals=0, bytes_accessed=0),
        name=name,
    )(*args)


def columns(index, size):
    return slice(index * size, (index + 1) * size)


def short_kernel(proj_ref, prev_ref, taps_ref, query_ref, keyed_ref, valued_ref, product_ref):
    parts, _, blk = query_ref.shape
    for b in range(parts):

        def mixed(stream):
            cols = columns(stream * parts + b, blk)
            values = proj_ref[:, cols].astype(F32)
            before = prev_ref[:, cols]
            taps = taps_ref[:, cols]
            total = taps[0:1] * values + taps[1:2] * rows_down(values, 1, before)
            return (total + taps[2:3] * rows_down(values, 2, before)).astype(BF16)

        query_ref[b] = mixed(0)
        keyed, valued = (mixed(1), mixed(2))
        keyed_ref[b] = keyed
        valued_ref[b] = valued
        product_ref[b] = (keyed.astype(F32) * valued.astype(F32)).astype(BF16)


def grad_long_kernel(me_ref, query_ref, *refs):
    pieces, (gate_grad_ref, grad_long_ref) = refs[:-2], refs[-2:]
    parts, _, blk = query_ref.shape
    ratio = parts // len(pieces)
    for k, piece in enumerate(pieces):
        for i in range(ratio):
            b = (me_ref[0] ^ k) * ratio + i
            values = piece[:, columns(i, blk)]
            gate_grad_ref[b] = values
            grad_long_ref[b] = (values.astype(F32) * query_ref[b].astype(F32)).astype(BF16)


def gate_kernel(me_ref, me_dp_ref, query_ref, *refs):
    parts, _, blk = query_ref.shape
    came, long_ref, pieces = refs[: parts // 2], refs[parts // 2], refs[parts // 2 + 1 :]
    ratio = parts // len(pieces)
    size = blk * ratio // parts
    for k, piece in enumerate(came):
        b = me_ref[0] ^ (2 * k)
        long_ref[b] = piece[0]
        long_ref[b ^ 1] = piece[1]
    for k, piece in enumerate(pieces):
        for i in range(ratio):
            b = (me_dp_ref[0] ^ k) * ratio + i
            gate = (query_ref[b].astype(F32) * long_ref[b].astype(F32)).astype(BF16)
            for q in range(blk // size):
                c = i * (blk // size) + q
                piece[:, columns(c % 2 * (parts // 2) + c // 2, size)] = gate[:, columns(q, size)]


def final_kernel(*refs):
    proj_ref, prev_ref, taps_ref, gate_grad_ref, long_ref, back_ref, keyed_ref, valued_ref = refs[:8]
    query_after_ref, pair_after_ref, skip_ref, out_ref, sums_ref = refs[8:]
    parts, rows, blk = long_ref.shape
    sums_ref[3:4, :] = jnp.zeros((1, sums_ref.shape[1]), F32)
    sums_ref[3:4, 0:blk] = skip_ref[...]
    for b in range(parts):
        back = back_ref[b, 0:rows].astype(F32)
        back_after = back_ref[b, rows : rows + 2].astype(F32)
        grads = (
            (
                gate_grad_ref[b].astype(F32) * long_ref[b].astype(F32),
                query_after_ref[b],
            ),
            (back * valued_ref[b].astype(F32), back_after * pair_after_ref[1, b]),
            (back * keyed_ref[b].astype(F32), back_after * pair_after_ref[0, b]),
        )
        for stream, (grad, after) in enumerate(grads):
            cols = columns(stream * parts + b, blk)
            taps = taps_ref[:, cols]
            total = taps[0:1] * grad + taps[1:2] * rows_up(grad, 1, after)
            out_ref[:, cols] = (total + taps[2:3] * rows_up(grad, 2, after)).astype(BF16)
            values = proj_ref[:, cols].astype(F32)
            before = prev_ref[:, cols]
            for j in range(3):
                moved = rows_down(values, j, before) if j else values
                sums_ref[j : j + 1, cols] = jnp.sum(grad * moved, 0, keepdims=True)


def table(first, freqs, seq_len):
    places = jnp.arange(seq_len)
    inner = min(32, freqs)
    outer = freqs // inner

    def waves(odd):
        phases = odd[:, None] * places[None, :] % (4 * seq_len)
        angles = phases.astype(F32) * (2.0 * math.pi / (4 * seq_len))
        return (jnp.cos(angles), jnp.sin(angles))

    outer_cos, outer_sin = waves(2 * (first + inner * jnp.arange(outer)))
    inner_cos, inner_sin = waves(2 * jnp.arange(inner) + 1)
    oc, os = (outer_cos[:, None], outer_sin[:, None])
    ic, is_ = (inner_cos[None], inner_sin[None])
    both = jnp.stack([oc * ic - os * is_, -(os * ic + oc * is_)])
    return both.astype(BF16).reshape(2 * freqs, seq_len)


def constant_table(seq_len):
    odd = 2 * np.arange(seq_len)[:, None] + 1
    angles = odd * np.arange(seq_len)[None, :] % (4 * seq_len) * (math.pi / (2 * seq_len))
    return np.stack([np.cos(angles), -np.sin(angles)]).astype(np.float32).astype(BF16)


def dot(left, right, left_dim, right_dim):
    return lax.dot_general(
        left, right, (((left_dim,), (right_dim,)), ((), ())), preferred_element_type=F32
    )


def spectral_product(left, right, conjugate_left):
    half = left.shape[0] // 2
    left_re, left_im = (left[:half], left[half:])
    right_re, right_im = (right[:half], right[half:])
    if conjugate_left:
        real = left_re * right_re + left_im * right_im
        imag = left_re * right_im - left_im * right_re
    else:
        real = left_re * right_re - left_im * right_im
        imag = left_re * right_im + left_im * right_re
    return jnp.concatenate([real, imag], 0).astype(BF16)


def filter_kernel(waves_ref, filter_ref, spec_ref):
    for i in range(2):
        spec_ref[i] = dot(filter_ref[...], waves_ref[i], 1, 1)


def out_kernel(waves_ref, filter_spec_ref, product_ref, skip_ref, spec_ref, long_ref, turned, total):
    step = pl.program_id(0)

    @pl.when(step == 0)
    def _():
        turned[...] = product_ref[...].astype(F32).T.astype(BF16)
        total[...] = jnp.zeros_like(total)

    spec_re, spec_im = (dot(turned[...], waves_ref[i], 1, 1) for i in range(2))
    spec_ref[0], spec_ref[1] = (spec_re, spec_im)
    filter_re, filter_im = (filter_spec_ref[0], filter_spec_ref[1])
    real = (filter_re * spec_re - filter_im * spec_im).astype(BF16)
    imag = (filter_re * spec_im + filter_im * spec_re).astype(BF16)
    total[...] += dot(real, waves_ref[0], 1, 0) + dot(imag, waves_ref[1], 1, 0)

    @pl.when(step == pl.num_programs(0) - 1)
    def _():
        inverse = 1.0 / total.shape[1]
        direct = skip_ref[...] * product_ref[...].astype(F32)
        long_ref[...] = (total[...].T * inverse + direct).astype(BF16)


def back_kernel(
    waves_ref, filter_spec_ref, spec_ref, grad_ref, product_ref, skip_ref,
    back_ref, lag_ref, sum_ref, turned, total,
):
    step = pl.program_id(0)

    @pl.when(step == 0)
    def _():
        turned[...] = grad_ref[...].astype(F32).T.astype(BF16)
        total[...] = jnp.zeros_like(total)
        lag_ref[...] = jnp.zeros_like(lag_ref)

    grad_re, grad_im = (dot(turned[...], waves_ref[i], 1, 1) for i in range(2))
    for ref, sums in ((filter_spec_ref, total), (spec_ref, lag_ref)):
        left_re, left_im = (ref[0], ref[1])
        real = (left_re * grad_re + left_im * grad_im).astype(BF16)
        imag = (left_re * grad_im - left_im * grad_re).astype(BF16)
        sums[...] += dot(real, waves_ref[0], 1, 0) + dot(imag, waves_ref[1], 1, 0)

    @pl.when(step == pl.num_programs(0) - 1)
    def _():
        inverse = 1.0 / total.shape[1]
        parts, rows = (back_ref.shape[0], back_ref.shape[1] - 2)
        grad = grad_ref[...].astype(F32)
        back = (total[...].T * inverse + skip_ref[...] * grad).astype(BF16)
        for b in range(parts):
            back_ref[b, 0:rows] = back[b * rows : (b + 1) * rows]
            if b < parts - 1:
                back_ref[b, rows : rows + 2] = back[(b + 1) * rows : (b + 1) * rows + 2]
            else:
                back_ref[b, rows : rows + 2] = jnp.zeros((2, back.shape[1]), BF16)
        sum_ref[...] = jnp.sum(grad * product_ref[...].astype(F32), 0, keepdims=True)


def chunked(kernel, name, waves, specs, planes, outs, spec_out, scratch):
    freqs, seq_len = waves.shape[1:]
    size = min(256, freqs)
    blk = (specs + spec_out)[0].shape[1]
    chunk = pl.BlockSpec((2, blk, size), lambda i: (0, 0, i))

    def whole(array):
        return pl.BlockSpec(array.shape, lambda i: (0,) * len(array.shape))

    return pl.pallas_call(
        kernel,
        out_shape=spec_out + outs,
        grid=(freqs // size,),
        in_specs=[pl.BlockSpec((2, size, seq_len), lambda i: (0, i, 0))]
        + [chunk] * len(specs)
        + [whole(a) for a in planes],
        out_specs=[chunk] * len(spec_out) + [whole(a) for a in outs],
        scratch_shapes=scratch,
        compiler_params=pltpu.CompilerParams(vmem_limit_bytes=60 * 2**20),
        cost_estimate=pl.CostEstimate(flops=0, transcendentals=0, bytes_accessed=0),
        name=name,
    )(waves, *specs, *planes)


def ordered(value, *first):
    return lax.optimization_barrier((value, *first))[0]


def transforms(waves, long_filter, product, grad_long):
    filter_spec = dot(waves, long_filter, 1, 1)
    product_spec = dot(waves, product, 1, 0)
    grad_spec = dot(waves, grad_long, 1, 0)
    out = dot(waves, spectral_product(filter_spec, product_spec, False), 0, 0)
    back = dot(waves, spectral_product(filter_spec, grad_spec, True), 0, 0)
    lag_grad = dot(spectral_product(product_spec, grad_spec, True), waves, 0, 0)
    return (out, back, lag_grad)


def all_sum(value, axis, bits):
    for pair in [bits[i : i + 2] for i in range(0, len(bits), 2)]:
        sums = [value]
        for bit in pair:
            sums += [swapped(value, axis, bit)]
        if len(pair) == 2:
            far = swapped(value, axis, pair[0] + pair[1])
            value = (sums[0] + sums[1]) + (sums[2] + far)
        else:
            value = sums[0] + sums[1]
    return value


def bits_of(count, first=1):
    return [1 << i for i in range(count.bit_length() - 1) if 1 << i >= first]


def own_share(gate_all, cot_all, parts):
    core = lax.axis_index("context") % 2
    width = gate_all.shape[1] // 2
    other = dot(lax.dynamic_slice_in_dim(gate_all, (1 - core) * width, width, 1), cot_all, 0, 0)
    other = other.astype(BF16)
    own_gate = ordered(lax.dynamic_slice_in_dim(gate_all, core * width, width, 1), other)
    own = dot(own_gate, cot_all, 0, 0)
    pair = (own + swapped(other, "context", 1).astype(F32)).astype(BF16)
    pair = pair.reshape(parts // 2, -1, pair.shape[-1])
    row = lax.axis_index("context") // 2
    shares = [lax.dynamic_index_in_dim(pair, row, 0, False)]
    for k in range(1, parts // 2):
        sent = lax.dynamic_index_in_dim(pair, row ^ k, 0, False)
        shares.append(swapped(sent, "context", 2 * k))
    return (pair, shares)


def summed_blocks(value, axis, dim):
    count = lax.axis_size(axis)
    size = value.shape[dim] // count
    me = lax.axis_index(axis)
    total = lax.dynamic_slice_in_dim(value, me * size, size, dim)
    for k in range(1, count):
        sent = lax.dynamic_slice_in_dim(value, (me ^ k) * size, size, dim).astype(BF16)
        total = total + swapped(sent, axis, k).astype(F32)
    return total


def to_channels(blocks):
    came = lax.all_to_all(blocks, "context", split_axis=0, concat_axis=0, tiled=True)
    return came.reshape(-1, came.shape[-1])


def to_positions(blocks):
    return lax.all_to_all(blocks, "context", split_axis=0, concat_axis=0, tiled=True)


def body(projected, short_taps, long_filter, skip_gain, out_proj, cotangent):
    rows, width = projected.shape
    chans = width // 3
    parts_dp, parts = (lax.axis_size("dp"), lax.axis_size("context"))
    blk = chans // parts
    seq_len = rows * parts
    scale_factor = 1.0 / math.sqrt(seq_len * parts_dp)
    me = lax.axis_index("context").astype(jnp.int32)
    me_dp = lax.axis_index("dp").astype(jnp.int32)[None]
    plane = jax.ShapeDtypeStruct((parts, rows, blk), BF16)

    prev_rows = passed_along(projected[rows - 2 :], "context", 1).astype(F32)
    cots = [cotangent] + [swapped(cotangent, "dp", k) for k in range(1, parts_dp)]
    query, keyed, valued, product_out = call(
        short_kernel, "short_convs", [plane] * 4, 0, 60, projected, prev_rows, short_taps
    )
    product = to_channels(product_out)

    filter_b = long_filter.astype(BF16)
    inverse = 1.0 / seq_len
    straight = seq_len <= 1024
    weights = out_proj
    if straight:
        waves = jnp.asarray(constant_table(seq_len))
        spec = jax.ShapeDtypeStruct((2, blk, seq_len), F32)
        scratch = [pltpu.VMEM((blk, seq_len), BF16), pltpu.VMEM((blk, seq_len), F32)]
        skip_row = skip_gain[None, :]
        (filter_spec,) = chunked(
            filter_kernel, "filter_spectrum", waves, [], [filter_b], [], [spec], []
        )
        weights = ordered(out_proj, filter_spec)
    found = [dot(cot, weights, 1, 1).astype(BF16) for cot in cots]
    found = [found[0]] + [swapped(found[k], "dp", k) for k in range(1, parts_dp)]
    gate_grad, grad_long_out = call(
        grad_long_kernel, "grad_long", [plane] * 2, 1, 12, me_dp, query, *found
    )
    grad_long = to_channels(grad_long_out)
    product_f, grad_long_f = (product.astype(F32), grad_long.astype(F32))

    def finished(total, direct):
        return (total * inverse + skip_gain[None, :] * direct).astype(BF16)

    def crossed(values):
        by_core = values.reshape(parts // 2, 2, rows, blk)
        core, row = (me % 2, me // 2)
        mine = lax.dynamic_index_in_dim(by_core, core, 1, False)
        near = swapped(lax.dynamic_index_in_dim(by_core, 1 - core, 1, False), "context", 1)
        stacked = jnp.stack([mine, near], 1)
        came = [lax.dynamic_index_in_dim(stacked, row, 0, False)]
        for k in range(1, parts // 2):
            sent = lax.dynamic_index_in_dim(stacked, row ^ k, 0, False)
            came.append(swapped(sent, "context", 2 * k))
        return came

    if straight:
        late_product = ordered(product, grad_long_out)
        product_spec, long_chan = chunked(
            out_kernel,
            "long_out",
            waves,
            [filter_spec],
            [late_product, skip_row],
            [jax.ShapeDtypeStruct((seq_len, blk), BF16)],
            [spec],
            scratch,
        )
        long_came = crossed(long_chan)
        back_sent, lag_sum, skip_sum = chunked(
            back_kernel,
            "grad_product",
            waves,
            [filter_spec, product_spec],
            [ordered(grad_long, *long_came[1:]), product, skip_row],
            [
                jax.ShapeDtypeStruct((parts, rows + 2, blk), BF16),
                jax.ShapeDtypeStruct((blk, seq_len), F32),
                jax.ShapeDtypeStruct((1, blk), F32),
            ],
            [],
            scratch,
        )
    else:
        freqs = 256

        def step(carry, first):
            new = transforms(table(first, freqs, seq_len), filter_b, product, grad_long)
            return (tuple(a + b for a, b in zip(carry, new)), None)

        zero = jnp.zeros((seq_len, blk), F32)
        start = (zero, zero, jnp.zeros((blk, seq_len), F32))
        terms, _ = lax.scan(step, start, jnp.arange(0, seq_len, freqs))
        out_sum, back_sum, lag_sum = terms
        long_came = crossed(finished(out_sum, product_f))
        back_blocks = finished(back_sum, grad_long_f).reshape(parts, rows, blk)
        next_heads = jnp.concatenate([back_blocks[1:, :2], jnp.zeros((1, 2, blk), BF16)], 0)
        back_sent = jnp.concatenate([back_blocks, next_heads], 1)
        skip_sum = jnp.sum(grad_long_f * product_f, 0, keepdims=True)
    grad_product = to_positions(back_sent)
    heads = ordered(jnp.stack([keyed[:, :2], valued[:, :2]]), grad_long_out)
    pair_after = passed_along(heads, "context", -1).astype(F32)
    long_came = lax.optimization_barrier((*long_came, back_sent, pair_after))[: parts // 2]

    piece = jax.ShapeDtypeStruct((rows, chans // parts_dp), BF16)
    long_out, *gates = call(
        gate_kernel, "gate", [plane] + [piece] * parts_dp, 2, 12, me[None], me_dp, query, *long_came
    )
    gates = [gates[0]] + [swapped(gates[k], "dp", k) for k in range(1, parts_dp)]
    query_heads = gate_grad[:, :2].astype(F32) * long_out[:, :2].astype(F32)
    query_after = passed_along(query_heads, "context", -1)
    early = (grad_product, query_after)
    gate_all = ordered(jnp.concatenate(gates, 0), *early)
    cot_all = jnp.concatenate(cots, 0)
    pair, shares = own_share(gate_all, cot_all, parts)
    grad_product = ordered(grad_product, pair)

    grad_inputs, tap_sums = call(
        final_kernel,
        "stream_grads",
        [
            jax.ShapeDtypeStruct((rows, width), BF16),
            jax.ShapeDtypeStruct((4, width), F32),
        ],
        0,
        60,
        projected,
        prev_rows,
        short_taps,
        gate_grad,
        long_out,
        grad_product,
        keyed,
        valued,
        query_after,
        pair_after,
        skip_sum,
    )

    tap_sums = all_sum(tap_sums, "dp", bits_of(parts_dp))
    lag_sum = ordered(lag_sum, tap_sums)
    grad_filter = summed_blocks(lag_sum, "dp", 1) * (scale_factor * inverse)
    grad_skip = tap_sums[3, :blk] * scale_factor
    tap_sums = tap_sums[:3] + swapped(tap_sums[:3], "context", 1)
    tap_sums = ordered(tap_sums, *shares[1:])
    grad_taps = all_sum(tap_sums, "context", bits_of(parts, 2)) * scale_factor
    grad_proj = sum(share.astype(F32) for share in shares) * scale_factor
    return (grad_inputs, grad_taps, grad_filter, grad_skip, grad_proj)


def solution(mesh):
    placed = (
        P(("dp", "context"), None),
        P(),
        P("context", None),
        P("context"),
        P("dp", None),
        P(("dp", "context"), None),
    )
    return jax.shard_map(
        body,
        mesh=mesh,
        in_specs=placed,
        out_specs=(
            P(("dp", "context"), None),
            P(),
            P("context", "dp"),
            P("context"),
            P(("dp", "context"), None),
        ),
        check_vma=False,
    )
```

```python
import math

import jax
import jax.numpy as jnp
import numpy as np
from jax import lax
from jax.experimental import pallas as pl
from jax.experimental.pallas import tpu as pltpu
from jax.sharding import PartitionSpec as P

BF16 = jnp.bfloat16
F32 = jnp.float32


def passed_along(value, axis, steps):
    count = lax.axis_size(axis)
    initial, last = (max(0, -steps), min(count, count - steps))
    return lax.ppermute(value, axis, [(source, source + steps) for source in range(initial, last)])


def swapped(value, axis, mask):
    return lax.ppermute(value, axis, [(i, i ^ mask) for i in range(lax.axis_size(axis))])


SMEM = pl.BlockSpec(memory_space=pltpu.SMEM)


def rows_down(values, steps, before):
    row = lax.broadcasted_iota(jnp.int32, values.shape, 0)
    moved = pltpu.roll(values, steps, axis=0)
    if steps == 1:
        return jnp.where(row == 0, before[1:2], moved)
    return jnp.where(row == 0, before[0:1], jnp.where(row == 1, before[1:2], moved))


def rows_up(values, steps, after):
    count = values.shape[0]
    row = lax.broadcasted_iota(jnp.int32, values.shape, 0)
    moved = pltpu.roll(values, count - steps, axis=0)
    if steps == 1:
        return jnp.where(row == count - 1, after[0:1], moved)
    return jnp.where(row == count - 1, after[1:2], jnp.where(row == count - 2, after[0:1], moved))


def call(kernel, name, outs, smem, limit, *args):
    arrays = args[smem:]
    count, given = (len(arrays), len(outs))

    def run(*refs):
        ends = refs[smem : smem + count + given]
        *buffers, sems = refs[smem + count + given :]
        copies = []
        for i, (end, buffer) in enumerate(zip(ends, buffers)):
            pair = (end, buffer) if i < count else (buffer, end)
            copies.append(pltpu.make_async_copy(*pair, sems.at[i]))
        for copy in copies[:count]:
            copy.start()
        for copy in copies[:count]:
            copy.wait()
        kernel(*refs[:smem], *buffers)
        for copy in copies[count:]:
            copy.start()
        for copy in copies[count:]:
            copy.wait()

    anywhere = pl.BlockSpec(memory_space=pl.ANY)
    return pl.pallas_call(
        run,
        out_shape=outs,
        in_specs=[SMEM] * smem + [anywhere] * count,
        out_specs=[anywhere] * given,
        scratch_shapes=[pltpu.VMEM(a.shape, a.dtype) for a in (*arrays, *outs)]
        + [pltpu.SemaphoreType.DMA((count + given,))],
        compiler_params=pltpu.CompilerParams(vmem_limit_bytes=limit * 2**20),
        cost_estimate=pl.CostEstimate(flops=0, transcendentals=0, bytes_accessed=0),
        name=name,
    )(*args)


def columns(index, size):
    return slice(index * size, (index + 1) * size)


def short_kernel(proj_ref, prev_ref, taps_ref, query_ref, keyed_ref, valued_ref, product_ref):
    parts, _, blk = query_ref.shape
    for b in range(parts):

        def mixed(stream):
            cols = columns(stream * parts + b, blk)
            values = proj_ref[:, cols].astype(F32)
            before = prev_ref[:, cols]
            taps = taps_ref[:, cols]
            total = taps[0:1] * values + taps[1:2] * rows_down(values, 1, before)
            return (total + taps[2:3] * rows_down(values, 2, before)).astype(BF16)

        query_ref[b] = mixed(0)
        keyed, valued = (mixed(1), mixed(2))
        keyed_ref[b] = keyed
        valued_ref[b] = valued
        product_ref[b] = (keyed.astype(F32) * valued.astype(F32)).astype(BF16)


def grad_long_kernel(me_ref, query_ref, *refs):
    pieces, (gate_grad_ref, grad_long_ref) = refs[:-2], refs[-2:]
    parts, _, blk = query_ref.shape
    ratio = parts // len(pieces)
    for k, piece in enumerate(pieces):
        for i in range(ratio):
            b = (me_ref[0] ^ k) * ratio + i
            values = piece[:, columns(i, blk)]
            gate_grad_ref[b] = values
            grad_long_ref[b] = (values.astype(F32) * query_ref[b].astype(F32)).astype(BF16)


def gate_kernel(me_ref, me_dp_ref, query_ref, *refs):
    parts, _, blk = query_ref.shape
    came, long_ref, pieces = refs[: parts // 2], refs[parts // 2], refs[parts // 2 + 1 :]
    ratio = parts // len(pieces)
    size = blk * ratio // parts
    for k, piece in enumerate(came):
        b = me_ref[0] ^ (2 * k)
        long_ref[b] = piece[0]
        long_ref[b ^ 1] = piece[1]
    for k, piece in enumerate(pieces):
        for i in range(ratio):
            b = (me_dp_ref[0] ^ k) * ratio + i
            gate = (query_ref[b].astype(F32) * long_ref[b].astype(F32)).astype(BF16)
            for q in range(blk // size):
                c = i * (blk // size) + q
                piece[:, columns(c % 2 * (parts // 2) + c // 2, size)] = gate[:, columns(q, size)]


def final_kernel(*refs):
    proj_ref, prev_ref, taps_ref, gate_grad_ref, long_ref, back_ref, keyed_ref, valued_ref = refs[:8]
    query_after_ref, pair_after_ref, skip_ref, out_ref, sums_ref = refs[8:]
    parts, rows, blk = long_ref.shape
    sums_ref[3:4, :] = jnp.zeros((1, sums_ref.shape[1]), F32)
    sums_ref[3:4, 0:blk] = skip_ref[...]
    for b in range(parts):
        back = back_ref[b, 0:rows].astype(F32)
        back_after = back_ref[b, rows : rows + 2].astype(F32)
        grads = (
            (
                gate_grad_ref[b].astype(F32) * long_ref[b].astype(F32),
                query_after_ref[b],
            ),
            (back * valued_ref[b].astype(F32), back_after * pair_after_ref[1, b]),
            (back * keyed_ref[b].astype(F32), back_after * pair_after_ref[0, b]),
        )
        for stream, (grad, after) in enumerate(grads):
            cols = columns(stream * parts + b, blk)
            taps = taps_ref[:, cols]
            total = taps[0:1] * grad + taps[1:2] * rows_up(grad, 1, after)
            out_ref[:, cols] = (total + taps[2:3] * rows_up(grad, 2, after)).astype(BF16)
            values = proj_ref[:, cols].astype(F32)
            before = prev_ref[:, cols]
            for j in range(3):
                moved = rows_down(values, j, before) if j else values
                sums_ref[j : j + 1, cols] = jnp.sum(grad * moved, 0, keepdims=True)


def table(first, freqs, seq_len):
    places = jnp.arange(seq_len)
    inner = min(32, freqs)
    outer = freqs // inner

    def waves(odd):
        phases = odd[:, None] * places[None, :] % (4 * seq_len)
        angles = phases.astype(F32) * (2.0 * math.pi / (4 * seq_len))
        return (jnp.cos(angles), jnp.sin(angles))

    outer_cos, outer_sin = waves(2 * (first + inner * jnp.arange(outer)))
    inner_cos, inner_sin = waves(2 * jnp.arange(inner) + 1)
    oc, os = (outer_cos[:, None], outer_sin[:, None])
    ic, is_ = (inner_cos[None], inner_sin[None])
    both = jnp.stack([oc * ic - os * is_, -(os * ic + oc * is_)])
    return both.astype(BF16).reshape(2 * freqs, seq_len)


def constant_table(seq_len):
    odd = 2 * np.arange(seq_len)[:, None] + 1
    angles = odd * np.arange(seq_len)[None, :] % (4 * seq_len) * (math.pi / (2 * seq_len))
    both = np.stack([np.cos(angles), -np.sin(angles)])
    size = min(128, seq_len)
    both = both.reshape(2, seq_len // size, size, seq_len).transpose(1, 0, 2, 3)
    return both.reshape(-1, 2 * size, seq_len).astype(np.float32).astype(BF16)


def dot(left, right, left_dim, right_dim):
    return lax.dot_general(
        left, right, (((left_dim,), (right_dim,)), ((), ())), preferred_element_type=F32
    )


def spectral_product(left, right, conjugate_left):
    half = left.shape[0] // 2
    left_re, left_im = (left[:half], left[half:])
    right_re, right_im = (right[:half], right[half:])
    if conjugate_left:
        real = left_re * right_re + left_im * right_im
        imag = left_re * right_im - left_im * right_re
    else:
        real = left_re * right_re - left_im * right_im
        imag = left_re * right_im + left_im * right_re
    return jnp.concatenate([real, imag], 0).astype(BF16)


def halves(value):
    half = value.shape[1] // 2
    return (value[:, :half], value[:, half:])


def filter_kernel(waves_ref, filter_ref, spec_ref):
    spec_ref[...] = dot(filter_ref[...].astype(BF16), waves_ref[...], 1, 1)


def out_kernel(waves_ref, filter_spec_ref, product_ref, skip_ref, spec_ref, long_ref, turned, total):
    step = pl.program_id(0)

    @pl.when(step == 0)
    def _():
        turned[...] = product_ref[...].astype(F32).T.astype(BF16)
        total[...] = jnp.zeros_like(total)

    spec = dot(turned[...], waves_ref[...], 1, 1)
    spec_ref[...] = spec
    real, imag = halves(spec)
    filter_re, filter_im = halves(filter_spec_ref[...])
    mixed = [filter_re * real - filter_im * imag, filter_re * imag + filter_im * real]
    total[...] += dot(jnp.concatenate(mixed, 1).astype(BF16), waves_ref[...], 1, 0)

    @pl.when(step == pl.num_programs(0) - 1)
    def _():
        inverse = 1.0 / total.shape[1]
        direct = skip_ref[...] * product_ref[...].astype(F32)
        long_ref[...] = (total[...].T * inverse + direct).astype(BF16)


def back_kernel(
    waves_ref, filter_spec_ref, spec_ref, grad_ref, product_ref, skip_ref,
    back_ref, lag_ref, sum_ref, turned, total,
):
    step = pl.program_id(0)

    @pl.when(step == 0)
    def _():
        turned[...] = grad_ref[...].astype(F32).T.astype(BF16)
        total[...] = jnp.zeros_like(total)
        lag_ref[...] = jnp.zeros_like(lag_ref)

    real, imag = halves(dot(turned[...], waves_ref[...], 1, 1))
    for ref, sums in ((filter_spec_ref, total), (spec_ref, lag_ref)):
        left_re, left_im = halves(ref[...])
        mixed = [left_re * real + left_im * imag, left_re * imag - left_im * real]
        sums[...] += dot(jnp.concatenate(mixed, 1).astype(BF16), waves_ref[...], 1, 0)

    @pl.when(step == pl.num_programs(0) - 1)
    def _():
        inverse = 1.0 / total.shape[1]
        parts, rows = (back_ref.shape[0], back_ref.shape[1] - 2)
        grad = grad_ref[...].astype(F32)
        back = (total[...].T * inverse + skip_ref[...] * grad).astype(BF16)
        for b in range(parts):
            back_ref[b, 0:rows] = back[b * rows : (b + 1) * rows]
            if b < parts - 1:
                back_ref[b, rows : rows + 2] = back[(b + 1) * rows : (b + 1) * rows + 2]
            else:
                back_ref[b, rows : rows + 2] = jnp.zeros((2, back.shape[1]), BF16)
        sum_ref[...] = jnp.sum(grad * product_ref[...].astype(F32), 0, keepdims=True)


def chunked(kernel, name, waves, specs, planes, outs, spec_out, scratch):
    def chunk(array):
        return pl.BlockSpec((None, *array.shape[1:]), lambda i: (i, 0, 0))

    def whole(array):
        return pl.BlockSpec(array.shape, lambda i: (0,) * len(array.shape))

    return pl.pallas_call(
        kernel,
        out_shape=spec_out + outs,
        grid=(waves.shape[0],),
        in_specs=[chunk(a) for a in (waves, *specs)] + [whole(a) for a in planes],
        out_specs=[chunk(a) for a in spec_out] + [whole(a) for a in outs],
        scratch_shapes=scratch,
        compiler_params=pltpu.CompilerParams(vmem_limit_bytes=60 * 2**20),
        cost_estimate=pl.CostEstimate(flops=0, transcendentals=0, bytes_accessed=0),
        name=name,
    )(waves, *specs, *planes)


def share_kernel(take, core_ref, *refs):
    refs, out_ref = refs[:-1], refs[-1]
    count = len(refs) // 2
    gates, cots = refs[:count], refs[count : 2 * count]
    width = out_ref.shape[0]
    core = core_ref[0] if take else 1 - core_ref[0]
    cols = pl.ds(pl.multiple_of(core * width, 128), width)
    turned = [gate[:, cols].astype(F32).T.astype(BF16) for gate in gates]
    size = min(512, out_ref.shape[1])
    for n in range(out_ref.shape[1] // size):
        total = sum(dot(turned[k], cots[k][:, columns(n, size)], 1, 0) for k in range(count))
        if take:
            total = total + refs[-1][:, columns(n, size)].astype(F32)
        out_ref[:, columns(n, size)] = total.astype(BF16)


def ordered(value, *first):
    return lax.optimization_barrier((value, *first))[0]


def transforms(waves, long_filter, product, grad_long):
    filter_spec = dot(waves, long_filter, 1, 1)
    product_spec = dot(waves, product, 1, 0)
    grad_spec = dot(waves, grad_long, 1, 0)
    out = dot(waves, spectral_product(filter_spec, product_spec, False), 0, 0)
    back = dot(waves, spectral_product(filter_spec, grad_spec, True), 0, 0)
    lag_grad = dot(spectral_product(product_spec, grad_spec, True), waves, 0, 0)
    return (out, back, lag_grad)


def all_sum(value, axis, bits):
    for pair in [bits[i : i + 2] for i in range(0, len(bits), 2)]:
        sums = [value]
        for bit in pair:
            sums += [swapped(value, axis, bit)]
        if len(pair) == 2:
            far = swapped(value, axis, pair[0] + pair[1])
            value = (sums[0] + sums[1]) + (sums[2] + far)
        else:
            value = sums[0] + sums[1]
    return value


def bits_of(count, first=1):
    return [1 << i for i in range(count.bit_length() - 1) if 1 << i >= first]


def own_share(gates, cots, parts):
    core = (lax.axis_index("context") % 2).astype(jnp.int32)[None]
    half = jax.ShapeDtypeStruct((gates[0].shape[1] // 2, cots[0].shape[1]), BF16)

    def product(take, name, *more):
        kernel = lambda *refs: share_kernel(take, *refs)
        return call(kernel, name, [half], 1, 60, core, *gates, *cots, *more)[0]

    other = product(False, "other_share")
    pair = product(True, "own_share", swapped(other, "context", 1))
    blocks = pair.reshape(parts // 2, -1, pair.shape[-1])
    row = lax.axis_index("context") // 2
    shares = [lax.dynamic_index_in_dim(blocks, row, 0, False)]
    for k in range(1, parts // 2):
        sent = lax.dynamic_index_in_dim(blocks, row ^ k, 0, False)
        shares.append(swapped(sent, "context", 2 * k))
    return (pair, shares)


def summed_blocks(value, axis, dim):
    count = lax.axis_size(axis)
    size = value.shape[dim] // count
    me = lax.axis_index(axis)
    total = lax.dynamic_slice_in_dim(value, me * size, size, dim)
    for k in range(1, count):
        sent = lax.dynamic_slice_in_dim(value, (me ^ k) * size, size, dim).astype(BF16)
        total = total + swapped(sent, axis, k).astype(F32)
    return total


def to_channels(blocks):
    came = lax.all_to_all(blocks, "context", split_axis=0, concat_axis=0, tiled=True)
    return came.reshape(-1, came.shape[-1])


def to_positions(blocks):
    return lax.all_to_all(blocks, "context", split_axis=0, concat_axis=0, tiled=True)


def body(projected, short_taps, long_filter, skip_gain, out_proj, cotangent):
    rows, width = projected.shape
    chans = width // 3
    parts_dp, parts = (lax.axis_size("dp"), lax.axis_size("context"))
    blk = chans // parts
    seq_len = rows * parts
    scale_factor = 1.0 / math.sqrt(seq_len * parts_dp)
    me = lax.axis_index("context").astype(jnp.int32)
    me_dp = lax.axis_index("dp").astype(jnp.int32)[None]
    plane = jax.ShapeDtypeStruct((parts, rows, blk), BF16)

    prev_rows = passed_along(projected[rows - 2 :], "context", 1).astype(F32)
    cots = [cotangent] + [swapped(cotangent, "dp", k) for k in range(1, parts_dp)]
    query, keyed, valued, product_out = call(
        short_kernel, "short_convs", [plane] * 4, 0, 60, projected, prev_rows, short_taps
    )
    product = to_channels(product_out)

    filter_b = long_filter.astype(BF16)
    inverse = 1.0 / seq_len
    straight = seq_len <= 1024
    weights = out_proj
    if straight:
        waves = jnp.asarray(constant_table(seq_len))
        spec = jax.ShapeDtypeStruct((waves.shape[0], blk, waves.shape[1]), F32)
        scratch = [pltpu.VMEM((blk, seq_len), BF16), pltpu.VMEM((blk, seq_len), F32)]
        skip_row = skip_gain[None, :]
        (filter_spec,) = chunked(
            filter_kernel, "filter_spectrum", waves, [], [long_filter], [], [spec], []
        )
        weights = ordered(out_proj, filter_spec)
    found = [dot(cot, weights, 1, 1).astype(BF16) for cot in cots]
    found = [found[0]] + [swapped(found[k], "dp", k) for k in range(1, parts_dp)]
    gate_grad, grad_long_out = call(
        grad_long_kernel, "grad_long", [plane] * 2, 1, 12, me_dp, query, *found
    )
    grad_long = to_channels(grad_long_out)
    product_f, grad_long_f = (product.astype(F32), grad_long.astype(F32))

    def finished(total, direct):
        return (total * inverse + skip_gain[None, :] * direct).astype(BF16)

    def crossed(values):
        by_core = values.reshape(parts // 2, 2, rows, blk)
        core, row = (me % 2, me // 2)
        mine = lax.dynamic_index_in_dim(by_core, core, 1, False)
        near = swapped(lax.dynamic_index_in_dim(by_core, 1 - core, 1, False), "context", 1)
        stacked = jnp.stack([mine, near], 1)
        came = [lax.dynamic_index_in_dim(stacked, row, 0, False)]
        for k in range(1, parts // 2):
            sent = lax.dynamic_index_in_dim(stacked, row ^ k, 0, False)
            came.append(swapped(sent, "context", 2 * k))
        return came

    if straight:
        late_product = ordered(product, grad_long_out)
        product_spec, long_chan = chunked(
            out_kernel,
            "long_out",
            waves,
            [filter_spec],
            [late_product, skip_row],
            [jax.ShapeDtypeStruct((seq_len, blk), BF16)],
            [spec],
            scratch,
        )
        long_came = crossed(long_chan)
        back_sent, lag_sum, skip_sum = chunked(
            back_kernel,
            "grad_product",
            waves,
            [filter_spec, product_spec],
            [ordered(grad_long, long_came[1]), product, skip_row],
            [
                jax.ShapeDtypeStruct((parts, rows + 2, blk), BF16),
                jax.ShapeDtypeStruct((blk, seq_len), F32),
                jax.ShapeDtypeStruct((1, blk), F32),
            ],
            [],
            scratch,
        )
    else:
        freqs = 256

        def step(carry, first):
            new = transforms(table(first, freqs, seq_len), filter_b, product, grad_long)
            return (tuple(a + b for a, b in zip(carry, new)), None)

        zero = jnp.zeros((seq_len, blk), F32)
        start = (zero, zero, jnp.zeros((blk, seq_len), F32))
        terms, _ = lax.scan(step, start, jnp.arange(0, seq_len, freqs))
        out_sum, back_sum, lag_sum = terms
        long_came = crossed(finished(out_sum, product_f))
        back_blocks = finished(back_sum, grad_long_f).reshape(parts, rows, blk)
        next_heads = jnp.concatenate([back_blocks[1:, :2], jnp.zeros((1, 2, blk), BF16)], 0)
        back_sent = jnp.concatenate([back_blocks, next_heads], 1)
        skip_sum = jnp.sum(grad_long_f * product_f, 0, keepdims=True)
    grad_product = to_positions(back_sent)
    heads = ordered(jnp.stack([keyed[:, :2], valued[:, :2]]), grad_long_out)
    pair_after = passed_along(heads, "context", -1).astype(F32)
    long_came = lax.optimization_barrier((*long_came, back_sent, pair_after))[: parts // 2]

    piece = jax.ShapeDtypeStruct((rows, chans // parts_dp), BF16)
    long_out, *gates = call(
        gate_kernel, "gate", [plane] + [piece] * parts_dp, 2, 12, me[None], me_dp, query, *long_came
    )
    gates = [gates[0]] + [swapped(gates[k], "dp", k) for k in range(1, parts_dp)]
    query_heads = gate_grad[:, :2].astype(F32) * long_out[:, :2].astype(F32)
    query_after = passed_along(query_heads, "context", -1)
    grad_filter = summed_blocks(lag_sum, "dp", 1) * (scale_factor * inverse)
    early = (grad_product, query_after, grad_filter)
    gates[0] = ordered(gates[0], *early)
    pair, shares = own_share(gates, cots, parts)
    grad_product = ordered(grad_product, pair)

    grad_inputs, tap_sums = call(
        final_kernel,
        "stream_grads",
        [
            jax.ShapeDtypeStruct((rows, width), BF16),
            jax.ShapeDtypeStruct((4, width), F32),
        ],
        0,
        60,
        projected,
        prev_rows,
        short_taps,
        gate_grad,
        long_out,
        grad_product,
        keyed,
        valued,
        query_after,
        pair_after,
        skip_sum,
    )

    tap_sums = all_sum(tap_sums, "dp", bits_of(parts_dp))
    grad_skip = tap_sums[3, :blk] * scale_factor
    tap_sums = tap_sums[:3] + swapped(tap_sums[:3], "context", 1)
    tap_sums = ordered(tap_sums, *shares[1:])
    grad_taps = all_sum(tap_sums, "context", bits_of(parts, 2)) * scale_factor
    grad_proj = sum(share.astype(F32) for share in shares) * scale_factor
    return (grad_inputs, grad_taps, grad_filter, grad_skip, grad_proj)


def solution(mesh):
    placed = (
        P(("dp", "context"), None),
        P(),
        P("context", None),
        P("context"),
        P("dp", None),
        P(("dp", "context"), None),
    )
    return jax.shard_map(
        body,
        mesh=mesh,
        in_specs=placed,
        out_specs=(
            P(("dp", "context"), None),
            P(),
            P("context", "dp"),
            P("context"),
            P(("dp", "context"), None),
        ),
        check_vma=False,
    )
```

```python
import math

import jax
import jax.numpy as jnp
import numpy as np
from jax import lax
from jax.experimental import pallas as pl
from jax.experimental.pallas import tpu as pltpu
from jax.sharding import PartitionSpec as P

BF16 = jnp.bfloat16
F32 = jnp.float32


def passed_along(value, axis, steps):
    count = lax.axis_size(axis)
    initial, last = (max(0, -steps), min(count, count - steps))
    return lax.ppermute(value, axis, [(source, source + steps) for source in range(initial, last)])


def swapped(value, axis, mask):
    return lax.ppermute(value, axis, [(i, i ^ mask) for i in range(lax.axis_size(axis))])


SMEM = pl.BlockSpec(memory_space=pltpu.SMEM)


def rows_down(values, steps, before):
    row = lax.broadcasted_iota(jnp.int32, values.shape, 0)
    moved = pltpu.roll(values, steps, axis=0)
    if steps == 1:
        return jnp.where(row == 0, before[1:2], moved)
    return jnp.where(row == 0, before[0:1], jnp.where(row == 1, before[1:2], moved))


def rows_up(values, steps, after):
    count = values.shape[0]
    row = lax.broadcasted_iota(jnp.int32, values.shape, 0)
    moved = pltpu.roll(values, count - steps, axis=0)
    if steps == 1:
        return jnp.where(row == count - 1, after[0:1], moved)
    return jnp.where(row == count - 1, after[1:2], jnp.where(row == count - 2, after[0:1], moved))


def call(kernel, name, outs, smem, limit, *args):
    arrays = args[smem:]
    count, given = (len(arrays), len(outs))

    def run(*refs):
        ends = refs[smem : smem + count + given]
        *buffers, sems = refs[smem + count + given :]
        copies = []
        for i, (end, buffer) in enumerate(zip(ends, buffers)):
            pair = (end, buffer) if i < count else (buffer, end)
            copies.append(pltpu.make_async_copy(*pair, sems.at[i]))
        for copy in copies[:count]:
            copy.start()
        for copy in copies[:count]:
            copy.wait()
        kernel(*refs[:smem], *buffers)
        for copy in copies[count:]:
            copy.start()
        for copy in copies[count:]:
            copy.wait()

    anywhere = pl.BlockSpec(memory_space=pl.ANY)
    return pl.pallas_call(
        run,
        out_shape=outs,
        in_specs=[SMEM] * smem + [anywhere] * count,
        out_specs=[anywhere] * given,
        scratch_shapes=[pltpu.VMEM(a.shape, a.dtype) for a in (*arrays, *outs)]
        + [pltpu.SemaphoreType.DMA((count + given,))],
        compiler_params=pltpu.CompilerParams(vmem_limit_bytes=limit * 2**20),
        cost_estimate=pl.CostEstimate(flops=0, transcendentals=0, bytes_accessed=0),
        name=name,
    )(*args)


def joined(pieces):
    count, rows = (len(pieces), pieces[0].shape[0])

    def kernel(*refs):
        ins, out_ref, sems = refs[:count], refs[count], refs[count + 1]
        copies = [
            pltpu.make_async_copy(ref, out_ref.at[pl.ds(k * rows, rows)], sems.at[k])
            for k, ref in enumerate(ins)
        ]
        for copy in copies:
            copy.start()
        for copy in copies:
            copy.wait()

    anywhere = pl.BlockSpec(memory_space=pl.ANY)
    return pl.pallas_call(
        kernel,
        out_shape=jax.ShapeDtypeStruct((count * rows, pieces[0].shape[1]), pieces[0].dtype),
        in_specs=[anywhere] * count,
        out_specs=anywhere,
        scratch_shapes=[pltpu.SemaphoreType.DMA((count,))],
        cost_estimate=pl.CostEstimate(flops=0, transcendentals=0, bytes_accessed=0),
        name="joined",
    )(*pieces)


def columns(index, size):
    return slice(index * size, (index + 1) * size)


def short_kernel(proj_ref, prev_ref, taps_ref, query_ref, keyed_ref, valued_ref, product_ref):
    parts, _, blk = query_ref.shape
    for b in range(parts):

        def mixed(stream):
            cols = columns(stream * parts + b, blk)
            values = proj_ref[:, cols].astype(F32)
            before = prev_ref[:, cols]
            taps = taps_ref[:, cols]
            total = taps[0:1] * values + taps[1:2] * rows_down(values, 1, before)
            return (total + taps[2:3] * rows_down(values, 2, before)).astype(BF16)

        query_ref[b] = mixed(0)
        keyed, valued = (mixed(1), mixed(2))
        keyed_ref[b] = keyed
        valued_ref[b] = valued
        product_ref[b] = (keyed.astype(F32) * valued.astype(F32)).astype(BF16)


def grad_long_kernel(me_ref, query_ref, *refs):
    pieces, (gate_grad_ref, grad_long_ref) = refs[:-2], refs[-2:]
    parts, _, blk = query_ref.shape
    ratio = parts // len(pieces)
    for k, piece in enumerate(pieces):
        for i in range(ratio):
            b = (me_ref[0] ^ k) * ratio + i
            values = piece[:, columns(i, blk)]
            gate_grad_ref[b] = values
            grad_long_ref[b] = (values.astype(F32) * query_ref[b].astype(F32)).astype(BF16)


def gate_kernel(me_ref, me_dp_ref, query_ref, *refs):
    parts, _, blk = query_ref.shape
    came, long_ref, pieces = refs[: parts // 2], refs[parts // 2], refs[parts // 2 + 1 :]
    ratio = parts // len(pieces)
    size = blk * ratio // parts
    for k, piece in enumerate(came):
        b = me_ref[0] ^ (2 * k)
        long_ref[b] = piece[0]
        long_ref[b ^ 1] = piece[1]
    for k, piece in enumerate(pieces):
        for i in range(ratio):
            b = (me_dp_ref[0] ^ k) * ratio + i
            gate = (query_ref[b].astype(F32) * long_ref[b].astype(F32)).astype(BF16)
            for q in range(blk // size):
                c = i * (blk // size) + q
                piece[:, columns(c % 2 * (parts // 2) + c // 2, size)] = gate[:, columns(q, size)]


def final_kernel(me_ref, *refs):
    proj_ref, prev_ref, taps_ref, gate_grad_ref, long_ref, back_ref, keyed_ref, valued_ref = refs[:8]
    query_after_ref, pair_after_ref, skip_ref, out_ref, sums_ref = refs[8:]
    parts, rows, blk = long_ref.shape
    sums_ref[3:4, :] = jnp.zeros((1, sums_ref.shape[1]), F32)
    for b in range(parts):
        sums_ref[3:4, columns(b, blk)] = jnp.where(me_ref[0] == b, skip_ref[...], 0.0)
    for b in range(parts):
        back = back_ref[b, 0:rows].astype(F32)
        back_after = back_ref[b, rows : rows + 2].astype(F32)
        grads = (
            (
                gate_grad_ref[b].astype(F32) * long_ref[b].astype(F32),
                query_after_ref[b],
            ),
            (back * valued_ref[b].astype(F32), back_after * pair_after_ref[1, b]),
            (back * keyed_ref[b].astype(F32), back_after * pair_after_ref[0, b]),
        )
        for stream, (grad, after) in enumerate(grads):
            cols = columns(stream * parts + b, blk)
            taps = taps_ref[:, cols]
            total = taps[0:1] * grad + taps[1:2] * rows_up(grad, 1, after)
            out_ref[:, cols] = (total + taps[2:3] * rows_up(grad, 2, after)).astype(BF16)
            values = proj_ref[:, cols].astype(F32)
            before = prev_ref[:, cols]
            for j in range(3):
                moved = rows_down(values, j, before) if j else values
                sums_ref[j : j + 1, cols] = jnp.sum(grad * moved, 0, keepdims=True)


def table(first, freqs, seq_len):
    places = jnp.arange(seq_len)
    inner = min(32, freqs)
    outer = freqs // inner

    def waves(odd):
        phases = odd[:, None] * places[None, :] % (4 * seq_len)
        angles = phases.astype(F32) * (2.0 * math.pi / (4 * seq_len))
        return (jnp.cos(angles), jnp.sin(angles))

    outer_cos, outer_sin = waves(2 * (first + inner * jnp.arange(outer)))
    inner_cos, inner_sin = waves(2 * jnp.arange(inner) + 1)
    oc, os = (outer_cos[:, None], outer_sin[:, None])
    ic, is_ = (inner_cos[None], inner_sin[None])
    both = jnp.stack([oc * ic - os * is_, -(os * ic + oc * is_)])
    return both.astype(BF16).reshape(2 * freqs, seq_len)


def constant_table(seq_len):
    odd = 2 * np.arange(seq_len)[:, None] + 1
    angles = odd * np.arange(seq_len)[None, :] % (4 * seq_len) * (math.pi / (2 * seq_len))
    return np.stack([np.cos(angles), -np.sin(angles)]).astype(np.float32).astype(BF16)


def dot(left, right, left_dim, right_dim):
    return lax.dot_general(
        left, right, (((left_dim,), (right_dim,)), ((), ())), preferred_element_type=F32
    )


def spectral_product(left, right, conjugate_left):
    half = left.shape[0] // 2
    left_re, left_im = (left[:half], left[half:])
    right_re, right_im = (right[:half], right[half:])
    if conjugate_left:
        real = left_re * right_re + left_im * right_im
        imag = left_re * right_im - left_im * right_re
    else:
        real = left_re * right_re - left_im * right_im
        imag = left_re * right_im + left_im * right_re
    return jnp.concatenate([real, imag], 0).astype(BF16)


def filter_kernel(waves_ref, filter_ref, spec_ref):
    values = filter_ref[...].astype(BF16)
    for i in range(2):
        spec_ref[i] = dot(values, waves_ref[i], 1, 1)


def out_kernel(waves_ref, filter_spec_ref, product_ref, skip_ref, spec_ref, long_ref, turned, total):
    step = pl.program_id(0)

    @pl.when(step == 0)
    def _():
        turned[...] = product_ref[...].astype(F32).T.astype(BF16)
        total[...] = jnp.zeros_like(total)

    spec_re, spec_im = (dot(turned[...], waves_ref[i], 1, 1) for i in range(2))
    spec_ref[0], spec_ref[1] = (spec_re, spec_im)
    filter_re, filter_im = (filter_spec_ref[0], filter_spec_ref[1])
    real = (filter_re * spec_re - filter_im * spec_im).astype(BF16)
    imag = (filter_re * spec_im + filter_im * spec_re).astype(BF16)
    total[...] += dot(real, waves_ref[0], 1, 0) + dot(imag, waves_ref[1], 1, 0)

    @pl.when(step == pl.num_programs(0) - 1)
    def _():
        inverse = 1.0 / total.shape[1]
        direct = skip_ref[...] * product_ref[...].astype(F32)
        long_ref[...] = (total[...].T * inverse + direct).astype(BF16)


def back_kernel(
    waves_ref, filter_spec_ref, spec_ref, grad_ref, product_ref, skip_ref,
    back_ref, lag_ref, sum_ref, turned, total,
):
    step = pl.program_id(0)

    @pl.when(step == 0)
    def _():
        turned[...] = grad_ref[...].astype(F32).T.astype(BF16)
        total[...] = jnp.zeros_like(total)
        lag_ref[...] = jnp.zeros_like(lag_ref)

    grad_re, grad_im = (dot(turned[...], waves_ref[i], 1, 1) for i in range(2))
    for ref, sums in ((filter_spec_ref, total), (spec_ref, lag_ref)):
        left_re, left_im = (ref[0], ref[1])
        real = (left_re * grad_re + left_im * grad_im).astype(BF16)
        imag = (left_re * grad_im - left_im * grad_re).astype(BF16)
        sums[...] += dot(real, waves_ref[0], 1, 0) + dot(imag, waves_ref[1], 1, 0)

    @pl.when(step == pl.num_programs(0) - 1)
    def _():
        inverse = 1.0 / total.shape[1]
        parts, rows = (back_ref.shape[0], back_ref.shape[1] - 2)
        grad = grad_ref[...].astype(F32)
        back = (total[...].T * inverse + skip_ref[...] * grad).astype(BF16)
        for b in range(parts):
            back_ref[b, 0:rows] = back[b * rows : (b + 1) * rows]
            if b < parts - 1:
                back_ref[b, rows : rows + 2] = back[(b + 1) * rows : (b + 1) * rows + 2]
            else:
                back_ref[b, rows : rows + 2] = jnp.zeros((2, back.shape[1]), BF16)
        sum_ref[...] = jnp.sum(grad * product_ref[...].astype(F32), 0, keepdims=True)


def chunked(kernel, name, waves, specs, planes, outs, spec_out, scratch):
    freqs, seq_len = waves.shape[1:]
    size = min(256, freqs)
    blk = (specs + spec_out)[0].shape[1]
    chunk = pl.BlockSpec((2, blk, size), lambda i: (0, 0, i))

    def whole(array):
        return pl.BlockSpec(array.shape, lambda i: (0,) * len(array.shape))

    return pl.pallas_call(
        kernel,
        out_shape=spec_out + outs,
        grid=(freqs // size,),
        in_specs=[pl.BlockSpec((2, size, seq_len), lambda i: (0, i, 0))]
        + [chunk] * len(specs)
        + [whole(a) for a in planes],
        out_specs=[chunk] * len(spec_out) + [whole(a) for a in outs],
        scratch_shapes=scratch,
        compiler_params=pltpu.CompilerParams(vmem_limit_bytes=60 * 2**20),
        cost_estimate=pl.CostEstimate(flops=0, transcendentals=0, bytes_accessed=0),
        name=name,
    )(waves, *specs, *planes)


def ordered(value, *first):
    return lax.optimization_barrier((value, *first))[0]


def transforms(waves, long_filter, product, grad_long):
    filter_spec = dot(waves, long_filter, 1, 1)
    product_spec = dot(waves, product, 1, 0)
    grad_spec = dot(waves, grad_long, 1, 0)
    out = dot(waves, spectral_product(filter_spec, product_spec, False), 0, 0)
    back = dot(waves, spectral_product(filter_spec, grad_spec, True), 0, 0)
    lag_grad = dot(spectral_product(product_spec, grad_spec, True), waves, 0, 0)
    return (out, back, lag_grad)


def all_sum(value, axis, bits):
    for pair in [bits[i : i + 2] for i in range(0, len(bits), 2)]:
        sums = [value]
        for bit in pair:
            sums += [swapped(value, axis, bit)]
        if len(pair) == 2:
            far = swapped(value, axis, pair[0] + pair[1])
            value = (sums[0] + sums[1]) + (sums[2] + far)
        else:
            value = sums[0] + sums[1]
    return value


def bits_of(count, first=1):
    return [1 << i for i in range(count.bit_length() - 1) if 1 << i >= first]


def own_share(gate_all, cot_all, parts):
    core = lax.axis_index("context") % 2
    width = gate_all.shape[1] // 2
    other = dot(lax.dynamic_slice_in_dim(gate_all, (1 - core) * width, width, 1), cot_all, 0, 0)
    other = other.astype(BF16)
    own_gate = ordered(lax.dynamic_slice_in_dim(gate_all, core * width, width, 1), other)
    own = dot(own_gate, cot_all, 0, 0)
    pair = (own + swapped(other, "context", 1).astype(F32)).astype(BF16)
    pair = pair.reshape(parts // 2, -1, pair.shape[-1])
    row = lax.axis_index("context") // 2
    shares = [lax.dynamic_index_in_dim(pair, row, 0, False)]
    for k in range(1, parts // 2):
        sent = lax.dynamic_index_in_dim(pair, row ^ k, 0, False)
        shares.append(swapped(sent, "context", 2 * k))
    return (pair, shares)


def summed_blocks(value, axis, dim):
    count = lax.axis_size(axis)
    size = value.shape[dim] // count
    me = lax.axis_index(axis)
    total = lax.dynamic_slice_in_dim(value, me * size, size, dim)
    for k in range(1, count):
        sent = lax.dynamic_slice_in_dim(value, (me ^ k) * size, size, dim).astype(BF16)
        total = total + swapped(sent, axis, k).astype(F32)
    return total


def to_channels(blocks):
    came = lax.all_to_all(blocks, "context", split_axis=0, concat_axis=0, tiled=True)
    return came.reshape(-1, came.shape[-1])


def to_positions(blocks):
    return lax.all_to_all(blocks, "context", split_axis=0, concat_axis=0, tiled=True)


def body(projected, short_taps, long_filter, skip_gain, out_proj, cotangent):
    rows, width = projected.shape
    chans = width // 3
    parts_dp, parts = (lax.axis_size("dp"), lax.axis_size("context"))
    blk = chans // parts
    seq_len = rows * parts
    scale_factor = 1.0 / math.sqrt(seq_len * parts_dp)
    me = lax.axis_index("context").astype(jnp.int32)
    me_dp = lax.axis_index("dp").astype(jnp.int32)[None]
    plane = jax.ShapeDtypeStruct((parts, rows, blk), BF16)

    prev_rows = passed_along(projected[rows - 2 :], "context", 1).astype(F32)
    cots = [cotangent] + [swapped(cotangent, "dp", k) for k in range(1, parts_dp)]
    query, keyed, valued, product_out = call(
        short_kernel, "short_convs", [plane] * 4, 0, 60, projected, prev_rows, short_taps
    )
    product = to_channels(product_out)

    filter_b = long_filter.astype(BF16)
    inverse = 1.0 / seq_len
    straight = seq_len <= 1024
    weights = out_proj
    if straight:
        waves = jnp.asarray(constant_table(seq_len))
        spec = jax.ShapeDtypeStruct((2, blk, seq_len), F32)
        scratch = [pltpu.VMEM((blk, seq_len), BF16), pltpu.VMEM((blk, seq_len), F32)]
        skip_row = skip_gain[None, :]
        (filter_spec,) = chunked(
            filter_kernel, "filter_spectrum", waves, [], [long_filter], [], [spec], []
        )
        weights = ordered(out_proj, filter_spec)
    found = [dot(cot, weights, 1, 1).astype(BF16) for cot in cots]
    found = [found[0]] + [swapped(found[k], "dp", k) for k in range(1, parts_dp)]
    cot_all = joined(cots)
    found[0] = ordered(found[0], cot_all)
    gate_grad, grad_long_out = call(
        grad_long_kernel, "grad_long", [plane] * 2, 1, 12, me_dp, query, *found
    )
    grad_long = to_channels(grad_long_out)
    product_f, grad_long_f = (product.astype(F32), grad_long.astype(F32))

    def finished(total, direct):
        return (total * inverse + skip_gain[None, :] * direct).astype(BF16)

    def crossed(values):
        by_core = values.reshape(parts // 2, 2, rows, blk)
        core, row = (me % 2, me // 2)
        mine = lax.dynamic_index_in_dim(by_core, core, 1, False)
        near = swapped(lax.dynamic_index_in_dim(by_core, 1 - core, 1, False), "context", 1)
        stacked = jnp.stack([mine, near], 1)
        came = [lax.dynamic_index_in_dim(stacked, row, 0, False)]
        for k in range(1, parts // 2):
            sent = lax.dynamic_index_in_dim(stacked, row ^ k, 0, False)
            came.append(swapped(sent, "context", 2 * k))
        return came

    if straight:
        late_product = ordered(product, grad_long_out)
        product_spec, long_chan = chunked(
            out_kernel,
            "long_out",
            waves,
            [filter_spec],
            [late_product, skip_row],
            [jax.ShapeDtypeStruct((seq_len, blk), BF16)],
            [spec],
            scratch,
        )
        long_came = crossed(long_chan)
        back_sent, lag_sum, skip_sum = chunked(
            back_kernel,
            "grad_product",
            waves,
            [filter_spec, product_spec],
            [ordered(grad_long, long_came[1]), product, skip_row],
            [
                jax.ShapeDtypeStruct((parts, rows + 2, blk), BF16),
                jax.ShapeDtypeStruct((blk, seq_len), F32),
                jax.ShapeDtypeStruct((1, blk), F32),
            ],
            [],
            scratch,
        )
    else:
        freqs = 256

        def step(carry, first):
            new = transforms(table(first, freqs, seq_len), filter_b, product, grad_long)
            return (tuple(a + b for a, b in zip(carry, new)), None)

        zero = jnp.zeros((seq_len, blk), F32)
        start = (zero, zero, jnp.zeros((blk, seq_len), F32))
        terms, _ = lax.scan(step, start, jnp.arange(0, seq_len, freqs))
        out_sum, back_sum, lag_sum = terms
        long_came = crossed(finished(out_sum, product_f))
        back_blocks = finished(back_sum, grad_long_f).reshape(parts, rows, blk)
        next_heads = jnp.concatenate([back_blocks[1:, :2], jnp.zeros((1, 2, blk), BF16)], 0)
        back_sent = jnp.concatenate([back_blocks, next_heads], 1)
        skip_sum = jnp.sum(grad_long_f * product_f, 0, keepdims=True)
    grad_product = to_positions(back_sent)
    heads = ordered(jnp.stack([keyed[:, :2], valued[:, :2]]), grad_long_out)
    pair_after = passed_along(heads, "context", -1).astype(F32)
    long_came = lax.optimization_barrier((*long_came, back_sent, pair_after))[: parts // 2]

    piece = jax.ShapeDtypeStruct((rows, chans // parts_dp), BF16)
    long_out, *gates = call(
        gate_kernel, "gate", [plane] + [piece] * parts_dp, 2, 12, me[None], me_dp, query, *long_came
    )
    gates = [gates[0]] + [swapped(gates[k], "dp", k) for k in range(1, parts_dp)]
    query_heads = gate_grad[:, :2].astype(F32) * long_out[:, :2].astype(F32)
    query_after = passed_along(query_heads, "context", -1)
    grad_filter = summed_blocks(lag_sum, "dp", 1) * (scale_factor * inverse)
    early = (grad_product, query_after, grad_filter)
    gate_all = ordered(jnp.concatenate(gates, 0), *early)
    pair, shares = own_share(gate_all, cot_all, parts)
    grad_product = ordered(grad_product, pair)

    grad_inputs, tap_sums = call(
        final_kernel,
        "stream_grads",
        [
            jax.ShapeDtypeStruct((rows, width), BF16),
            jax.ShapeDtypeStruct((4, width), F32),
        ],
        1,
        60,
        me[None],
        projected,
        prev_rows,
        short_taps,
        gate_grad,
        long_out,
        grad_product,
        keyed,
        valued,
        query_after,
        pair_after,
        skip_sum,
    )

    tap_sums = all_sum(tap_sums, "dp", bits_of(parts_dp))
    tap_sums = ordered(tap_sums + swapped(tap_sums, "context", 1), *shares[1:])
    tap_sums = all_sum(tap_sums, "context", bits_of(parts, 2)) * scale_factor
    grad_taps = tap_sums[:3]
    skip_blocks = tap_sums[3, :chans].reshape(parts, blk)
    grad_skip = lax.dynamic_index_in_dim(skip_blocks, me, 0, False)
    grad_proj = sum(share.astype(F32) for share in shares) * scale_factor
    return (grad_inputs, grad_taps, grad_filter, grad_skip, grad_proj)


def solution(mesh):
    placed = (
        P(("dp", "context"), None),
        P(),
        P("context", None),
        P("context"),
        P("dp", None),
        P(("dp", "context"), None),
    )
    return jax.shard_map(
        body,
        mesh=mesh,
        in_specs=placed,
        out_specs=(
            P(("dp", "context"), None),
            P(),
            P("context", "dp"),
            P("context"),
            P(("dp", "context"), None),
        ),
        check_vma=False,
    )
```

```python
import math

import jax
import jax.numpy as jnp
import numpy as np
from jax import lax
from jax.experimental import pallas as pl
from jax.experimental.pallas import tpu as pltpu
from jax.sharding import PartitionSpec as P

BF16 = jnp.bfloat16
F32 = jnp.float32


def passed_along(value, axis, steps):
    count = lax.axis_size(axis)
    initial, last = (max(0, -steps), min(count, count - steps))
    return lax.ppermute(value, axis, [(source, source + steps) for source in range(initial, last)])


def swapped(value, axis, mask):
    return lax.ppermute(value, axis, [(i, i ^ mask) for i in range(lax.axis_size(axis))])


SMEM = pl.BlockSpec(memory_space=pltpu.SMEM)


def rows_down(values, steps, before):
    row = lax.broadcasted_iota(jnp.int32, values.shape, 0)
    moved = pltpu.roll(values, steps, axis=0)
    if steps == 1:
        return jnp.where(row == 0, before[1:2], moved)
    return jnp.where(row == 0, before[0:1], jnp.where(row == 1, before[1:2], moved))


def rows_up(values, steps, after):
    count = values.shape[0]
    row = lax.broadcasted_iota(jnp.int32, values.shape, 0)
    moved = pltpu.roll(values, count - steps, axis=0)
    if steps == 1:
        return jnp.where(row == count - 1, after[0:1], moved)
    return jnp.where(row == count - 1, after[1:2], jnp.where(row == count - 2, after[0:1], moved))


def call(kernel, name, outs, smem, limit, *args):
    arrays = args[smem:]
    count, given = (len(arrays), len(outs))

    def run(*refs):
        ends = refs[smem : smem + count + given]
        *buffers, sems = refs[smem + count + given :]
        copies = []
        for i, (end, buffer) in enumerate(zip(ends, buffers)):
            pair = (end, buffer) if i < count else (buffer, end)
            copies.append(pltpu.make_async_copy(*pair, sems.at[i]))
        for copy in copies[:count]:
            copy.start()
        for copy in copies[:count]:
            copy.wait()
        kernel(*refs[:smem], *buffers)
        for copy in copies[count:]:
            copy.start()
        for copy in copies[count:]:
            copy.wait()

    anywhere = pl.BlockSpec(memory_space=pl.ANY)
    return pl.pallas_call(
        run,
        out_shape=outs,
        in_specs=[SMEM] * smem + [anywhere] * count,
        out_specs=[anywhere] * given,
        scratch_shapes=[pltpu.VMEM(a.shape, a.dtype) for a in (*arrays, *outs)]
        + [pltpu.SemaphoreType.DMA((count + given,))],
        compiler_params=pltpu.CompilerParams(vmem_limit_bytes=limit * 2**20),
        cost_estimate=pl.CostEstimate(flops=0, transcendentals=0, bytes_accessed=0),
        name=name,
    )(*args)


def columns(index, size):
    return slice(index * size, (index + 1) * size)


def short_kernel(proj_ref, prev_ref, taps_ref, query_ref, keyed_ref, valued_ref, product_ref):
    parts, _, blk = query_ref.shape
    for b in range(parts):

        def mixed(stream):
            cols = columns(stream * parts + b, blk)
            values = proj_ref[:, cols].astype(F32)
            before = prev_ref[:, cols]
            taps = taps_ref[:, cols]
            total = taps[0:1] * values + taps[1:2] * rows_down(values, 1, before)
            return (total + taps[2:3] * rows_down(values, 2, before)).astype(BF16)

        query_ref[b] = mixed(0)
        keyed, valued = (mixed(1), mixed(2))
        keyed_ref[b] = keyed
        valued_ref[b] = valued
        product_ref[b] = (keyed.astype(F32) * valued.astype(F32)).astype(BF16)


def grad_long_kernel(me_ref, query_ref, *refs):
    pieces, (gate_grad_ref, grad_long_ref) = refs[:-2], refs[-2:]
    parts, _, blk = query_ref.shape
    ratio = parts // len(pieces)
    for k, piece in enumerate(pieces):
        for i in range(ratio):
            b = (me_ref[0] ^ k) * ratio + i
            values = piece[:, columns(i, blk)]
            gate_grad_ref[b] = values
            grad_long_ref[b] = (values.astype(F32) * query_ref[b].astype(F32)).astype(BF16)


def gate_kernel(me_ref, me_dp_ref, query_ref, *refs):
    parts, _, blk = query_ref.shape
    came, long_ref, pieces = refs[: parts // 2], refs[parts // 2], refs[parts // 2 + 1 :]
    ratio = parts // len(pieces)
    size = blk * ratio // parts
    for k, piece in enumerate(came):
        b = me_ref[0] ^ (2 * k)
        long_ref[b] = piece[0]
        long_ref[b ^ 1] = piece[1]
    for k, piece in enumerate(pieces):
        for i in range(ratio):
            b = (me_dp_ref[0] ^ k) * ratio + i
            gate = (query_ref[b].astype(F32) * long_ref[b].astype(F32)).astype(BF16)
            for q in range(blk // size):
                c = i * (blk // size) + q
                piece[:, columns(c % 2 * (parts // 2) + c // 2, size)] = gate[:, columns(q, size)]


def final_kernel(me_ref, *refs):
    proj_ref, prev_ref, taps_ref, gate_grad_ref, long_ref, back_ref, keyed_ref, valued_ref = refs[:8]
    query_after_ref, pair_after_ref, skip_ref, out_ref, sums_ref = refs[8:]
    parts, rows, blk = long_ref.shape
    sums_ref[3:4, :] = jnp.zeros((1, sums_ref.shape[1]), F32)
    for b in range(parts):
        sums_ref[3:4, columns(b, blk)] = jnp.where(me_ref[0] == b, skip_ref[...], 0.0)
    for b in range(parts):
        back = back_ref[b, 0:rows].astype(F32)
        back_after = back_ref[b, rows : rows + 2].astype(F32)
        grads = (
            (
                gate_grad_ref[b].astype(F32) * long_ref[b].astype(F32),
                query_after_ref[b],
            ),
            (back * valued_ref[b].astype(F32), back_after * pair_after_ref[1, b]),
            (back * keyed_ref[b].astype(F32), back_after * pair_after_ref[0, b]),
        )
        for stream, (grad, after) in enumerate(grads):
            cols = columns(stream * parts + b, blk)
            taps = taps_ref[:, cols]
            total = taps[0:1] * grad + taps[1:2] * rows_up(grad, 1, after)
            out_ref[:, cols] = (total + taps[2:3] * rows_up(grad, 2, after)).astype(BF16)
            values = proj_ref[:, cols].astype(F32)
            before = prev_ref[:, cols]
            for j in range(3):
                moved = rows_down(values, j, before) if j else values
                sums_ref[j : j + 1, cols] = jnp.sum(grad * moved, 0, keepdims=True)


def table(first, freqs, seq_len):
    places = jnp.arange(seq_len)
    inner = min(32, freqs)
    outer = freqs // inner

    def waves(odd):
        phases = odd[:, None] * places[None, :] % (4 * seq_len)
        angles = phases.astype(F32) * (2.0 * math.pi / (4 * seq_len))
        return (jnp.cos(angles), jnp.sin(angles))

    outer_cos, outer_sin = waves(2 * (first + inner * jnp.arange(outer)))
    inner_cos, inner_sin = waves(2 * jnp.arange(inner) + 1)
    oc, os = (outer_cos[:, None], outer_sin[:, None])
    ic, is_ = (inner_cos[None], inner_sin[None])
    both = jnp.stack([oc * ic - os * is_, -(os * ic + oc * is_)])
    return both.astype(BF16).reshape(2 * freqs, seq_len)


def constant_table(seq_len):
    odd = 2 * np.arange(seq_len)[:, None] + 1
    angles = odd * np.arange(seq_len)[None, :] % (4 * seq_len) * (math.pi / (2 * seq_len))
    return np.stack([np.cos(angles), -np.sin(angles)]).astype(np.float32).astype(BF16)


def dot(left, right, left_dim, right_dim):
    return lax.dot_general(
        left, right, (((left_dim,), (right_dim,)), ((), ())), preferred_element_type=F32
    )


def spectral_product(left, right, conjugate_left):
    half = left.shape[0] // 2
    left_re, left_im = (left[:half], left[half:])
    right_re, right_im = (right[:half], right[half:])
    if conjugate_left:
        real = left_re * right_re + left_im * right_im
        imag = left_re * right_im - left_im * right_re
    else:
        real = left_re * right_re - left_im * right_im
        imag = left_re * right_im + left_im * right_re
    return jnp.concatenate([real, imag], 0).astype(BF16)


def filter_kernel(waves_ref, filter_ref, spec_ref):
    values = filter_ref[...].astype(BF16)
    for i in range(2):
        spec_ref[i] = dot(values, waves_ref[i], 1, 1)


def out_kernel(waves_ref, filter_spec_ref, product_ref, skip_ref, spec_ref, long_ref, turned, total):
    step = pl.program_id(0)

    @pl.when(step == 0)
    def _():
        turned[...] = product_ref[...].astype(F32).T.astype(BF16)
        total[...] = jnp.zeros_like(total)

    spec_re, spec_im = (dot(turned[...], waves_ref[i], 1, 1) for i in range(2))
    spec_ref[0], spec_ref[1] = (spec_re, spec_im)
    filter_re, filter_im = (filter_spec_ref[0], filter_spec_ref[1])
    real = (filter_re * spec_re - filter_im * spec_im).astype(BF16)
    imag = (filter_re * spec_im + filter_im * spec_re).astype(BF16)
    total[...] += dot(real, waves_ref[0], 1, 0) + dot(imag, waves_ref[1], 1, 0)

    @pl.when(step == pl.num_programs(0) - 1)
    def _():
        inverse = 1.0 / total.shape[1]
        direct = skip_ref[...] * product_ref[...].astype(F32)
        long_ref[...] = (total[...].T * inverse + direct).astype(BF16)


def back_kernel(
    waves_ref, filter_spec_ref, spec_ref, grad_ref, product_ref, skip_ref,
    back_ref, lag_ref, sum_ref, turned, total,
):
    step = pl.program_id(0)

    @pl.when(step == 0)
    def _():
        turned[...] = grad_ref[...].astype(F32).T.astype(BF16)
        total[...] = jnp.zeros_like(total)
        lag_ref[...] = jnp.zeros_like(lag_ref)

    grad_re, grad_im = (dot(turned[...], waves_ref[i], 1, 1) for i in range(2))
    for ref, sums in ((filter_spec_ref, total), (spec_ref, lag_ref)):
        left_re, left_im = (ref[0], ref[1])
        real = (left_re * grad_re + left_im * grad_im).astype(BF16)
        imag = (left_re * grad_im - left_im * grad_re).astype(BF16)
        sums[...] += dot(real, waves_ref[0], 1, 0) + dot(imag, waves_ref[1], 1, 0)

    @pl.when(step == pl.num_programs(0) - 1)
    def _():
        inverse = 1.0 / total.shape[1]
        parts, rows = (back_ref.shape[0], back_ref.shape[1] - 2)
        grad = grad_ref[...].astype(F32)
        back = (total[...].T * inverse + skip_ref[...] * grad).astype(BF16)
        for b in range(parts):
            back_ref[b, 0:rows] = back[b * rows : (b + 1) * rows]
            if b < parts - 1:
                back_ref[b, rows : rows + 2] = back[(b + 1) * rows : (b + 1) * rows + 2]
            else:
                back_ref[b, rows : rows + 2] = jnp.zeros((2, back.shape[1]), BF16)
        sum_ref[...] = jnp.sum(grad * product_ref[...].astype(F32), 0, keepdims=True)


def chunked(kernel, name, waves, specs, planes, outs, spec_out, scratch):
    freqs, seq_len = waves.shape[1:]
    size = min(256, freqs)
    blk = (specs + spec_out)[0].shape[1]
    chunk = pl.BlockSpec((2, blk, size), lambda i: (0, 0, i))

    def whole(array):
        return pl.BlockSpec(array.shape, lambda i: (0,) * len(array.shape))

    return pl.pallas_call(
        kernel,
        out_shape=spec_out + outs,
        grid=(freqs // size,),
        in_specs=[pl.BlockSpec((2, size, seq_len), lambda i: (0, i, 0))]
        + [chunk] * len(specs)
        + [whole(a) for a in planes],
        out_specs=[chunk] * len(spec_out) + [whole(a) for a in outs],
        scratch_shapes=scratch,
        compiler_params=pltpu.CompilerParams(vmem_limit_bytes=60 * 2**20),
        cost_estimate=pl.CostEstimate(flops=0, transcendentals=0, bytes_accessed=0),
        name=name,
    )(waves, *specs, *planes)


def ordered(value, *first):
    return lax.optimization_barrier((value, *first))[0]


def transforms(waves, long_filter, product, grad_long):
    filter_spec = dot(waves, long_filter, 1, 1)
    product_spec = dot(waves, product, 1, 0)
    grad_spec = dot(waves, grad_long, 1, 0)
    out = dot(waves, spectral_product(filter_spec, product_spec, False), 0, 0)
    back = dot(waves, spectral_product(filter_spec, grad_spec, True), 0, 0)
    lag_grad = dot(spectral_product(product_spec, grad_spec, True), waves, 0, 0)
    return (out, back, lag_grad)


def all_sum(value, axis, bits):
    for pair in [bits[i : i + 2] for i in range(0, len(bits), 2)]:
        sums = [value]
        for bit in pair:
            sums += [swapped(value, axis, bit)]
        if len(pair) == 2:
            far = swapped(value, axis, pair[0] + pair[1])
            value = (sums[0] + sums[1]) + (sums[2] + far)
        else:
            value = sums[0] + sums[1]
    return value


def bits_of(count, first=1):
    return [1 << i for i in range(count.bit_length() - 1) if 1 << i >= first]


def own_share(gate_all, cot_all, parts):
    core = lax.axis_index("context") % 2
    width = gate_all.shape[1] // 2
    other = dot(lax.dynamic_slice_in_dim(gate_all, (1 - core) * width, width, 1), cot_all, 0, 0)
    other = other.astype(BF16)
    own_gate = ordered(lax.dynamic_slice_in_dim(gate_all, core * width, width, 1), other)
    own = dot(own_gate, cot_all, 0, 0)
    pair = (own + swapped(other, "context", 1).astype(F32)).astype(BF16)
    pair = pair.reshape(parts // 2, -1, pair.shape[-1])
    row = lax.axis_index("context") // 2
    shares = [lax.dynamic_index_in_dim(pair, row, 0, False)]
    for k in range(1, parts // 2):
        sent = lax.dynamic_index_in_dim(pair, row ^ k, 0, False)
        shares.append(swapped(sent, "context", 2 * k))
    return (pair, shares)


def summed_blocks(value, axis, dim):
    count = lax.axis_size(axis)
    size = value.shape[dim] // count
    me = lax.axis_index(axis)
    total = lax.dynamic_slice_in_dim(value, me * size, size, dim)
    for k in range(1, count):
        sent = lax.dynamic_slice_in_dim(value, (me ^ k) * size, size, dim).astype(BF16)
        total = total + swapped(sent, axis, k).astype(F32)
    return total


def to_channels(blocks):
    came = lax.all_to_all(blocks, "context", split_axis=0, concat_axis=0, tiled=True)
    return came.reshape(-1, came.shape[-1])


def to_positions(blocks):
    return lax.all_to_all(blocks, "context", split_axis=0, concat_axis=0, tiled=True)


def body(projected, short_taps, long_filter, skip_gain, out_proj, cotangent):
    rows, width = projected.shape
    chans = width // 3
    parts_dp, parts = (lax.axis_size("dp"), lax.axis_size("context"))
    blk = chans // parts
    seq_len = rows * parts
    scale_factor = 1.0 / math.sqrt(seq_len * parts_dp)
    me = lax.axis_index("context").astype(jnp.int32)
    me_dp = lax.axis_index("dp").astype(jnp.int32)[None]
    plane = jax.ShapeDtypeStruct((parts, rows, blk), BF16)

    prev_rows = passed_along(projected[rows - 2 :], "context", 1).astype(F32)
    cots = [cotangent] + [swapped(cotangent, "dp", k) for k in range(1, parts_dp)]
    query, keyed, valued, product_out = call(
        short_kernel, "short_convs", [plane] * 4, 0, 60, projected, prev_rows, short_taps
    )
    product = to_channels(product_out)

    filter_b = long_filter.astype(BF16)
    inverse = 1.0 / seq_len
    straight = seq_len <= 1024
    found = [dot(cot, out_proj, 1, 1).astype(BF16) for cot in cots]
    if straight:
        waves = jnp.asarray(constant_table(seq_len))
        spec = jax.ShapeDtypeStruct((2, blk, seq_len), F32)
        scratch = [pltpu.VMEM((blk, seq_len), BF16), pltpu.VMEM((blk, seq_len), F32)]
        skip_row = skip_gain[None, :]
        (filter_spec,) = chunked(
            filter_kernel, "filter_spectrum", waves, [], [ordered(long_filter, *found)], [], [spec], []
        )
        found[0] = ordered(found[0], filter_spec)
    found = [found[0]] + [swapped(found[k], "dp", k) for k in range(1, parts_dp)]
    gate_grad, grad_long_out = call(
        grad_long_kernel, "grad_long", [plane] * 2, 1, 12, me_dp, query, *found
    )
    grad_long = to_channels(grad_long_out)
    product_f, grad_long_f = (product.astype(F32), grad_long.astype(F32))

    def finished(total, direct):
        return (total * inverse + skip_gain[None, :] * direct).astype(BF16)

    heads = ordered(jnp.stack([keyed[:, :2], valued[:, :2]]), grad_long_out)
    pair_after = passed_along(heads, "context", -1).astype(F32)

    def crossed(values):
        by_core = values.reshape(parts // 2, 2, rows, blk)
        core, row = (me % 2, me // 2)
        mine = lax.dynamic_index_in_dim(by_core, core, 1, False)
        near = swapped(lax.dynamic_index_in_dim(by_core, 1 - core, 1, False), "context", 1)
        stacked = jnp.stack([mine, near], 1)
        came = [lax.dynamic_index_in_dim(stacked, row, 0, False)]
        for k in range(1, parts // 2):
            sent = lax.dynamic_index_in_dim(stacked, row ^ k, 0, False)
            came.append(swapped(sent, "context", 2 * k))
        return came

    if straight:
        late_product = ordered(product, grad_long_out)
        product_spec, long_chan = chunked(
            out_kernel,
            "long_out",
            waves,
            [filter_spec],
            [late_product, skip_row],
            [jax.ShapeDtypeStruct((seq_len, blk), BF16)],
            [spec],
            scratch,
        )
        long_came = crossed(long_chan)
        back_sent, lag_sum, skip_sum = chunked(
            back_kernel,
            "grad_product",
            waves,
            [filter_spec, product_spec],
            [ordered(grad_long, long_came[1], pair_after), product, skip_row],
            [
                jax.ShapeDtypeStruct((parts, rows + 2, blk), BF16),
                jax.ShapeDtypeStruct((blk, seq_len), F32),
                jax.ShapeDtypeStruct((1, blk), F32),
            ],
            [],
            scratch,
        )
    else:
        freqs = 256

        def step(carry, first):
            new = transforms(table(first, freqs, seq_len), filter_b, product, grad_long)
            return (tuple(a + b for a, b in zip(carry, new)), None)

        zero = jnp.zeros((seq_len, blk), F32)
        start = (zero, zero, jnp.zeros((blk, seq_len), F32))
        terms, _ = lax.scan(step, start, jnp.arange(0, seq_len, freqs))
        out_sum, back_sum, lag_sum = terms
        long_came = crossed(finished(out_sum, product_f))
        back_blocks = finished(back_sum, grad_long_f).reshape(parts, rows, blk)
        next_heads = jnp.concatenate([back_blocks[1:, :2], jnp.zeros((1, 2, blk), BF16)], 0)
        back_sent = jnp.concatenate([back_blocks, next_heads], 1)
        skip_sum = jnp.sum(grad_long_f * product_f, 0, keepdims=True)
    grad_product = to_positions(back_sent)
    long_came = lax.optimization_barrier((*long_came, back_sent, pair_after))[: parts // 2]

    piece = jax.ShapeDtypeStruct((rows, chans // parts_dp), BF16)
    long_out, *gates = call(
        gate_kernel, "gate", [plane] + [piece] * parts_dp, 2, 12, me[None], me_dp, query, *long_came
    )
    gates = [gates[0]] + [swapped(gates[k], "dp", k) for k in range(1, parts_dp)]
    query_heads = gate_grad[:, :2].astype(F32) * long_out[:, :2].astype(F32)
    query_after = passed_along(query_heads, "context", -1)
    early = (grad_product, query_after)
    cot_all = jnp.concatenate(lax.optimization_barrier((*cots, gates[0]))[:parts_dp], 0)
    gate_all = ordered(jnp.concatenate(gates, 0), *early)
    pair, shares = own_share(gate_all, cot_all, parts)
    grad_product = ordered(grad_product, pair)

    grad_inputs, tap_sums = call(
        final_kernel,
        "stream_grads",
        [
            jax.ShapeDtypeStruct((rows, width), BF16),
            jax.ShapeDtypeStruct((4, width), F32),
        ],
        1,
        60,
        me[None],
        projected,
        prev_rows,
        short_taps,
        gate_grad,
        long_out,
        grad_product,
        keyed,
        valued,
        query_after,
        pair_after,
        skip_sum,
    )

    tap_sums = all_sum(tap_sums, "dp", bits_of(parts_dp))
    lag_sum = ordered(lag_sum, tap_sums)
    grad_filter = summed_blocks(lag_sum, "dp", 1) * (scale_factor * inverse)
    tap_sums = ordered(tap_sums + swapped(tap_sums, "context", 1), *shares[1:])
    tap_sums = all_sum(tap_sums, "context", bits_of(parts, 2)) * scale_factor
    grad_taps = tap_sums[:3]
    skip_blocks = tap_sums[3, :chans].reshape(parts, blk)
    grad_skip = lax.dynamic_index_in_dim(skip_blocks, me, 0, False)
    grad_proj = sum(share.astype(F32) for share in shares) * scale_factor
    return (grad_inputs, grad_taps, grad_filter, grad_skip, grad_proj)


def solution(mesh):
    placed = (
        P(("dp", "context"), None),
        P(),
        P("context", None),
        P("context"),
        P("dp", None),
        P(("dp", "context"), None),
    )
    return jax.shard_map(
        body,
        mesh=mesh,
        in_specs=placed,
        out_specs=(
            P(("dp", "context"), None),
            P(),
            P("context", "dp"),
            P("context"),
            P(("dp", "context"), None),
        ),
        check_vma=False,
    )
```

```python
import math

import jax
import jax.numpy as jnp
import numpy as np
from jax import lax
from jax.experimental import pallas as pl
from jax.experimental.pallas import tpu as pltpu
from jax.sharding import PartitionSpec as P

BF16 = jnp.bfloat16
F32 = jnp.float32


def passed_along(value, axis, steps):
    count = lax.axis_size(axis)
    initial, last = (max(0, -steps), min(count, count - steps))
    return lax.ppermute(value, axis, [(source, source + steps) for source in range(initial, last)])


def swapped(value, axis, mask):
    return lax.ppermute(value, axis, [(i, i ^ mask) for i in range(lax.axis_size(axis))])


SMEM = pl.BlockSpec(memory_space=pltpu.SMEM)


def rows_down(values, steps, before):
    row = lax.broadcasted_iota(jnp.int32, values.shape, 0)
    moved = pltpu.roll(values, steps, axis=0)
    if steps == 1:
        return jnp.where(row == 0, before[1:2], moved)
    return jnp.where(row == 0, before[0:1], jnp.where(row == 1, before[1:2], moved))


def rows_up(values, steps, after):
    count = values.shape[0]
    row = lax.broadcasted_iota(jnp.int32, values.shape, 0)
    moved = pltpu.roll(values, count - steps, axis=0)
    if steps == 1:
        return jnp.where(row == count - 1, after[0:1], moved)
    return jnp.where(row == count - 1, after[1:2], jnp.where(row == count - 2, after[0:1], moved))


def call(kernel, name, outs, smem, limit, *args):
    arrays = args[smem:]
    count, given = (len(arrays), len(outs))

    def run(*refs):
        ends = refs[smem : smem + count + given]
        *buffers, sems = refs[smem + count + given :]
        copies = []
        for i, (end, buffer) in enumerate(zip(ends, buffers)):
            pair = (end, buffer) if i < count else (buffer, end)
            copies.append(pltpu.make_async_copy(*pair, sems.at[i]))
        for copy in copies[:count]:
            copy.start()
        for copy in copies[:count]:
            copy.wait()
        kernel(*refs[:smem], *buffers)
        for copy in copies[count:]:
            copy.start()
        for copy in copies[count:]:
            copy.wait()

    anywhere = pl.BlockSpec(memory_space=pl.ANY)
    return pl.pallas_call(
        run,
        out_shape=outs,
        in_specs=[SMEM] * smem + [anywhere] * count,
        out_specs=[anywhere] * given,
        scratch_shapes=[pltpu.VMEM(a.shape, a.dtype) for a in (*arrays, *outs)]
        + [pltpu.SemaphoreType.DMA((count + given,))],
        compiler_params=pltpu.CompilerParams(vmem_limit_bytes=limit * 2**20),
        cost_estimate=pl.CostEstimate(flops=0, transcendentals=0, bytes_accessed=0),
        name=name,
    )(*args)


def columns(index, size):
    return slice(index * size, (index + 1) * size)


def short_kernel(proj_ref, prev_ref, taps_ref, query_ref, keyed_ref, valued_ref, product_ref):
    parts, _, blk = query_ref.shape
    for b in range(parts):

        def mixed(stream):
            cols = columns(stream * parts + b, blk)
            values = proj_ref[:, cols].astype(F32)
            before = prev_ref[:, cols]
            taps = taps_ref[:, cols]
            total = taps[0:1] * values + taps[1:2] * rows_down(values, 1, before)
            return (total + taps[2:3] * rows_down(values, 2, before)).astype(BF16)

        query_ref[b] = mixed(0)
        keyed, valued = (mixed(1), mixed(2))
        keyed_ref[b] = keyed
        valued_ref[b] = valued
        product_ref[b] = (keyed.astype(F32) * valued.astype(F32)).astype(BF16)


def grad_long_kernel(me_ref, query_ref, *refs):
    pieces, (gate_grad_ref, grad_long_ref) = refs[:-2], refs[-2:]
    parts, _, blk = query_ref.shape
    ratio = parts // len(pieces)
    for k, piece in enumerate(pieces):
        for i in range(ratio):
            b = (me_ref[0] ^ k) * ratio + i
            values = piece[:, columns(i, blk)]
            gate_grad_ref[b] = values
            grad_long_ref[b] = (values.astype(F32) * query_ref[b].astype(F32)).astype(BF16)


def gate_kernel(me_ref, me_dp_ref, query_ref, *refs):
    parts, _, blk = query_ref.shape
    came, long_ref, pieces = refs[: parts // 2], refs[parts // 2], refs[parts // 2 + 1 :]
    ratio = parts // len(pieces)
    size = blk * ratio // parts
    for k, piece in enumerate(came):
        b = me_ref[0] ^ (2 * k)
        long_ref[b] = piece[0]
        long_ref[b ^ 1] = piece[1]
    for k, piece in enumerate(pieces):
        for i in range(ratio):
            b = (me_dp_ref[0] ^ k) * ratio + i
            gate = (query_ref[b].astype(F32) * long_ref[b].astype(F32)).astype(BF16)
            for q in range(blk // size):
                c = i * (blk // size) + q
                piece[:, columns(c % 2 * (parts // 2) + c // 2, size)] = gate[:, columns(q, size)]


def final_kernel(*refs):
    proj_ref, prev_ref, taps_ref, gate_grad_ref, long_ref, back_ref, keyed_ref, valued_ref = refs[:8]
    query_after_ref, pair_after_ref, skip_ref, out_ref, sums_ref = refs[8:]
    parts, rows, blk = long_ref.shape
    sums_ref[3:4, :] = jnp.zeros((1, sums_ref.shape[1]), F32)
    sums_ref[3:4, 0:blk] = skip_ref[...]
    for b in range(parts):
        back = back_ref[b, 0:rows].astype(F32)
        back_after = back_ref[b, rows : rows + 2].astype(F32)
        grads = (
            (
                gate_grad_ref[b].astype(F32) * long_ref[b].astype(F32),
                query_after_ref[b],
            ),
            (back * valued_ref[b].astype(F32), back_after * pair_after_ref[1, b]),
            (back * keyed_ref[b].astype(F32), back_after * pair_after_ref[0, b]),
        )
        for stream, (grad, after) in enumerate(grads):
            cols = columns(stream * parts + b, blk)
            taps = taps_ref[:, cols]
            total = taps[0:1] * grad + taps[1:2] * rows_up(grad, 1, after)
            out_ref[:, cols] = (total + taps[2:3] * rows_up(grad, 2, after)).astype(BF16)
            values = proj_ref[:, cols].astype(F32)
            before = prev_ref[:, cols]
            for j in range(3):
                moved = rows_down(values, j, before) if j else values
                sums_ref[j : j + 1, cols] = jnp.sum(grad * moved, 0, keepdims=True)


def table(first, freqs, seq_len):
    places = jnp.arange(seq_len)
    inner = min(32, freqs)
    outer = freqs // inner

    def waves(odd):
        phases = odd[:, None] * places[None, :] % (4 * seq_len)
        angles = phases.astype(F32) * (2.0 * math.pi / (4 * seq_len))
        return (jnp.cos(angles), jnp.sin(angles))

    outer_cos, outer_sin = waves(2 * (first + inner * jnp.arange(outer)))
    inner_cos, inner_sin = waves(2 * jnp.arange(inner) + 1)
    oc, os = (outer_cos[:, None], outer_sin[:, None])
    ic, is_ = (inner_cos[None], inner_sin[None])
    both = jnp.stack([oc * ic - os * is_, -(os * ic + oc * is_)])
    return both.astype(BF16).reshape(2 * freqs, seq_len)


def constant_table(seq_len):
    odd = 2 * np.arange(seq_len)[:, None] + 1
    angles = odd * np.arange(seq_len)[None, :] % (4 * seq_len) * (math.pi / (2 * seq_len))
    return np.stack([np.cos(angles), -np.sin(angles)]).astype(np.float32).astype(BF16)


def dot(left, right, left_dim, right_dim):
    return lax.dot_general(
        left, right, (((left_dim,), (right_dim,)), ((), ())), preferred_element_type=F32
    )


def spectral_product(left, right, conjugate_left):
    half = left.shape[0] // 2
    left_re, left_im = (left[:half], left[half:])
    right_re, right_im = (right[:half], right[half:])
    if conjugate_left:
        real = left_re * right_re + left_im * right_im
        imag = left_re * right_im - left_im * right_re
    else:
        real = left_re * right_re - left_im * right_im
        imag = left_re * right_im + left_im * right_re
    return jnp.concatenate([real, imag], 0).astype(BF16)


def filter_kernel(waves_ref, filter_ref, spec_ref):
    values = filter_ref[...].astype(BF16)
    for i in range(2):
        spec_ref[i] = dot(values, waves_ref[i], 1, 1)


def out_kernel(waves_ref, filter_spec_ref, product_ref, skip_ref, spec_ref, long_ref, turned, total):
    step = pl.program_id(0)

    @pl.when(step == 0)
    def _():
        turned[...] = product_ref[...].astype(F32).T.astype(BF16)
        total[...] = jnp.zeros_like(total)

    spec_re, spec_im = (dot(turned[...], waves_ref[i], 1, 1) for i in range(2))
    spec_ref[0], spec_ref[1] = (spec_re, spec_im)
    filter_re, filter_im = (filter_spec_ref[0], filter_spec_ref[1])
    real = (filter_re * spec_re - filter_im * spec_im).astype(BF16)
    imag = (filter_re * spec_im + filter_im * spec_re).astype(BF16)
    total[...] += dot(real, waves_ref[0], 1, 0) + dot(imag, waves_ref[1], 1, 0)

    @pl.when(step == pl.num_programs(0) - 1)
    def _():
        inverse = 1.0 / total.shape[1]
        direct = skip_ref[...] * product_ref[...].astype(F32)
        long_ref[...] = (total[...].T * inverse + direct).astype(BF16)


def back_kernel(
    waves_ref, filter_spec_ref, spec_ref, grad_ref, product_ref, skip_ref,
    back_ref, lag_ref, sum_ref, turned, total,
):
    step = pl.program_id(0)

    @pl.when(step == 0)
    def _():
        turned[...] = grad_ref[...].astype(F32).T.astype(BF16)
        total[...] = jnp.zeros_like(total)
        lag_ref[...] = jnp.zeros_like(lag_ref)

    grad_re, grad_im = (dot(turned[...], waves_ref[i], 1, 1) for i in range(2))
    for ref, sums in ((filter_spec_ref, total), (spec_ref, lag_ref)):
        left_re, left_im = (ref[0], ref[1])
        real = (left_re * grad_re + left_im * grad_im).astype(BF16)
        imag = (left_re * grad_im - left_im * grad_re).astype(BF16)
        sums[...] += dot(real, waves_ref[0], 1, 0) + dot(imag, waves_ref[1], 1, 0)

    @pl.when(step == pl.num_programs(0) - 1)
    def _():
        inverse = 1.0 / total.shape[1]
        parts, rows = (back_ref.shape[0], back_ref.shape[1] - 2)
        grad = grad_ref[...].astype(F32)
        back = (total[...].T * inverse + skip_ref[...] * grad).astype(BF16)
        for b in range(parts):
            back_ref[b, 0:rows] = back[b * rows : (b + 1) * rows]
            if b < parts - 1:
                back_ref[b, rows : rows + 2] = back[(b + 1) * rows : (b + 1) * rows + 2]
            else:
                back_ref[b, rows : rows + 2] = jnp.zeros((2, back.shape[1]), BF16)
        sum_ref[...] = jnp.sum(grad * product_ref[...].astype(F32), 0, keepdims=True)


def chunked(kernel, name, waves, specs, planes, outs, spec_out, scratch):
    freqs, seq_len = waves.shape[1:]
    size = min(256, freqs)
    blk = (specs + spec_out)[0].shape[1]
    chunk = pl.BlockSpec((2, blk, size), lambda i: (0, 0, i))

    def whole(array):
        return pl.BlockSpec(array.shape, lambda i: (0,) * len(array.shape))

    return pl.pallas_call(
        kernel,
        out_shape=spec_out + outs,
        grid=(freqs // size,),
        in_specs=[pl.BlockSpec((2, size, seq_len), lambda i: (0, i, 0))]
        + [chunk] * len(specs)
        + [whole(a) for a in planes],
        out_specs=[chunk] * len(spec_out) + [whole(a) for a in outs],
        scratch_shapes=scratch,
        compiler_params=pltpu.CompilerParams(vmem_limit_bytes=60 * 2**20),
        cost_estimate=pl.CostEstimate(flops=0, transcendentals=0, bytes_accessed=0),
        name=name,
    )(waves, *specs, *planes)


def ordered(value, *first):
    return lax.optimization_barrier((value, *first))[0]


def transforms(waves, long_filter, product, grad_long):
    filter_spec = dot(waves, long_filter, 1, 1)
    product_spec = dot(waves, product, 1, 0)
    grad_spec = dot(waves, grad_long, 1, 0)
    out = dot(waves, spectral_product(filter_spec, product_spec, False), 0, 0)
    back = dot(waves, spectral_product(filter_spec, grad_spec, True), 0, 0)
    lag_grad = dot(spectral_product(product_spec, grad_spec, True), waves, 0, 0)
    return (out, back, lag_grad)


def all_sum(value, axis, bits):
    for pair in [bits[i : i + 2] for i in range(0, len(bits), 2)]:
        sums = [value]
        for bit in pair:
            sums += [swapped(value, axis, bit)]
        if len(pair) == 2:
            far = swapped(value, axis, pair[0] + pair[1])
            value = (sums[0] + sums[1]) + (sums[2] + far)
        else:
            value = sums[0] + sums[1]
    return value


def bits_of(count, first=1):
    return [1 << i for i in range(count.bit_length() - 1) if 1 << i >= first]


def own_share(gate_all, cot_all, parts):
    core = lax.axis_index("context") % 2
    width = gate_all.shape[1] // 2
    other = dot(lax.dynamic_slice_in_dim(gate_all, (1 - core) * width, width, 1), cot_all, 0, 0)
    other = other.astype(BF16)
    own_gate = ordered(lax.dynamic_slice_in_dim(gate_all, core * width, width, 1), other)
    own = dot(own_gate, cot_all, 0, 0)
    pair = (own + swapped(other, "context", 1).astype(F32)).astype(BF16)
    pair = pair.reshape(parts // 2, -1, pair.shape[-1])
    row = lax.axis_index("context") // 2
    shares = [lax.dynamic_index_in_dim(pair, row, 0, False)]
    for k in range(1, parts // 2):
        sent = lax.dynamic_index_in_dim(pair, row ^ k, 0, False)
        shares.append(swapped(sent, "context", 2 * k))
    return (pair, shares)


def summed_blocks(value, axis, dim):
    count = lax.axis_size(axis)
    size = value.shape[dim] // count
    me = lax.axis_index(axis)
    total = lax.dynamic_slice_in_dim(value, me * size, size, dim)
    for k in range(1, count):
        sent = lax.dynamic_slice_in_dim(value, (me ^ k) * size, size, dim).astype(BF16)
        total = total + swapped(sent, axis, k).astype(F32)
    return total


def to_channels(blocks):
    came = lax.all_to_all(blocks, "context", split_axis=0, concat_axis=0, tiled=True)
    return came.reshape(-1, came.shape[-1])


def to_positions(blocks):
    return lax.all_to_all(blocks, "context", split_axis=0, concat_axis=0, tiled=True)


def body(projected, short_taps, long_filter, skip_gain, out_proj, cotangent):
    rows, width = projected.shape
    chans = width // 3
    parts_dp, parts = (lax.axis_size("dp"), lax.axis_size("context"))
    blk = chans // parts
    seq_len = rows * parts
    scale_factor = 1.0 / math.sqrt(seq_len * parts_dp)
    me = lax.axis_index("context").astype(jnp.int32)
    me_dp = lax.axis_index("dp").astype(jnp.int32)[None]
    plane = jax.ShapeDtypeStruct((parts, rows, blk), BF16)

    prev_rows = passed_along(projected[rows - 2 :], "context", 1).astype(F32)
    cots = [cotangent] + [swapped(cotangent, "dp", k) for k in range(1, parts_dp)]
    query, keyed, valued, product_out = call(
        short_kernel, "short_convs", [plane] * 4, 0, 60, projected, prev_rows, short_taps
    )
    product = to_channels(product_out)

    filter_b = long_filter.astype(BF16)
    inverse = 1.0 / seq_len
    straight = seq_len <= 1024
    weights = out_proj
    if straight:
        waves = jnp.asarray(constant_table(seq_len))
        spec = jax.ShapeDtypeStruct((2, blk, seq_len), F32)
        scratch = [pltpu.VMEM((blk, seq_len), BF16), pltpu.VMEM((blk, seq_len), F32)]
        skip_row = skip_gain[None, :]
        (filter_spec,) = chunked(
            filter_kernel, "filter_spectrum", waves, [], [long_filter], [], [spec], []
        )
        weights = ordered(out_proj, filter_spec)
    found = [dot(cot, weights, 1, 1).astype(BF16) for cot in cots]
    found = [found[0]] + [swapped(found[k], "dp", k) for k in range(1, parts_dp)]
    gate_grad, grad_long_out = call(
        grad_long_kernel, "grad_long", [plane] * 2, 1, 12, me_dp, query, *found
    )
    heads = jnp.stack([keyed[:, :2], valued[:, :2]])
    pair_after = passed_along(heads, "context", -1).astype(F32)
    grad_long = to_channels(ordered(grad_long_out, pair_after))
    product_f, grad_long_f = (product.astype(F32), grad_long.astype(F32))

    def finished(total, direct):
        return (total * inverse + skip_gain[None, :] * direct).astype(BF16)

    def crossed(values):
        by_core = values.reshape(parts // 2, 2, rows, blk)
        core, row = (me % 2, me // 2)
        mine = lax.dynamic_index_in_dim(by_core, core, 1, False)
        near = swapped(lax.dynamic_index_in_dim(by_core, 1 - core, 1, False), "context", 1)
        stacked = jnp.stack([mine, near], 1)
        came = [lax.dynamic_index_in_dim(stacked, row, 0, False)]
        for k in range(1, parts // 2):
            sent = lax.dynamic_index_in_dim(stacked, row ^ k, 0, False)
            came.append(swapped(sent, "context", 2 * k))
        return came

    if straight:
        late_product = ordered(product, grad_long_out)
        product_spec, long_chan = chunked(
            out_kernel,
            "long_out",
            waves,
            [filter_spec],
            [late_product, skip_row],
            [jax.ShapeDtypeStruct((seq_len, blk), BF16)],
            [spec],
            scratch,
        )
        long_came = crossed(long_chan)
        back_sent, lag_sum, skip_sum = chunked(
            back_kernel,
            "grad_product",
            waves,
            [filter_spec, product_spec],
            [ordered(grad_long, long_came[1]), product, skip_row],
            [
                jax.ShapeDtypeStruct((parts, rows + 2, blk), BF16),
                jax.ShapeDtypeStruct((blk, seq_len), F32),
                jax.ShapeDtypeStruct((1, blk), F32),
            ],
            [],
            scratch,
        )
    else:
        freqs = 256

        def step(carry, first):
            new = transforms(table(first, freqs, seq_len), filter_b, product, grad_long)
            return (tuple(a + b for a, b in zip(carry, new)), None)

        zero = jnp.zeros((seq_len, blk), F32)
        start = (zero, zero, jnp.zeros((blk, seq_len), F32))
        terms, _ = lax.scan(step, start, jnp.arange(0, seq_len, freqs))
        out_sum, back_sum, lag_sum = terms
        long_came = crossed(finished(out_sum, product_f))
        back_blocks = finished(back_sum, grad_long_f).reshape(parts, rows, blk)
        next_heads = jnp.concatenate([back_blocks[1:, :2], jnp.zeros((1, 2, blk), BF16)], 0)
        back_sent = jnp.concatenate([back_blocks, next_heads], 1)
        skip_sum = jnp.sum(grad_long_f * product_f, 0, keepdims=True)
    grad_product = to_positions(back_sent)
    long_came = lax.optimization_barrier((*long_came, back_sent, pair_after))[: parts // 2]

    piece = jax.ShapeDtypeStruct((rows, chans // parts_dp), BF16)
    long_out, *gates = call(
        gate_kernel, "gate", [plane] + [piece] * parts_dp, 2, 12, me[None], me_dp, query, *long_came
    )
    gates = [gates[0]] + [swapped(gates[k], "dp", k) for k in range(1, parts_dp)]
    query_heads = gate_grad[:, :2].astype(F32) * long_out[:, :2].astype(F32)
    query_after = passed_along(query_heads, "context", -1)
    early = (grad_product, query_after)
    cot_all = jnp.concatenate(lax.optimization_barrier((*cots, gates[0]))[:parts_dp], 0)
    gate_all = ordered(jnp.concatenate(gates, 0), *early)
    pair, shares = own_share(gate_all, cot_all, parts)
    grad_product = ordered(grad_product, pair)

    grad_inputs, tap_sums = call(
        final_kernel,
        "stream_grads",
        [
            jax.ShapeDtypeStruct((rows, width), BF16),
            jax.ShapeDtypeStruct((4, width), F32),
        ],
        0,
        60,
        projected,
        prev_rows,
        short_taps,
        gate_grad,
        long_out,
        grad_product,
        keyed,
        valued,
        query_after,
        pair_after,
        skip_sum,
    )

    tap_sums = all_sum(tap_sums, "dp", bits_of(parts_dp))
    lag_sum = ordered(lag_sum, tap_sums)
    grad_filter = summed_blocks(lag_sum, "dp", 1) * (scale_factor * inverse)
    grad_skip = tap_sums[3, :blk] * scale_factor
    tap_sums = tap_sums[:3] + swapped(tap_sums[:3], "context", 1)
    tap_sums = ordered(tap_sums, *shares[1:])
    grad_taps = all_sum(tap_sums, "context", bits_of(parts, 2)) * scale_factor
    grad_proj = sum(share.astype(F32) for share in shares) * scale_factor
    return (grad_inputs, grad_taps, grad_filter, grad_skip, grad_proj)


def solution(mesh):
    placed = (
        P(("dp", "context"), None),
        P(),
        P("context", None),
        P("context"),
        P("dp", None),
        P(("dp", "context"), None),
    )
    return jax.shard_map(
        body,
        mesh=mesh,
        in_specs=placed,
        out_specs=(
            P(("dp", "context"), None),
            P(),
            P("context", "dp"),
            P("context"),
            P(("dp", "context"), None),
        ),
        check_vma=False,
    )
```

```python
import math

import jax
import jax.numpy as jnp
import numpy as np
from jax import lax
from jax.experimental import pallas as pl
from jax.experimental.pallas import tpu as pltpu
from jax.sharding import PartitionSpec as P

BF16 = jnp.bfloat16
F32 = jnp.float32


def passed_along(value, axis, steps):
    count = lax.axis_size(axis)
    initial, last = (max(0, -steps), min(count, count - steps))
    return lax.ppermute(value, axis, [(source, source + steps) for source in range(initial, last)])


def swapped(value, axis, mask):
    return lax.ppermute(value, axis, [(i, i ^ mask) for i in range(lax.axis_size(axis))])


SMEM = pl.BlockSpec(memory_space=pltpu.SMEM)


def rows_down(values, steps, before):
    row = lax.broadcasted_iota(jnp.int32, values.shape, 0)
    moved = pltpu.roll(values, steps, axis=0)
    if steps == 1:
        return jnp.where(row == 0, before[1:2], moved)
    return jnp.where(row == 0, before[0:1], jnp.where(row == 1, before[1:2], moved))


def rows_up(values, steps, after):
    count = values.shape[0]
    row = lax.broadcasted_iota(jnp.int32, values.shape, 0)
    moved = pltpu.roll(values, count - steps, axis=0)
    if steps == 1:
        return jnp.where(row == count - 1, after[0:1], moved)
    return jnp.where(row == count - 1, after[1:2], jnp.where(row == count - 2, after[0:1], moved))


def call(kernel, name, outs, smem, limit, *args):
    arrays = args[smem:]
    count, given = (len(arrays), len(outs))

    def run(*refs):
        ends = refs[smem : smem + count + given]
        *buffers, sems = refs[smem + count + given :]
        copies = []
        for i, (end, buffer) in enumerate(zip(ends, buffers)):
            pair = (end, buffer) if i < count else (buffer, end)
            copies.append(pltpu.make_async_copy(*pair, sems.at[i]))
        for copy in copies[:count]:
            copy.start()
        for copy in copies[:count]:
            copy.wait()
        kernel(*refs[:smem], *buffers)
        for copy in copies[count:]:
            copy.start()
        for copy in copies[count:]:
            copy.wait()

    anywhere = pl.BlockSpec(memory_space=pl.ANY)
    return pl.pallas_call(
        run,
        out_shape=outs,
        in_specs=[SMEM] * smem + [anywhere] * count,
        out_specs=[anywhere] * given,
        scratch_shapes=[pltpu.VMEM(a.shape, a.dtype) for a in (*arrays, *outs)]
        + [pltpu.SemaphoreType.DMA((count + given,))],
        compiler_params=pltpu.CompilerParams(vmem_limit_bytes=limit * 2**20),
        cost_estimate=pl.CostEstimate(flops=0, transcendentals=0, bytes_accessed=0),
        name=name,
    )(*args)


def columns(index, size):
    return slice(index * size, (index + 1) * size)


def short_kernel(proj_ref, prev_ref, taps_ref, query_ref, keyed_ref, valued_ref, product_ref):
    parts, _, blk = query_ref.shape
    for b in range(parts):

        def mixed(stream):
            cols = columns(stream * parts + b, blk)
            values = proj_ref[:, cols].astype(F32)
            before = prev_ref[:, cols]
            taps = taps_ref[:, cols]
            total = taps[0:1] * values + taps[1:2] * rows_down(values, 1, before)
            return (total + taps[2:3] * rows_down(values, 2, before)).astype(BF16)

        query_ref[b] = mixed(0)
        keyed, valued = (mixed(1), mixed(2))
        keyed_ref[b] = keyed
        valued_ref[b] = valued
        product_ref[b] = (keyed.astype(F32) * valued.astype(F32)).astype(BF16)


def grad_long_kernel(me_ref, query_ref, *refs):
    pieces, (gate_grad_ref, grad_long_ref) = refs[:-2], refs[-2:]
    parts, _, blk = query_ref.shape
    ratio = parts // len(pieces)
    for k, piece in enumerate(pieces):
        for i in range(ratio):
            b = (me_ref[0] ^ k) * ratio + i
            values = piece[:, columns(i, blk)]
            gate_grad_ref[b] = values
            grad_long_ref[b] = (values.astype(F32) * query_ref[b].astype(F32)).astype(BF16)


def gate_kernel(me_ref, me_dp_ref, query_ref, *refs):
    parts, _, blk = query_ref.shape
    came, long_ref, pieces = refs[: parts // 2], refs[parts // 2], refs[parts // 2 + 1 :]
    ratio = parts // len(pieces)
    size = blk * ratio // parts
    for k, piece in enumerate(came):
        b = me_ref[0] ^ (2 * k)
        long_ref[b] = piece[0]
        long_ref[b ^ 1] = piece[1]
    for k, piece in enumerate(pieces):
        for i in range(ratio):
            b = (me_dp_ref[0] ^ k) * ratio + i
            gate = (query_ref[b].astype(F32) * long_ref[b].astype(F32)).astype(BF16)
            for q in range(blk // size):
                c = i * (blk // size) + q
                piece[:, columns(c % 2 * (parts // 2) + c // 2, size)] = gate[:, columns(q, size)]


def final_kernel(*refs):
    proj_ref, prev_ref, taps_ref, gate_grad_ref, long_ref, back_ref, keyed_ref, valued_ref = refs[:8]
    query_after_ref, pair_after_ref, skip_ref, out_ref, sums_ref = refs[8:]
    parts, rows, blk = long_ref.shape
    sums_ref[3:4, :] = jnp.zeros((1, sums_ref.shape[1]), F32)
    sums_ref[3:4, 0:blk] = skip_ref[...]
    for b in range(parts):
        back = back_ref[b, 0:rows].astype(F32)
        back_after = back_ref[b, rows : rows + 2].astype(F32)
        grads = (
            (
                gate_grad_ref[b].astype(F32) * long_ref[b].astype(F32),
                query_after_ref[b],
            ),
            (back * valued_ref[b].astype(F32), back_after * pair_after_ref[1, b]),
            (back * keyed_ref[b].astype(F32), back_after * pair_after_ref[0, b]),
        )
        for stream, (grad, after) in enumerate(grads):
            cols = columns(stream * parts + b, blk)
            taps = taps_ref[:, cols]
            total = taps[0:1] * grad + taps[1:2] * rows_up(grad, 1, after)
            out_ref[:, cols] = (total + taps[2:3] * rows_up(grad, 2, after)).astype(BF16)
            values = proj_ref[:, cols].astype(F32)
            before = prev_ref[:, cols]
            for j in range(3):
                moved = rows_down(values, j, before) if j else values
                sums_ref[j : j + 1, cols] = jnp.sum(grad * moved, 0, keepdims=True)


def table(first, freqs, seq_len):
    places = jnp.arange(seq_len)
    inner = min(32, freqs)
    outer = freqs // inner

    def waves(odd):
        phases = odd[:, None] * places[None, :] % (4 * seq_len)
        angles = phases.astype(F32) * (2.0 * math.pi / (4 * seq_len))
        return (jnp.cos(angles), jnp.sin(angles))

    outer_cos, outer_sin = waves(2 * (first + inner * jnp.arange(outer)))
    inner_cos, inner_sin = waves(2 * jnp.arange(inner) + 1)
    oc, os = (outer_cos[:, None], outer_sin[:, None])
    ic, is_ = (inner_cos[None], inner_sin[None])
    both = jnp.stack([oc * ic - os * is_, -(os * ic + oc * is_)])
    return both.astype(BF16).reshape(2 * freqs, seq_len)


def constant_table(seq_len):
    odd = 2 * np.arange(seq_len)[:, None] + 1
    angles = odd * np.arange(seq_len)[None, :] % (4 * seq_len) * (math.pi / (2 * seq_len))
    return np.stack([np.cos(angles), -np.sin(angles)]).astype(np.float32).astype(BF16)


def dot(left, right, left_dim, right_dim):
    return lax.dot_general(
        left, right, (((left_dim,), (right_dim,)), ((), ())), preferred_element_type=F32
    )


def spectral_product(left, right, conjugate_left):
    half = left.shape[0] // 2
    left_re, left_im = (left[:half], left[half:])
    right_re, right_im = (right[:half], right[half:])
    if conjugate_left:
        real = left_re * right_re + left_im * right_im
        imag = left_re * right_im - left_im * right_re
    else:
        real = left_re * right_re - left_im * right_im
        imag = left_re * right_im + left_im * right_re
    return jnp.concatenate([real, imag], 0).astype(BF16)


def filter_kernel(waves_ref, filter_ref, spec_ref):
    values = filter_ref[...].astype(BF16)
    for i in range(2):
        spec_ref[i] = dot(values, waves_ref[i], 1, 1)


def out_kernel(waves_ref, filter_spec_ref, product_ref, skip_ref, spec_ref, long_ref, turned, total):
    step = pl.program_id(0)

    @pl.when(step == 0)
    def _():
        turned[...] = product_ref[...].astype(F32).T.astype(BF16)
        total[...] = jnp.zeros_like(total)

    spec_re, spec_im = (dot(turned[...], waves_ref[i], 1, 1) for i in range(2))
    spec_ref[0], spec_ref[1] = (spec_re, spec_im)
    filter_re, filter_im = (filter_spec_ref[0], filter_spec_ref[1])
    real = (filter_re * spec_re - filter_im * spec_im).astype(BF16)
    imag = (filter_re * spec_im + filter_im * spec_re).astype(BF16)
    total[...] += dot(real, waves_ref[0], 1, 0) + dot(imag, waves_ref[1], 1, 0)

    @pl.when(step == pl.num_programs(0) - 1)
    def _():
        inverse = 1.0 / total.shape[1]
        direct = skip_ref[...] * product_ref[...].astype(F32)
        long_ref[...] = (total[...].T * inverse + direct).astype(BF16)


def back_kernel(
    waves_ref, filter_spec_ref, spec_ref, grad_ref, product_ref, skip_ref,
    back_ref, lag_ref, sum_ref, turned, total,
):
    step = pl.program_id(0)

    @pl.when(step == 0)
    def _():
        turned[...] = grad_ref[...].astype(F32).T.astype(BF16)
        total[...] = jnp.zeros_like(total)
        lag_ref[...] = jnp.zeros_like(lag_ref)

    grad_re, grad_im = (dot(turned[...], waves_ref[i], 1, 1) for i in range(2))
    for ref, sums in ((filter_spec_ref, total), (spec_ref, lag_ref)):
        left_re, left_im = (ref[0], ref[1])
        real = (left_re * grad_re + left_im * grad_im).astype(BF16)
        imag = (left_re * grad_im - left_im * grad_re).astype(BF16)
        sums[...] += dot(real, waves_ref[0], 1, 0) + dot(imag, waves_ref[1], 1, 0)

    @pl.when(step == pl.num_programs(0) - 1)
    def _():
        inverse = 1.0 / total.shape[1]
        parts, rows = (back_ref.shape[0], back_ref.shape[1] - 2)
        grad = grad_ref[...].astype(F32)
        back = (total[...].T * inverse + skip_ref[...] * grad).astype(BF16)
        for b in range(parts):
            back_ref[b, 0:rows] = back[b * rows : (b + 1) * rows]
            if b < parts - 1:
                back_ref[b, rows : rows + 2] = back[(b + 1) * rows : (b + 1) * rows + 2]
            else:
                back_ref[b, rows : rows + 2] = jnp.zeros((2, back.shape[1]), BF16)
        sum_ref[...] = jnp.sum(grad * product_ref[...].astype(F32), 0, keepdims=True)


def chunked(kernel, name, waves, specs, planes, outs, spec_out, scratch):
    freqs, seq_len = waves.shape[1:]
    size = min(256, freqs)
    blk = (specs + spec_out)[0].shape[1]
    chunk = pl.BlockSpec((2, blk, size), lambda i: (0, 0, i))

    def whole(array):
        return pl.BlockSpec(array.shape, lambda i: (0,) * len(array.shape))

    return pl.pallas_call(
        kernel,
        out_shape=spec_out + outs,
        grid=(freqs // size,),
        in_specs=[pl.BlockSpec((2, size, seq_len), lambda i: (0, i, 0))]
        + [chunk] * len(specs)
        + [whole(a) for a in planes],
        out_specs=[chunk] * len(spec_out) + [whole(a) for a in outs],
        scratch_shapes=scratch,
        compiler_params=pltpu.CompilerParams(vmem_limit_bytes=60 * 2**20),
        cost_estimate=pl.CostEstimate(flops=0, transcendentals=0, bytes_accessed=0),
        name=name,
    )(waves, *specs, *planes)


def ordered(value, *first):
    return lax.optimization_barrier((value, *first))[0]


def transforms(waves, long_filter, product, grad_long):
    filter_spec = dot(waves, long_filter, 1, 1)
    product_spec = dot(waves, product, 1, 0)
    grad_spec = dot(waves, grad_long, 1, 0)
    out = dot(waves, spectral_product(filter_spec, product_spec, False), 0, 0)
    back = dot(waves, spectral_product(filter_spec, grad_spec, True), 0, 0)
    lag_grad = dot(spectral_product(product_spec, grad_spec, True), waves, 0, 0)
    return (out, back, lag_grad)


def all_sum(value, axis, bits):
    for pair in [bits[i : i + 2] for i in range(0, len(bits), 2)]:
        sums = [value]
        for bit in pair:
            sums += [swapped(value, axis, bit)]
        if len(pair) == 2:
            far = swapped(value, axis, pair[0] + pair[1])
            value = (sums[0] + sums[1]) + (sums[2] + far)
        else:
            value = sums[0] + sums[1]
    return value


def bits_of(count, first=1):
    return [1 << i for i in range(count.bit_length() - 1) if 1 << i >= first]


def own_share(gate_all, cot_all, parts):
    core = lax.axis_index("context") % 2
    width = gate_all.shape[1] // 2
    other = dot(lax.dynamic_slice_in_dim(gate_all, (1 - core) * width, width, 1), cot_all, 0, 0)
    other = other.astype(BF16)
    own_gate = ordered(lax.dynamic_slice_in_dim(gate_all, core * width, width, 1), other)
    own = dot(own_gate, cot_all, 0, 0)
    pair = (own + swapped(other, "context", 1).astype(F32)).astype(BF16)
    pair = pair.reshape(parts // 2, -1, pair.shape[-1])
    row = lax.axis_index("context") // 2
    shares = [lax.dynamic_index_in_dim(pair, row, 0, False)]
    for k in range(1, parts // 2):
        sent = lax.dynamic_index_in_dim(pair, row ^ k, 0, False)
        shares.append(swapped(sent, "context", 2 * k))
    return (pair, shares)


def summed_blocks(value, axis, dim):
    count = lax.axis_size(axis)
    size = value.shape[dim] // count
    me = lax.axis_index(axis)
    total = lax.dynamic_slice_in_dim(value, me * size, size, dim)
    for k in range(1, count):
        sent = lax.dynamic_slice_in_dim(value, (me ^ k) * size, size, dim).astype(BF16)
        total = total + swapped(sent, axis, k).astype(F32)
    return total


def to_channels(blocks):
    came = lax.all_to_all(blocks, "context", split_axis=0, concat_axis=0, tiled=True)
    return came.reshape(-1, came.shape[-1])


def to_positions(blocks):
    return lax.all_to_all(blocks, "context", split_axis=0, concat_axis=0, tiled=True)


def body(projected, short_taps, long_filter, skip_gain, out_proj, cotangent):
    rows, width = projected.shape
    chans = width // 3
    parts_dp, parts = (lax.axis_size("dp"), lax.axis_size("context"))
    blk = chans // parts
    seq_len = rows * parts
    scale_factor = 1.0 / math.sqrt(seq_len * parts_dp)
    me = lax.axis_index("context").astype(jnp.int32)
    me_dp = lax.axis_index("dp").astype(jnp.int32)[None]
    plane = jax.ShapeDtypeStruct((parts, rows, blk), BF16)

    prev_rows = passed_along(projected[rows - 2 :], "context", 1).astype(F32)
    cots = [cotangent] + [swapped(cotangent, "dp", k) for k in range(1, parts_dp)]
    query, keyed, valued, product_out = call(
        short_kernel, "short_convs", [plane] * 4, 0, 60, projected, prev_rows, short_taps
    )
    product = to_channels(product_out)

    filter_b = long_filter.astype(BF16)
    inverse = 1.0 / seq_len
    straight = seq_len <= 1024
    weights = out_proj
    if straight:
        waves = jnp.asarray(constant_table(seq_len))
        spec = jax.ShapeDtypeStruct((2, blk, seq_len), F32)
        scratch = [pltpu.VMEM((blk, seq_len), BF16), pltpu.VMEM((blk, seq_len), F32)]
        skip_row = skip_gain[None, :]
        (filter_spec,) = chunked(
            filter_kernel, "filter_spectrum", waves, [], [long_filter], [], [spec], []
        )
        weights = ordered(out_proj, filter_spec)
    formed = [dot(cot, weights, 1, 1).astype(BF16) for cot in cots]
    found = [formed[0]] + [swapped(formed[k], "dp", k) for k in range(1, parts_dp)]
    gate_grad, grad_long_out = call(
        grad_long_kernel, "grad_long", [plane] * 2, 1, 12, me_dp, query, *found
    )
    heads = lax.optimization_barrier((keyed[:, :2], valued[:, :2], *formed))[:2]
    heads = jnp.stack(heads)
    pair_after = passed_along(heads, "context", -1).astype(F32)
    grad_long = to_channels(ordered(grad_long_out, pair_after))
    product_f, grad_long_f = (product.astype(F32), grad_long.astype(F32))

    def finished(total, direct):
        return (total * inverse + skip_gain[None, :] * direct).astype(BF16)

    def crossed(values):
        by_core = values.reshape(parts // 2, 2, rows, blk)
        core, row = (me % 2, me // 2)
        mine = lax.dynamic_index_in_dim(by_core, core, 1, False)
        near = swapped(lax.dynamic_index_in_dim(by_core, 1 - core, 1, False), "context", 1)
        stacked = jnp.stack([mine, near], 1)
        came = [lax.dynamic_index_in_dim(stacked, row, 0, False)]
        for k in range(1, parts // 2):
            sent = lax.dynamic_index_in_dim(stacked, row ^ k, 0, False)
            came.append(swapped(sent, "context", 2 * k))
        return came

    if straight:
        late_product = ordered(product, grad_long_out)
        product_spec, long_chan = chunked(
            out_kernel,
            "long_out",
            waves,
            [filter_spec],
            [late_product, skip_row],
            [jax.ShapeDtypeStruct((seq_len, blk), BF16)],
            [spec],
            scratch,
        )
        long_came = crossed(long_chan)
        back_sent, lag_sum, skip_sum = chunked(
            back_kernel,
            "grad_product",
            waves,
            [filter_spec, product_spec],
            [ordered(grad_long, long_came[1]), product, skip_row],
            [
                jax.ShapeDtypeStruct((parts, rows + 2, blk), BF16),
                jax.ShapeDtypeStruct((blk, seq_len), F32),
                jax.ShapeDtypeStruct((1, blk), F32),
            ],
            [],
            scratch,
        )
    else:
        freqs = 256

        def step(carry, first):
            new = transforms(table(first, freqs, seq_len), filter_b, product, grad_long)
            return (tuple(a + b for a, b in zip(carry, new)), None)

        zero = jnp.zeros((seq_len, blk), F32)
        start = (zero, zero, jnp.zeros((blk, seq_len), F32))
        terms, _ = lax.scan(step, start, jnp.arange(0, seq_len, freqs))
        out_sum, back_sum, lag_sum = terms
        long_came = crossed(finished(out_sum, product_f))
        back_blocks = finished(back_sum, grad_long_f).reshape(parts, rows, blk)
        next_heads = jnp.concatenate([back_blocks[1:, :2], jnp.zeros((1, 2, blk), BF16)], 0)
        back_sent = jnp.concatenate([back_blocks, next_heads], 1)
        skip_sum = jnp.sum(grad_long_f * product_f, 0, keepdims=True)
    grad_product = to_positions(back_sent)
    long_came = lax.optimization_barrier((*long_came, back_sent, pair_after))[: parts // 2]

    piece = jax.ShapeDtypeStruct((rows, chans // parts_dp), BF16)
    long_out, *gates = call(
        gate_kernel, "gate", [plane] + [piece] * parts_dp, 2, 12, me[None], me_dp, query, *long_came
    )
    gates = [gates[0]] + [swapped(gates[k], "dp", k) for k in range(1, parts_dp)]
    query_heads = gate_grad[:, :2].astype(F32) * long_out[:, :2].astype(F32)
    query_after = passed_along(query_heads, "context", -1)
    early = (grad_product, query_after)
    cot_all = jnp.concatenate(lax.optimization_barrier((*cots, gates[0]))[:parts_dp], 0)
    gate_all = ordered(jnp.concatenate(gates, 0), *early)
    pair, shares = own_share(gate_all, cot_all, parts)
    grad_product = ordered(grad_product, pair)

    grad_inputs, tap_sums = call(
        final_kernel,
        "stream_grads",
        [
            jax.ShapeDtypeStruct((rows, width), BF16),
            jax.ShapeDtypeStruct((4, width), F32),
        ],
        0,
        60,
        projected,
        prev_rows,
        short_taps,
        gate_grad,
        long_out,
        grad_product,
        keyed,
        valued,
        query_after,
        pair_after,
        skip_sum,
    )

    tap_sums = all_sum(tap_sums, "dp", bits_of(parts_dp))
    lag_sum = ordered(lag_sum, tap_sums)
    grad_filter = summed_blocks(lag_sum, "dp", 1) * (scale_factor * inverse)
    grad_skip = tap_sums[3, :blk] * scale_factor
    tap_sums = tap_sums[:3] + swapped(tap_sums[:3], "context", 1)
    tap_sums = ordered(tap_sums, *shares[1:])
    grad_taps = all_sum(tap_sums, "context", bits_of(parts, 2)) * scale_factor
    grad_proj = sum(share.astype(F32) for share in shares) * scale_factor
    return (grad_inputs, grad_taps, grad_filter, grad_skip, grad_proj)


def solution(mesh):
    placed = (
        P(("dp", "context"), None),
        P(),
        P("context", None),
        P("context"),
        P("dp", None),
        P(("dp", "context"), None),
    )
    return jax.shard_map(
        body,
        mesh=mesh,
        in_specs=placed,
        out_specs=(
            P(("dp", "context"), None),
            P(),
            P("context", "dp"),
            P("context"),
            P(("dp", "context"), None),
        ),
        check_vma=False,
    )
```

```python
import math

import jax
import jax.numpy as jnp
import numpy as np
from jax import lax
from jax.experimental import pallas as pl
from jax.experimental.pallas import tpu as pltpu
from jax.sharding import PartitionSpec as P

BF16 = jnp.bfloat16
F32 = jnp.float32


def passed_along(value, axis, steps):
    count = lax.axis_size(axis)
    initial, last = (max(0, -steps), min(count, count - steps))
    return lax.ppermute(value, axis, [(source, source + steps) for source in range(initial, last)])


def swapped(value, axis, mask):
    return lax.ppermute(value, axis, [(i, i ^ mask) for i in range(lax.axis_size(axis))])


SMEM = pl.BlockSpec(memory_space=pltpu.SMEM)


def rows_down(values, steps, before):
    row = lax.broadcasted_iota(jnp.int32, values.shape, 0)
    moved = pltpu.roll(values, steps, axis=0)
    if steps == 1:
        return jnp.where(row == 0, before[1:2], moved)
    return jnp.where(row == 0, before[0:1], jnp.where(row == 1, before[1:2], moved))


def rows_up(values, steps, after):
    count = values.shape[0]
    row = lax.broadcasted_iota(jnp.int32, values.shape, 0)
    moved = pltpu.roll(values, count - steps, axis=0)
    if steps == 1:
        return jnp.where(row == count - 1, after[0:1], moved)
    return jnp.where(row == count - 1, after[1:2], jnp.where(row == count - 2, after[0:1], moved))


def call(kernel, name, outs, smem, limit, *args):
    arrays = args[smem:]
    count, given = (len(arrays), len(outs))

    def run(*refs):
        ends = refs[smem : smem + count + given]
        *buffers, sems = refs[smem + count + given :]
        copies = []
        for i, (end, buffer) in enumerate(zip(ends, buffers)):
            pair = (end, buffer) if i < count else (buffer, end)
            copies.append(pltpu.make_async_copy(*pair, sems.at[i]))
        for copy in copies[:count]:
            copy.start()
        for copy in copies[:count]:
            copy.wait()
        kernel(*refs[:smem], *buffers)
        for copy in copies[count:]:
            copy.start()
        for copy in copies[count:]:
            copy.wait()

    anywhere = pl.BlockSpec(memory_space=pl.ANY)
    return pl.pallas_call(
        run,
        out_shape=outs,
        in_specs=[SMEM] * smem + [anywhere] * count,
        out_specs=[anywhere] * given,
        scratch_shapes=[pltpu.VMEM(a.shape, a.dtype) for a in (*arrays, *outs)]
        + [pltpu.SemaphoreType.DMA((count + given,))],
        compiler_params=pltpu.CompilerParams(vmem_limit_bytes=limit * 2**20),
        cost_estimate=pl.CostEstimate(flops=0, transcendentals=0, bytes_accessed=0),
        name=name,
    )(*args)


def columns(index, size):
    return slice(index * size, (index + 1) * size)


def short_kernel(proj_ref, prev_ref, taps_ref, query_ref, keyed_ref, valued_ref, product_ref):
    parts, _, blk = query_ref.shape
    for b in range(parts):

        def mixed(stream):
            cols = columns(stream * parts + b, blk)
            values = proj_ref[:, cols].astype(F32)
            before = prev_ref[:, cols].astype(F32)
            taps = taps_ref[:, cols]
            total = taps[0:1] * values + taps[1:2] * rows_down(values, 1, before)
            return (total + taps[2:3] * rows_down(values, 2, before)).astype(BF16)

        query_ref[b] = mixed(0)
        keyed, valued = (mixed(1), mixed(2))
        keyed_ref[b] = keyed
        valued_ref[b] = valued
        product_ref[b] = (keyed.astype(F32) * valued.astype(F32)).astype(BF16)


def grad_long_kernel(me_ref, query_ref, *refs):
    pieces, (gate_grad_ref, grad_long_ref) = refs[:-2], refs[-2:]
    parts, _, blk = query_ref.shape
    ratio = parts // len(pieces)
    for k, piece in enumerate(pieces):
        for i in range(ratio):
            b = (me_ref[0] ^ k) * ratio + i
            values = piece[:, columns(i, blk)]
            gate_grad_ref[b] = values
            grad_long_ref[b] = (values.astype(F32) * query_ref[b].astype(F32)).astype(BF16)


def gate_kernel(me_ref, me_dp_ref, query_ref, *refs):
    parts, _, blk = query_ref.shape
    came, long_ref, pieces = refs[: parts // 2], refs[parts // 2], refs[parts // 2 + 1 :]
    ratio = parts // len(pieces)
    size = blk * ratio // parts
    for k, piece in enumerate(came):
        b = me_ref[0] ^ (2 * k)
        long_ref[b] = piece[0]
        long_ref[b ^ 1] = piece[1]
    for k, piece in enumerate(pieces):
        for i in range(ratio):
            b = (me_dp_ref[0] ^ k) * ratio + i
            gate = (query_ref[b].astype(F32) * long_ref[b].astype(F32)).astype(BF16)
            for q in range(blk // size):
                c = i * (blk // size) + q
                piece[:, columns(c % 2 * (parts // 2) + c // 2, size)] = gate[:, columns(q, size)]


def final_kernel(*refs):
    proj_ref, prev_ref, taps_ref, gate_grad_ref, long_ref, back_ref, keyed_ref, valued_ref = refs[:8]
    query_after_ref, pair_after_ref, skip_ref, out_ref, sums_ref = refs[8:]
    parts, rows, blk = long_ref.shape
    sums_ref[3:4, :] = jnp.zeros((1, sums_ref.shape[1]), F32)
    sums_ref[3:4, 0:blk] = skip_ref[...]
    for b in range(parts):
        back = back_ref[b, 0:rows].astype(F32)
        back_after = back_ref[b, rows : rows + 2].astype(F32)
        grads = (
            (
                gate_grad_ref[b].astype(F32) * long_ref[b].astype(F32),
                query_after_ref[b],
            ),
            (back * valued_ref[b].astype(F32), back_after * pair_after_ref[1, b].astype(F32)),
            (back * keyed_ref[b].astype(F32), back_after * pair_after_ref[0, b].astype(F32)),
        )
        for stream, (grad, after) in enumerate(grads):
            cols = columns(stream * parts + b, blk)
            taps = taps_ref[:, cols]
            total = taps[0:1] * grad + taps[1:2] * rows_up(grad, 1, after)
            out_ref[:, cols] = (total + taps[2:3] * rows_up(grad, 2, after)).astype(BF16)
            values = proj_ref[:, cols].astype(F32)
            before = prev_ref[:, cols].astype(F32)
            for j in range(3):
                moved = rows_down(values, j, before) if j else values
                sums_ref[j : j + 1, cols] = jnp.sum(grad * moved, 0, keepdims=True)


def table(first, freqs, seq_len):
    places = jnp.arange(seq_len)
    inner = min(32, freqs)
    outer = freqs // inner

    def waves(odd):
        phases = odd[:, None] * places[None, :] % (4 * seq_len)
        angles = phases.astype(F32) * (2.0 * math.pi / (4 * seq_len))
        return (jnp.cos(angles), jnp.sin(angles))

    outer_cos, outer_sin = waves(2 * (first + inner * jnp.arange(outer)))
    inner_cos, inner_sin = waves(2 * jnp.arange(inner) + 1)
    oc, os = (outer_cos[:, None], outer_sin[:, None])
    ic, is_ = (inner_cos[None], inner_sin[None])
    both = jnp.stack([oc * ic - os * is_, -(os * ic + oc * is_)])
    return both.astype(BF16).reshape(2 * freqs, seq_len)


def constant_table(seq_len):
    odd = 2 * np.arange(seq_len)[:, None] + 1
    angles = odd * np.arange(seq_len)[None, :] % (4 * seq_len) * (math.pi / (2 * seq_len))
    return np.stack([np.cos(angles), -np.sin(angles)]).astype(np.float32).astype(BF16)


def dot(left, right, left_dim, right_dim):
    return lax.dot_general(
        left, right, (((left_dim,), (right_dim,)), ((), ())), preferred_element_type=F32
    )


def spectral_product(left, right, conjugate_left):
    half = left.shape[0] // 2
    left_re, left_im = (left[:half], left[half:])
    right_re, right_im = (right[:half], right[half:])
    if conjugate_left:
        real = left_re * right_re + left_im * right_im
        imag = left_re * right_im - left_im * right_re
    else:
        real = left_re * right_re - left_im * right_im
        imag = left_re * right_im + left_im * right_re
    return jnp.concatenate([real, imag], 0).astype(BF16)


def filter_kernel(waves_ref, filter_ref, spec_ref):
    values = filter_ref[...].astype(BF16)
    for i in range(2):
        spec_ref[i] = dot(values, waves_ref[i], 1, 1)


def out_kernel(waves_ref, filter_spec_ref, product_ref, skip_ref, spec_ref, long_ref, turned, total):
    step = pl.program_id(0)

    @pl.when(step == 0)
    def _():
        turned[...] = product_ref[...].astype(F32).T.astype(BF16)
        total[...] = jnp.zeros_like(total)

    spec_re, spec_im = (dot(turned[...], waves_ref[i], 1, 1) for i in range(2))
    spec_ref[0], spec_ref[1] = (spec_re, spec_im)
    filter_re, filter_im = (filter_spec_ref[0], filter_spec_ref[1])
    real = (filter_re * spec_re - filter_im * spec_im).astype(BF16)
    imag = (filter_re * spec_im + filter_im * spec_re).astype(BF16)
    total[...] += dot(real, waves_ref[0], 1, 0) + dot(imag, waves_ref[1], 1, 0)

    @pl.when(step == pl.num_programs(0) - 1)
    def _():
        inverse = 1.0 / total.shape[1]
        direct = skip_ref[...] * product_ref[...].astype(F32)
        long_ref[...] = (total[...].T * inverse + direct).astype(BF16)


def back_kernel(
    waves_ref, filter_spec_ref, spec_ref, grad_ref, product_ref, skip_ref,
    back_ref, lag_ref, sum_ref, turned, total,
):
    step = pl.program_id(0)

    @pl.when(step == 0)
    def _():
        turned[...] = grad_ref[...].astype(F32).T.astype(BF16)
        total[...] = jnp.zeros_like(total)
        lag_ref[...] = jnp.zeros_like(lag_ref)

    grad_re, grad_im = (dot(turned[...], waves_ref[i], 1, 1) for i in range(2))
    for ref, sums in ((filter_spec_ref, total), (spec_ref, lag_ref)):
        left_re, left_im = (ref[0], ref[1])
        real = (left_re * grad_re + left_im * grad_im).astype(BF16)
        imag = (left_re * grad_im - left_im * grad_re).astype(BF16)
        sums[...] += dot(real, waves_ref[0], 1, 0) + dot(imag, waves_ref[1], 1, 0)

    @pl.when(step == pl.num_programs(0) - 1)
    def _():
        inverse = 1.0 / total.shape[1]
        parts, rows = (back_ref.shape[0], back_ref.shape[1] - 2)
        grad = grad_ref[...].astype(F32)
        back = (total[...].T * inverse + skip_ref[...] * grad).astype(BF16)
        for b in range(parts):
            back_ref[b, 0:rows] = back[b * rows : (b + 1) * rows]
            if b < parts - 1:
                back_ref[b, rows : rows + 2] = back[(b + 1) * rows : (b + 1) * rows + 2]
            else:
                back_ref[b, rows : rows + 2] = jnp.zeros((2, back.shape[1]), BF16)
        sum_ref[...] = jnp.sum(grad * product_ref[...].astype(F32), 0, keepdims=True)


def chunked(kernel, name, waves, specs, planes, outs, spec_out, scratch):
    freqs, seq_len = waves.shape[1:]
    size = min(256, freqs)
    blk = (specs + spec_out)[0].shape[1]
    chunk = pl.BlockSpec((2, blk, size), lambda i: (0, 0, i))

    def whole(array):
        return pl.BlockSpec(array.shape, lambda i: (0,) * len(array.shape))

    return pl.pallas_call(
        kernel,
        out_shape=spec_out + outs,
        grid=(freqs // size,),
        in_specs=[pl.BlockSpec((2, size, seq_len), lambda i: (0, i, 0))]
        + [chunk] * len(specs)
        + [whole(a) for a in planes],
        out_specs=[chunk] * len(spec_out) + [whole(a) for a in outs],
        scratch_shapes=scratch,
        compiler_params=pltpu.CompilerParams(vmem_limit_bytes=60 * 2**20),
        cost_estimate=pl.CostEstimate(flops=0, transcendentals=0, bytes_accessed=0),
        name=name,
    )(waves, *specs, *planes)


def ordered(value, *first):
    return lax.optimization_barrier((value, *first))[0]


def transforms(waves, long_filter, product, grad_long):
    filter_spec = dot(waves, long_filter, 1, 1)
    product_spec = dot(waves, product, 1, 0)
    grad_spec = dot(waves, grad_long, 1, 0)
    out = dot(waves, spectral_product(filter_spec, product_spec, False), 0, 0)
    back = dot(waves, spectral_product(filter_spec, grad_spec, True), 0, 0)
    lag_grad = dot(spectral_product(product_spec, grad_spec, True), waves, 0, 0)
    return (out, back, lag_grad)


def all_sum(value, axis, bits):
    for pair in [bits[i : i + 2] for i in range(0, len(bits), 2)]:
        sums = [value]
        for bit in pair:
            sums += [swapped(value, axis, bit)]
        if len(pair) == 2:
            far = swapped(value, axis, pair[0] + pair[1])
            value = (sums[0] + sums[1]) + (sums[2] + far)
        else:
            value = sums[0] + sums[1]
    return value


def bits_of(count, first=1):
    return [1 << i for i in range(count.bit_length() - 1) if 1 << i >= first]


def own_share(gate_all, cot_all, parts):
    core = lax.axis_index("context") % 2
    width = gate_all.shape[1] // 2
    other = dot(lax.dynamic_slice_in_dim(gate_all, (1 - core) * width, width, 1), cot_all, 0, 0)
    other = other.astype(BF16)
    own_gate = ordered(lax.dynamic_slice_in_dim(gate_all, core * width, width, 1), other)
    own = dot(own_gate, cot_all, 0, 0)
    pair = (own + swapped(other, "context", 1).astype(F32)).astype(BF16)
    pair = pair.reshape(parts // 2, -1, pair.shape[-1])
    row = lax.axis_index("context") // 2
    shares = [lax.dynamic_index_in_dim(pair, row, 0, False)]
    for k in range(1, parts // 2):
        sent = lax.dynamic_index_in_dim(pair, row ^ k, 0, False)
        shares.append(swapped(sent, "context", 2 * k))
    return (pair, shares)


def summed_blocks(value, axis, dim):
    count = lax.axis_size(axis)
    size = value.shape[dim] // count
    me = lax.axis_index(axis)
    total = lax.dynamic_slice_in_dim(value, me * size, size, dim)
    for k in range(1, count):
        sent = lax.dynamic_slice_in_dim(value, (me ^ k) * size, size, dim).astype(BF16)
        total = total + swapped(sent, axis, k).astype(F32)
    return total


def to_channels(blocks):
    came = lax.all_to_all(blocks, "context", split_axis=0, concat_axis=0, tiled=True)
    return came.reshape(-1, came.shape[-1])


def to_positions(blocks):
    return lax.all_to_all(blocks, "context", split_axis=0, concat_axis=0, tiled=True)


def body(projected, short_taps, long_filter, skip_gain, out_proj, cotangent):
    rows, width = projected.shape
    chans = width // 3
    parts_dp, parts = (lax.axis_size("dp"), lax.axis_size("context"))
    blk = chans // parts
    seq_len = rows * parts
    scale_factor = 1.0 / math.sqrt(seq_len * parts_dp)
    me = lax.axis_index("context").astype(jnp.int32)
    me_dp = lax.axis_index("dp").astype(jnp.int32)[None]
    plane = jax.ShapeDtypeStruct((parts, rows, blk), BF16)

    prev_rows = passed_along(projected[rows - 2 :], "context", 1)
    cots = [cotangent] + [swapped(cotangent, "dp", k) for k in range(1, parts_dp)]
    query, keyed, valued, product_out = call(
        short_kernel, "short_convs", [plane] * 4, 0, 60, projected, prev_rows, short_taps
    )
    product = to_channels(product_out)

    filter_b = long_filter.astype(BF16)
    inverse = 1.0 / seq_len
    straight = seq_len <= 1024
    weights = out_proj
    if straight:
        waves = jnp.asarray(constant_table(seq_len))
        spec = jax.ShapeDtypeStruct((2, blk, seq_len), F32)
        scratch = [pltpu.VMEM((blk, seq_len), BF16), pltpu.VMEM((blk, seq_len), F32)]
        skip_row = skip_gain[None, :]
        (filter_spec,) = chunked(
            filter_kernel, "filter_spectrum", waves, [], [long_filter], [], [spec], []
        )
        weights = ordered(out_proj, filter_spec)
    formed = [dot(cot, weights, 1, 1).astype(BF16) for cot in cots]
    found = [formed[0]] + [swapped(formed[k], "dp", k) for k in range(1, parts_dp)]
    gate_grad, grad_long_out = call(
        grad_long_kernel, "grad_long", [plane] * 2, 1, 12, me_dp, query, *found
    )
    heads = lax.optimization_barrier((keyed[:, :2], valued[:, :2], *formed))[:2]
    heads = jnp.stack(heads)
    pair_after = passed_along(heads, "context", -1)
    grad_long = to_channels(ordered(grad_long_out, pair_after))
    product_f, grad_long_f = (product.astype(F32), grad_long.astype(F32))

    def finished(total, direct):
        return (total * inverse + skip_gain[None, :] * direct).astype(BF16)

    def crossed(values):
        by_core = values.reshape(parts // 2, 2, rows, blk)
        core, row = (me % 2, me // 2)
        mine = lax.dynamic_index_in_dim(by_core, core, 1, False)
        near = swapped(lax.dynamic_index_in_dim(by_core, 1 - core, 1, False), "context", 1)
        stacked = jnp.stack([mine, near], 1)
        came = [lax.dynamic_index_in_dim(stacked, row, 0, False)]
        for k in range(1, parts // 2):
            sent = lax.dynamic_index_in_dim(stacked, row ^ k, 0, False)
            came.append(swapped(sent, "context", 2 * k))
        return came

    if straight:
        late_product = ordered(product, grad_long_out)
        product_spec, long_chan = chunked(
            out_kernel,
            "long_out",
            waves,
            [filter_spec],
            [late_product, skip_row],
            [jax.ShapeDtypeStruct((seq_len, blk), BF16)],
            [spec],
            scratch,
        )
        long_came = crossed(long_chan)
        back_sent, lag_sum, skip_sum = chunked(
            back_kernel,
            "grad_product",
            waves,
            [filter_spec, product_spec],
            [ordered(grad_long, long_came[1]), product, skip_row],
            [
                jax.ShapeDtypeStruct((parts, rows + 2, blk), BF16),
                jax.ShapeDtypeStruct((blk, seq_len), F32),
                jax.ShapeDtypeStruct((1, blk), F32),
            ],
            [],
            scratch,
        )
    else:
        freqs = 256

        def step(carry, first):
            new = transforms(table(first, freqs, seq_len), filter_b, product, grad_long)
            return (tuple(a + b for a, b in zip(carry, new)), None)

        zero = jnp.zeros((seq_len, blk), F32)
        start = (zero, zero, jnp.zeros((blk, seq_len), F32))
        terms, _ = lax.scan(step, start, jnp.arange(0, seq_len, freqs))
        out_sum, back_sum, lag_sum = terms
        long_came = crossed(finished(out_sum, product_f))
        back_blocks = finished(back_sum, grad_long_f).reshape(parts, rows, blk)
        next_heads = jnp.concatenate([back_blocks[1:, :2], jnp.zeros((1, 2, blk), BF16)], 0)
        back_sent = jnp.concatenate([back_blocks, next_heads], 1)
        skip_sum = jnp.sum(grad_long_f * product_f, 0, keepdims=True)
    grad_product = to_positions(back_sent)
    long_came = lax.optimization_barrier((*long_came, back_sent, pair_after))[: parts // 2]

    piece = jax.ShapeDtypeStruct((rows, chans // parts_dp), BF16)
    long_out, *gates = call(
        gate_kernel, "gate", [plane] + [piece] * parts_dp, 2, 12, me[None], me_dp, query, *long_came
    )
    gates = [gates[0]] + [swapped(gates[k], "dp", k) for k in range(1, parts_dp)]
    query_heads = gate_grad[:, :2].astype(F32) * long_out[:, :2].astype(F32)
    query_after = passed_along(query_heads, "context", -1)
    early = (grad_product, query_after)
    cot_all = jnp.concatenate(lax.optimization_barrier((*cots, gates[0]))[:parts_dp], 0)
    gate_all = ordered(jnp.concatenate(gates, 0), *early)
    pair, shares = own_share(gate_all, cot_all, parts)
    grad_product = ordered(grad_product, pair)

    grad_inputs, tap_sums = call(
        final_kernel,
        "stream_grads",
        [
            jax.ShapeDtypeStruct((rows, width), BF16),
            jax.ShapeDtypeStruct((4, width), F32),
        ],
        0,
        60,
        projected,
        prev_rows,
        short_taps,
        gate_grad,
        long_out,
        grad_product,
        keyed,
        valued,
        query_after,
        pair_after,
        skip_sum,
    )

    tap_sums = all_sum(tap_sums, "dp", bits_of(parts_dp))
    lag_sum = ordered(lag_sum, tap_sums)
    grad_filter = summed_blocks(lag_sum, "dp", 1) * (scale_factor * inverse)
    grad_skip = tap_sums[3, :blk] * scale_factor
    tap_sums = tap_sums[:3] + swapped(tap_sums[:3], "context", 1)
    tap_sums = ordered(tap_sums, *shares[1:])
    grad_taps = all_sum(tap_sums, "context", bits_of(parts, 2)) * scale_factor
    grad_proj = sum(share.astype(F32) for share in shares) * scale_factor
    return (grad_inputs, grad_taps, grad_filter, grad_skip, grad_proj)


def solution(mesh):
    placed = (
        P(("dp", "context"), None),
        P(),
        P("context", None),
        P("context"),
        P("dp", None),
        P(("dp", "context"), None),
    )
    return jax.shard_map(
        body,
        mesh=mesh,
        in_specs=placed,
        out_specs=(
            P(("dp", "context"), None),
            P(),
            P("context", "dp"),
            P("context"),
            P(("dp", "context"), None),
        ),
        check_vma=False,
    )
```
